32 devices in a mesh: edge: 8 (over z, x), chan: 4 (over y, core).
Axes of the slice: x: 2, y: 2, z: 4, core: 2. Of those that a mesh axis runs over, the one named last changes fastest.
Arguments:
- edge_emb: bfloat16 [32768, 512], P('edge', 'chan'), may hold values from -6 to 6
- atom_emb: bfloat16 [1024, 256], P('edge'), may hold values from -6 to 6
- radial: bfloat16 [32768, 128], P('edge'), may hold values from 0 to 1
- circular: bfloat16 [16, 16, 32768], P(None, None, 'edge'), may hold values from -6 to 6
- spherical: bfloat16 [32, 8, 32768], P(None, None, 'edge'), may hold values from -6 to 6
- atom_tags: int32 [1024], P('edge'), may hold values from 0 to 2
- edge_source: int32 [32768], P('edge'), may hold values from 0 to 1023, as said below
- edge_target: int32 [32768], P('edge'), may hold values from 0 to 1023, as said below
- trip_source: int32 [16, 32768], P(None, 'edge'), may hold values from 0 to 12287, as said below
- trip_mask: int32 [16, 32768], P(None, 'edge'), may hold values from 0 to 1
- quad_source: int32 [8, 32768], P(None, 'edge'), may hold values from 0 to 12287, as said below
- quad_mask: int32 [8, 32768], P(None, 'edge'), may hold values from 0 to 1
- triplet_down_weight: bfloat16 [512, 64], P(None, 'chan'), may hold values from -0.25 to 0.25
- trip_radial: bfloat16 [128, 64], P(None, 'chan'), may hold values from -0.5 to 0.5
- triplet_bilinear_weight: bfloat16 [16, 64, 64], P(None, 'chan'), may hold values from -0.1875 to 0.1875
- trip_up: bfloat16 [64, 512], P(None, 'chan'), may hold values from -0.75 to 0.75
- quad_down: bfloat16 [512, 32], P(None, 'chan'), may hold values from -0.25 to 0.25
- quad_radial: bfloat16 [128, 32], P(None, 'chan'), may hold values from -0.5 to 0.5
- quad_bilinear: bfloat16 [32, 32, 32], P(None, 'chan'), may hold values from -0.1875 to 0.1875
- quad_up: bfloat16 [32, 512], P(None, 'chan'), may hold values from -1 to 1
- source_proj: bfloat16 [256, 512], P(None, 'chan'), may hold values from -0.375 to 0.375
- target_proj: bfloat16 [256, 512], P(None, 'chan'), may hold values from -0.375 to 0.375
- resid_first: bfloat16 [512, 512], P(None, 'chan'), may hold values from -0.25 to 0.25
- resid_second: bfloat16 [512, 512], P('chan'), may hold values from -0.25 to 0.25
- edge_to_atom: bfloat16 [512, 256], P('chan'), may hold values from -0.046875 to 0.046875
- atom_update: bfloat16 [256, 256], replicated, may hold values from -0.375 to 0.375
- output_first: bfloat16 [256, 256], replicated, may hold values from -0.375 to 0.375
- output_second: bfloat16 [256], replicated, may hold values from -0.375 to 0.375
- tag_table: bfloat16 [3, 256], replicated, may hold values from -3 to 3
- grad_edges: bfloat16 [32768, 512], P('edge', 'chan'), may hold values from -6 to 6
- grad_atoms: bfloat16 [1024, 256], P('edge'), may hold values from -6 to 6
- grad_energy: float32 [1024], P('edge'), may hold values from -6 to 6
Outputs:
- edges_out: bfloat16 [32768, 512], P('edge', 'chan')
- atoms_out: bfloat16 [1024, 256], P('edge')
- energy: float32 [1024], P('edge')
- edge_grad: float32 [32768, 512], P('edge', 'chan')
- atom_grad: float32 [1024, 256], P('edge')
- trip_down_grad: float32 [512, 64], P(None, 'chan')
- trip_radial_grad: float32 [128, 64], P(None, 'chan')
- trip_bilinear_grad: float32 [16, 64, 64], P(None, 'chan')
- trip_up_grad: float32 [64, 512], P(None, 'chan')
- quad_down_grad: float32 [512, 32], P(None, 'chan')
- quad_radial_grad: float32 [128, 32], P(None, 'chan')
- quad_bilinear_grad: float32 [32, 32, 32], P(None, 'chan')
- quad_up_grad: float32 [32, 512], P(None, 'chan')
- source_proj_grad: float32 [256, 512], P(None, 'chan')
- target_proj_grad: float32 [256, 512], P(None, 'chan')
- resid_first_grad: float32 [512, 512], P(None, 'chan')
- resid_second_grad: float32 [512, 512], P('chan')
- edge_to_atom_grad: float32 [512, 256], P('chan')
- atom_update_grad: float32 [256, 256], replicated
- output_first_grad: float32 [256, 256], replicated
- output_second_grad: float32 [256], replicated
- tag_table_grad: float32 [3, 256], replicated
The draws below stay inside these ranges and needn't reach their ends.
Inputs may be any that keep to these rules, and one draw needn't show every extreme that they name: `edge_source`: partition q holds edges q * 4096 to (q + 1) * 4096 - 1 and atoms q * 128 to (q + 1) * 128 - 1. The source atom of an edge lies in the edge's partition or in the partition just before or after it, the partitions closing into a loop. `edge_target`: the target atom of an edge lies in the edge's own partition. `trip_source`: values below 4096 name an edge of the partition before the slot's edge, the next 4096 one of its own partition, the last 4096 one of the partition after it, the partitions closing into a loop. `quad_source`: values below 4096 name an edge of the partition before the slot's edge, the next 4096 one of its own partition, the last 4096 one of the partition after it, the partitions closing into a loop.
All inputs are finite; a program needn't handle non-finite values.
Results may differ from the reference program's by a relative error of at most 0.014.
Values may be sent and summed in bfloat16 or wider, within the bound.
No kernel may reach another device: no remote copies, remote signals or barrier semaphores. Data moves between devices by JAX's collectives and lax.ppermute only.
A program may use at most 320 MiB of HBM per device.

```python
import jax
import jax.numpy as jnp
from jax import lax

D = 512
DA = 256
TRIPLET_WIDTH = 64
DQ = 32
R = 128
CIRCULAR_WIDTH = 16
SBF = 32
TAGS = 3
TRIPLET_SLOTS = 16
KQ = 8
NBR = 32
A_DEV = 128
E_DEV = 4096
ATOMS = 1024
EDGE_COUNT = 32768


def near_index(key, leading, block_size, total):
    partitions = EDGE_COUNT // E_DEV
    owner_part = jnp.arange(EDGE_COUNT, dtype=jnp.int32) // E_DEV
    key_one, key_two = jax.random.split(key)
    offset = jax.random.randint(key_one, leading + (EDGE_COUNT,), -1, 2)
    within = jax.random.randint(key_two, leading + (EDGE_COUNT,), 0, block_size)
    picked = (owner_part + offset) % partitions * block_size + within
    flattened = picked.reshape(-1).at[0].set(total - 1).at[1].set(0)
    return flattened.reshape(picked.shape).astype(jnp.int32)


def slot_window(key, leading):
    key_one, key_two = jax.random.split(key)
    offset = jax.random.randint(key_one, leading + (EDGE_COUNT,), 0, 3)
    within = jax.random.randint(key_two, leading + (EDGE_COUNT,), 0, E_DEV)
    picked = offset * E_DEV + within
    flattened = picked.reshape(-1).at[0].set(3 * E_DEV - 1).at[1].set(0)
    return flattened.reshape(picked.shape).astype(jnp.int32)


def keep_slots(key, slots):
    partitions = EDGE_COUNT // E_DEV
    owner_part = jnp.arange(EDGE_COUNT, dtype=jnp.int32) // E_DEV
    key_one, key_two = jax.random.split(key)
    density_level = jax.random.randint(key_one, (partitions,), 0, 12)
    random_draws = jax.random.randint(key_two, (slots, EDGE_COUNT), 0, 20)
    picked = (random_draws < 9 + density_level[owner_part][None, :]).astype(jnp.int32)
    flattened = picked.reshape(-1).at[0].set(0).at[1].set(1)
    return flattened.reshape(picked.shape)


def draw_edge_source(key, part):
    return near_index(jax.random.fold_in(key, 15), (), A_DEV, ATOMS)


def draw_edge_target(key, part):
    owner_part = jnp.arange(EDGE_COUNT, dtype=jnp.int32) // E_DEV
    within = jax.random.randint(jax.random.fold_in(key, 16), (EDGE_COUNT,), 0, A_DEV)
    picked = owner_part * A_DEV + within
    return picked.at[0].set(0).at[EDGE_COUNT - 1].set(ATOMS - 1).astype(jnp.int32)


def draw_trip_source(key, part):
    return slot_window(jax.random.fold_in(key, 11), (TRIPLET_SLOTS,))


def draw_trip_mask(key, part):
    return keep_slots(jax.random.fold_in(key, 12), TRIPLET_SLOTS)


def draw_quad_source(key, part):
    return slot_window(jax.random.fold_in(key, 13), (KQ,))


def draw_quad_mask(key, part):
    return keep_slots(jax.random.fold_in(key, 14), KQ)


def set_ends(values, rng, least, top_value):
    place = [jax.random.randint(jax.random.fold_in(rng, axis), (), 0, length) for axis, length in enumerate(values.shape)]
    main_axis = values.shape.index(max(values.shape))
    beside = place[:main_axis] + [(place[main_axis] + 1) % values.shape[main_axis]] + place[main_axis + 1:]
    return values.at[tuple(place)].set(least).at[tuple(beside)].set(top_value)


def shard_levels(stream_key, dims, cuts, smallest, high):
    level, own = 1.0, jax.random.fold_in(stream_key, 6)
    for dim, parts in cuts:
        heights = jnp.exp(jax.random.uniform(jax.random.fold_in(own, dim), (parts,), jnp.float32, smallest / len(cuts), high / len(cuts)))
        level = level * jnp.repeat(heights, dims[dim] // parts).reshape([-1 if axis == dim else 1 for axis in range(len(dims))])
    return level


def gaussian(own_key, extent, scale, reach, cuts=(), kind=jnp.bfloat16):
    values = jax.random.normal(own_key, extent, jnp.float32) * scale
    if len(cuts) > 0:
        values = shard_levels(own_key, extent, cuts, -0.22, 0.18) * values
    return jnp.clip(values, min=-reach, max=reach).astype(kind)


def setup_inputs(seed: int = 0) -> dict:
    keys = jax.random.split(jax.random.key(seed), 33)
    edge_emb = gaussian(keys[0], (EDGE_COUNT, D), 1.0, 6.0, ((0, 8), (1, 4)))
    atom_emb = gaussian(keys[1], (ATOMS, DA), 1.0, 6.0, ((0, 8),))
    radial = jnp.clip(1.0 * jax.random.uniform(keys[2], (EDGE_COUNT, R), jnp.float32) ** shard_levels(keys[2], (EDGE_COUNT, R), ((0, 8),), -0.2, 0.2), 0.0, 1.0).astype(jnp.bfloat16)
    circular = gaussian(keys[3], (CIRCULAR_WIDTH, TRIPLET_SLOTS, EDGE_COUNT), 1.0, 6.0, ((2, 8),))
    spherical = gaussian(keys[4], (SBF, KQ, EDGE_COUNT), 1.0, 6.0, ((2, 8),))
    atom_tags = set_ends(jax.random.randint(keys[5], (ATOMS,), 0, TAGS), jax.random.fold_in(keys[5], 1), 0, TAGS - 1).astype(jnp.int32)
    edge_source = draw_edge_source(jax.random.fold_in(keys[32], 71), 0)
    edge_target = draw_edge_target(jax.random.fold_in(keys[32], 71), 0)
    trip_source = draw_trip_source(jax.random.fold_in(keys[32], 71), 0)
    trip_mask = draw_trip_mask(jax.random.fold_in(keys[32], 71), 0)
    quad_source = draw_quad_source(jax.random.fold_in(keys[32], 71), 0)
    quad_mask = draw_quad_mask(jax.random.fold_in(keys[32], 71), 0)
    triplet_down_weight = gaussian(keys[12], (D, TRIPLET_WIDTH), D ** -0.5, 0.25, ((1, 4),))
    trip_radial = gaussian(keys[13], (R, TRIPLET_WIDTH), R ** -0.5, 0.5, ((1, 4),))
    triplet_bilinear_weight = gaussian(keys[14], (CIRCULAR_WIDTH, TRIPLET_WIDTH, TRIPLET_WIDTH), (CIRCULAR_WIDTH * TRIPLET_WIDTH) ** -0.5, 0.1875, ((1, 4),))
    trip_up = gaussian(keys[15], (TRIPLET_WIDTH, D), TRIPLET_WIDTH ** -0.5, 0.75, ((1, 4),))
    quad_down = gaussian(keys[16], (D, DQ), D ** -0.5, 0.25, ((1, 4),))
    quad_radial = gaussian(keys[17], (R, DQ), R ** -0.5, 0.5, ((1, 4),))
    quad_bilinear = gaussian(keys[18], (SBF, DQ, DQ), (SBF * DQ) ** -0.5, 0.1875, ((1, 4),))
    quad_up = gaussian(keys[19], (DQ, D), DQ ** -0.5, 1.0, ((1, 4),))
    source_proj = gaussian(keys[20], (DA, D), DA ** -0.5, 0.375, ((1, 4),))
    target_proj = gaussian(keys[21], (DA, D), DA ** -0.5, 0.375, ((1, 4),))
    resid_first = gaussian(keys[22], (D, D), D ** -0.5, 0.25, ((1, 4),))
    resid_second = gaussian(keys[23], (D, D), D ** -0.5, 0.25, ((0, 4),))
    edge_to_atom = gaussian(keys[24], (D, DA), (D * NBR) ** -0.5, 0.046875, ((0, 4),))
    atom_update = gaussian(keys[25], (DA, DA), DA ** -0.5, 0.375)
    output_first = gaussian(keys[26], (DA, DA), DA ** -0.5, 0.375)
    output_second = gaussian(keys[27], (DA,), DA ** -0.5, 0.375)
    tag_table = gaussian(keys[28], (TAGS, DA), 0.5, 3.0)
    grad_edges = gaussian(keys[29], (EDGE_COUNT, D), 1.0, 6.0, ((0, 8), (1, 4)))
    grad_atoms = gaussian(keys[30], (ATOMS, DA), 1.0, 6.0, ((0, 8),))
    grad_energy = gaussian(keys[31], (ATOMS,), 1.0, 6.0, ((0, 8),), jnp.float32)
    return dict(edge_emb=edge_emb, atom_emb=atom_emb, radial=radial, circular=circular, spherical=spherical, atom_tags=atom_tags, edge_source=edge_source, edge_target=edge_target, trip_source=trip_source, trip_mask=trip_mask, quad_source=quad_source, quad_mask=quad_mask, triplet_down_weight=triplet_down_weight, trip_radial=trip_radial, triplet_bilinear_weight=triplet_bilinear_weight, trip_up=trip_up, quad_down=quad_down, quad_radial=quad_radial, quad_bilinear=quad_bilinear, quad_up=quad_up, source_proj=source_proj, target_proj=target_proj, resid_first=resid_first, resid_second=resid_second, edge_to_atom=edge_to_atom, atom_update=atom_update, output_first=output_first, output_second=output_second, tag_table=tag_table, grad_edges=grad_edges, grad_atoms=grad_atoms, grad_energy=grad_energy)


HIGHEST = lax.Precision.HIGHEST

@jax.custom_vjp
def low(v):
    return lax.optimization_barrier(v.astype(jnp.bfloat16)).astype(jnp.float32)

@jax.custom_vjp
def low_back(v):
    return v

def low_keep(v):
    return (low(v), None)

def low_pass(kept, grad):
    return (grad,)

def back_keep(v):
    return (v, None)

def back_low(kept, grad):
    return (low(grad),)
low.defvjp(low_keep, low_pass)
low_back.defvjp(back_keep, back_low)

def product(first_op, second_op):
    return jnp.dot(first_op, second_op, precision=HIGHEST)

def global_edges(slot_place):
    blocks = EDGE_COUNT // E_DEV
    owner_part = jnp.arange(EDGE_COUNT, dtype=jnp.int32) // E_DEV
    part_index = (owner_part[None, :] + slot_place // E_DEV - 1) % blocks
    return (part_index * E_DEV + slot_place % E_DEV).astype(jnp.int32)

def branch_block(dense_rows, bilinear, pieces):
    basis_vals, source, keep_mask = pieces
    gathered = dense_rows[source]
    weighted = basis_vals * keep_mask.astype(jnp.float32)[None]
    summed = low(jnp.einsum('bke,kew->bwe', weighted, gathered, precision=HIGHEST))
    return jnp.einsum('bwe,bwo->eo', summed, bilinear, precision=HIGHEST)

def branch(dense_rows, bilinear, basis_vals, slot_place, keep_mask):
    blocks = EDGE_COUNT // E_DEV
    source = global_edges(slot_place)
    basis_blocks = jnp.transpose(basis_vals.reshape(basis_vals.shape[0], basis_vals.shape[1], blocks, E_DEV), (2, 0, 1, 3))
    source_blocks = jnp.transpose(source.reshape(source.shape[0], blocks, E_DEV), (1, 0, 2))
    mask_blocks = jnp.transpose(keep_mask.reshape(keep_mask.shape[0], blocks, E_DEV), (1, 0, 2))
    blockwise = jax.checkpoint(lambda pieces: branch_block(dense_rows, bilinear, pieces))
    result = lax.map(blockwise, (basis_blocks, source_blocks, mask_blocks))
    return low(low_back(result.reshape(EDGE_COUNT, bilinear.shape[2])))

def reference(edge_emb, atom_emb, radial, circular, spherical, atom_tags, edge_source, edge_target, trip_source, trip_mask, quad_source, quad_mask, triplet_down_weight, trip_radial, triplet_bilinear_weight, trip_up, quad_down, quad_radial, quad_bilinear, quad_up, source_proj, target_proj, resid_first, resid_second, edge_to_atom, atom_update, output_first, output_second, tag_table, grad_edges, grad_atoms, grad_energy):
    radial_f = radial.astype(jnp.float32)
    circular_f = circular.astype(jnp.float32)
    spherical_f = spherical.astype(jnp.float32)

    def forward(edge_vals, atom_vals, triplet_down_weight, trip_radial, triplet_bilinear_weight, trip_up, quad_down, quad_radial, quad_bilinear, quad_up, source_proj, target_proj, resid_first, resid_second, edge_to_atom, atom_update, output_first, output_second, tag_table):
        trip_dense = low(jax.nn.silu(low_back(product(edge_vals, triplet_down_weight))) * low_back(product(radial_f, trip_radial)))
        quad_dense = low(jax.nn.silu(low_back(product(edge_vals, quad_down))) * low_back(product(radial_f, quad_radial)))
        trip_agg = branch(trip_dense, triplet_bilinear_weight, circular_f, trip_source, trip_mask)
        quad_agg = branch(quad_dense, quad_bilinear, spherical_f, quad_source, quad_mask)
        atom_full = atom_vals + tag_table[atom_tags]
        atom_low = low(atom_full)
        message = low_back(product(atom_low[edge_source], source_proj) + product(atom_low[edge_target], target_proj))
        trip_out = jax.nn.silu(low_back(product(trip_agg, trip_up)))
        quad_out = jax.nn.silu(low_back(product(quad_agg, quad_up)))
        hidden_one = edge_vals + trip_out + quad_out + jax.nn.silu(message)
        first_reduced = low(jax.nn.silu(low_back(product(low(hidden_one), resid_first))))
        hidden_two = hidden_one + jax.nn.silu(low_back(product(first_reduced, resid_second)))
        edges_low = low(hidden_two)
        edge_part = low_back(product(edges_low, edge_to_atom))
        atom_sum = jax.ops.segment_sum(edge_part, edge_target, num_segments=ATOMS)
        atoms_new = atom_full + jax.nn.silu(low_back(product(low(atom_sum), atom_update)))
        atoms_low = low(atoms_new)
        output_low = low(jax.nn.silu(low_back(product(atoms_low, output_first))))
        energy = product(output_low, output_second)
        return (edges_low, atoms_low, energy)
    primals = (edge_emb, atom_emb, triplet_down_weight, trip_radial, triplet_bilinear_weight, trip_up, quad_down, quad_radial, quad_bilinear, quad_up, source_proj, target_proj, resid_first, resid_second, edge_to_atom, atom_update, output_first, output_second, tag_table)
    primals = tuple((element.astype(jnp.float32) for element in primals))
    outputs, pullback = jax.vjp(forward, *primals)
    grads = pullback((grad_edges.astype(jnp.float32), grad_atoms.astype(jnp.float32), grad_energy))
    return (outputs[0].astype(jnp.bfloat16), outputs[1].astype(jnp.bfloat16), outputs[2], grads[0], grads[1], grads[2], grads[3], grads[4], grads[5], grads[6], grads[7], grads[8], grads[9], grads[10], grads[11], grads[12], grads[13], grads[14], grads[15], grads[16], grads[17], grads[18])
```

```python
import functools

import jax
import jax.numpy as jnp
from jax import lax
from jax.experimental import pallas as pl
from jax.experimental.pallas import tpu as pltpu
from jax.sharding import PartitionSpec as P

TAGS = 3
LANES = 128
BLOCK = 16
BF16 = jnp.bfloat16
F32 = jnp.float32
HIGHEST = lax.Precision.HIGHEST


def chan_swap(value, mask):
    count = lax.axis_size("chan")
    return lax.ppermute(value, "chan", [(i, i ^ mask) for i in range(count)])


def edge_swap(value, mask):
    count = lax.axis_size("edge")
    return lax.ppermute(value, "edge", [(i, i ^ mask) for i in range(count)])


def edge_shift(value, step):
    count = lax.axis_size("edge")
    return lax.ppermute(value, "edge", [(i, (i + step) % count) for i in range(count)])


def pick(blocks, place):
    return lax.dynamic_index_in_dim(blocks, place, 0, keepdims=False)


def reorder(blocks, rank):
    low_bit = (rank & 1) == 1
    high_bit = (rank & 2) == 2
    first = [jnp.where(low_bit, blocks[i ^ 1], blocks[i]) for i in range(4)]
    return [jnp.where(high_bit, first[i ^ 2], first[i]) for i in range(4)]


def gather_chan(value):
    across = chan_swap(value, 2)
    beside = chan_swap(jnp.stack([value, across]), 1)
    return [value, beside[0], across, beside[1]]


def exchange(blocks, rank):
    got = [pick(blocks, rank)]
    for step in (1, 2, 3):
        got.append(chan_swap(pick(blocks, rank ^ step), step))
    return reorder(got, rank)


def silu_grad(pre_act):
    sigmoid = jax.nn.sigmoid(pre_act)
    return sigmoid * (1.0 + pre_act * (1.0 - sigmoid))


def matmul(first_op, second_op):
    return jnp.dot(first_op, second_op, preferred_element_type=F32)


def inner(first_op, second_op):
    return lax.dot_general(
        first_op, second_op, (((0,), (0,)), ((), ())), preferred_element_type=F32
    )


def outer(first_op, second_op):
    return lax.dot_general(
        first_op, second_op, (((1,), (1,)), ((), ())), preferred_element_type=F32
    )


def block_weights(basis_ref, block, diagonal):
    basis = basis_ref[block].astype(F32)
    count, width = basis.shape
    spread = jnp.broadcast_to(basis[:, None, :], (count, BLOCK, width))
    spread = spread.reshape(count * BLOCK, width)
    return jnp.where(diagonal, spread, 0.0).astype(BF16)


def diagonal_mask(rows, width):
    row = lax.broadcasted_iota(jnp.int32, (rows, width), 0) % BLOCK
    col = lax.broadcasted_iota(jnp.int32, (rows, width), 1) % BLOCK
    return row == col


def gather_body(
    index_ref, packed_ref, basis_ref, bilinear_ref, agg_ref, sum_ref, table, rows_a, rows_b
):
    pieces, piece_rows, _ = packed_ref.shape
    basis_count, edges, width = sum_ref.shape
    slots = basis_ref.shape[2] // BLOCK
    folds = LANES // width
    step = min(piece_rows, 128)
    per_piece = piece_rows // step

    def unpack(turn, _):
        piece = turn // per_piece
        start = pl.multiple_of((turn % per_piece) * step, step)
        values = packed_ref[piece, pl.ds(start, step), :].astype(F32)
        for fold in range(folds):
            place = pl.multiple_of((piece * folds + fold) * piece_rows + start, step)
            shifted = values
            if fold:
                shifted = pltpu.roll(values, LANES - fold * width, 1)
            table[pl.ds(place, step), :] = shifted
        return 0

    lax.fori_loop(0, pieces * per_piece, unpack, 0)
    diagonal = diagonal_mask(basis_count * BLOCK, slots * BLOCK)

    def fetch(block, rows):
        base = block * BLOCK
        for slot in range(slots):
            for within in range(BLOCK):
                place = index_ref[slot * edges + base + within]
                at = slot * BLOCK + within
                rows[pl.ds(at, 1), :] = table[pl.ds(place, 1), :]

    def combine(block, rows):
        weights = block_weights(basis_ref, block, diagonal)
        got = matmul(weights, rows[...].astype(BF16))[:, :width].astype(BF16)
        start = pl.multiple_of(block * BLOCK, BLOCK)
        sum_ref[:, pl.ds(start, BLOCK), :] = got.reshape(basis_count, BLOCK, width)

    blocks = edges // BLOCK
    fetch(0, rows_a)

    def turn(pair, _):
        fetch(2 * pair + 1, rows_b)
        combine(2 * pair, rows_a)
        fetch(jnp.minimum(2 * pair + 2, blocks - 1), rows_a)
        combine(2 * pair + 1, rows_b)
        return 0

    lax.fori_loop(0, blocks // 2, turn, 0)
    total = matmul(sum_ref[0], bilinear_ref[0])
    for basis in range(1, basis_count):
        total = total + matmul(sum_ref[basis], bilinear_ref[basis])
    agg_ref[...] = total.astype(BF16)


def branch_forward(index, packed, basis, bilinear, edges, name):
    basis_count, width, out_width = bilinear.shape
    table_rows = packed.shape[0] * edges
    vmem = pl.BlockSpec(memory_space=pltpu.VMEM)
    return pl.pallas_call(
        gather_body,
        out_shape=(
            jax.ShapeDtypeStruct((edges, out_width), BF16),
            jax.ShapeDtypeStruct((basis_count, edges, width), BF16),
        ),
        in_specs=[pl.BlockSpec(memory_space=pltpu.SMEM), vmem, vmem, vmem],
        out_specs=(vmem, vmem),
        scratch_shapes=[
            pltpu.VMEM((table_rows, LANES), F32),
            pltpu.VMEM((basis.shape[2], LANES), F32),
            pltpu.VMEM((basis.shape[2], LANES), F32),
        ],
        compiler_params=pltpu.CompilerParams(vmem_limit_bytes=56 << 20),
        name=name,
    )(index, packed, basis, bilinear)


TABLES = 4


def scatter_body(
    index_ref, basis_ref, grad_ref, bilinear_ref, packed_ref, part, rows_a, rows_b, *tables
):
    pieces, piece_rows, _ = packed_ref.shape
    basis_count, edges, width = part.shape
    slots = basis_ref.shape[2] // BLOCK
    folds = LANES // width
    chunk = 256
    table_rows = tables[0].shape[0]

    def clear(turn, _):
        start = pl.multiple_of(turn * chunk, chunk)
        for table in tables:
            table[pl.ds(start, chunk), :] = jnp.zeros((chunk, LANES), F32)
        return 0

    lax.fori_loop(0, table_rows // chunk, clear, 0)
    rows_a[...] = jnp.zeros_like(rows_a)
    rows_b[...] = jnp.zeros_like(rows_b)
    for basis in range(basis_count):
        part[basis] = outer(grad_ref[...], bilinear_ref[basis]).astype(BF16)
    diagonal = diagonal_mask(basis_count * BLOCK, slots * BLOCK)

    def spread(block, rows):
        weights = block_weights(basis_ref, block, diagonal)
        start = pl.multiple_of(block * BLOCK, BLOCK)
        values = part[:, pl.ds(start, BLOCK), :].reshape(basis_count * BLOCK, width)
        rows[:, :width] = inner(weights, values)

    def store(block, rows):
        base = block * BLOCK
        for slot in range(slots):
            for within in range(BLOCK):
                place = index_ref[slot * edges + base + within]
                at = slot * BLOCK + within
                table = tables[at % len(tables)]
                table[pl.ds(place, 1), :] += rows[pl.ds(at, 1), :]

    blocks = edges // BLOCK
    spread(0, rows_a)

    def turn(pair, _):
        spread(2 * pair + 1, rows_b)
        store(2 * pair, rows_a)
        spread(jnp.minimum(2 * pair + 2, blocks - 1), rows_a)
        store(2 * pair + 1, rows_b)
        return 0

    lax.fori_loop(0, blocks // 2, turn, 0)
    step = min(piece_rows, 128)
    per_piece = piece_rows // step
    lane = lax.broadcasted_iota(jnp.int32, (step, LANES), 1) // width

    def pack(turn, _):
        piece = turn // per_piece
        start = pl.multiple_of((turn % per_piece) * step, step)
        joined = jnp.zeros((step, LANES), F32)
        for fold in range(folds):
            place = pl.multiple_of((piece * folds + fold) * piece_rows + start, step)
            total = tables[0][pl.ds(place, step), :]
            for table in tables[1:]:
                total = total + table[pl.ds(place, step), :]
            if fold:
                total = pltpu.roll(total, fold * width, 1)
            joined = jnp.where(lane == fold, total, joined)
        packed_ref[piece, pl.ds(start, step), :] = joined.astype(BF16)
        return 0

    lax.fori_loop(0, pieces * per_piece, pack, 0)


def branch_backward(index, basis, grad, bilinear, pieces, name):
    edges = grad.shape[0]
    basis_count, width, _ = bilinear.shape
    vmem = pl.BlockSpec(memory_space=pltpu.VMEM)
    return pl.pallas_call(
        scatter_body,
        out_shape=jax.ShapeDtypeStruct((pieces, edges * width // LANES, LANES), BF16),
        in_specs=[pl.BlockSpec(memory_space=pltpu.SMEM), vmem, vmem, vmem],
        out_specs=vmem,
        scratch_shapes=[
            pltpu.VMEM((basis_count, edges, width), BF16),
            pltpu.VMEM((basis.shape[2], LANES), F32),
            pltpu.VMEM((basis.shape[2], LANES), F32),
        ]
        + [pltpu.VMEM((pieces * edges, LANES), F32)] * TABLES,
        compiler_params=pltpu.CompilerParams(vmem_limit_bytes=58 << 20),
        name=name,
    )(index, basis, grad, bilinear)


def fold_lanes(rows):
    count, width = rows.shape
    folds = LANES // width
    each = count // folds
    return jnp.concatenate([rows[i * each : (i + 1) * each] for i in range(folds)], axis=1)


def unfold_lanes(packed, width):
    folds = LANES // width
    return jnp.concatenate([packed[:, i * width : (i + 1) * width] for i in range(folds)], axis=0)


def columns(array):
    return jnp.concatenate(
        [array[:, i : i + LANES] for i in range(0, array.shape[1], LANES)], axis=0
    )


def uncolumns(rows, width):
    each = rows.shape[0] * LANES // width
    return jnp.concatenate(
        [rows[i * each : (i + 1) * each] for i in range(width // LANES)], axis=1
    )


def slot_blocks(basis_vals, keep_mask):
    count, slots, edges = basis_vals.shape
    weighted = basis_vals * keep_mask.astype(BF16)[None]
    split = weighted.reshape(count, slots, edges // BLOCK, BLOCK)
    return jnp.transpose(split, (2, 0, 1, 3)).reshape(edges // BLOCK, count, slots * BLOCK)


def edge_reduce(rows):
    count = lax.axis_size("edge")
    rank = lax.axis_index("edge")
    steps = []
    size = 1
    while size < count:
        steps.append(size)
        size *= 2
    total = rows.shape[0]
    padded = -(-total // (16 * count)) * 16 * count
    value = jnp.pad(rows, ((0, padded - total), (0, 0)))
    for mask in steps:
        half = value.shape[0] // 2
        bit = (rank & mask) != 0
        keep = jnp.where(bit, value[half:], value[:half])
        send = jnp.where(bit, value[:half], value[half:])
        got = edge_swap(send, mask)
        value = (keep.astype(F32) + got.astype(F32)).astype(BF16)
    for mask in reversed(steps):
        bit = (rank & mask) != 0
        got = edge_swap(value, mask)
        value = jnp.concatenate(
            [jnp.where(bit, got, value), jnp.where(bit, value, got)], axis=0
        )
    return value[:total]


def edge_sum(value):
    count = lax.axis_size("edge")
    size = 1
    while size < count:
        value = value + edge_swap(value, size)
        size *= 2
    return value


def per_device(
    edge_emb,
    atom_emb,
    radial,
    circular,
    spherical,
    atom_tags,
    edge_source,
    edge_target,
    trip_source,
    trip_mask,
    quad_source,
    quad_mask,
    triplet_down_weight,
    trip_radial,
    triplet_bilinear_weight,
    trip_up,
    quad_down,
    quad_radial,
    quad_bilinear,
    quad_up,
    source_proj,
    target_proj,
    resid_first,
    resid_second,
    edge_to_atom,
    atom_update,
    output_first,
    output_second,
    tag_table,
    grad_edges,
    grad_atoms,
    grad_energy,
):
    edges_here = edge_emb.shape[0]
    atoms_here = atom_emb.shape[0]
    parts = lax.axis_size("chan")
    edge_parts = lax.axis_size("edge")
    rank = lax.axis_index("chan")
    edge_rank = lax.axis_index("edge")
    edges = edges_here // parts
    cols = edge_emb.shape[1]
    start = rank * edges

    def own(array, axis):
        return lax.dynamic_slice_in_dim(array, start, edges, axis)

    own_edges = jnp.concatenate(exchange(edge_emb.reshape(parts, edges, cols), rank), axis=1)
    grad_two = jnp.concatenate(exchange(grad_edges.reshape(parts, edges, cols), rank), axis=1)

    trip_cols = triplet_down_weight.shape[1]
    quad_cols = quad_down.shape[1]
    small = jnp.concatenate(
        [
            jnp.concatenate([triplet_down_weight, quad_down], axis=1),
            jnp.concatenate([trip_radial, quad_radial], axis=1),
        ],
        axis=0,
    ).T
    small = jnp.stack(reorder(gather_chan(small), rank))
    trip_both = small[:, :trip_cols].reshape(parts * trip_cols, -1).T
    quad_both = small[:, trip_cols:].reshape(parts * quad_cols, -1).T
    both = jnp.concatenate([trip_both, quad_both], axis=1)
    channels = parts * cols
    down_full, radial_full = both[:channels], both[channels:]
    trip_width = trip_both.shape[1]

    large = jnp.concatenate(
        [
            fold_lanes(triplet_bilinear_weight.reshape(-1, triplet_bilinear_weight.shape[2])),
            fold_lanes(quad_bilinear.reshape(-1, quad_bilinear.shape[2])),
            trip_up,
            quad_up,
            source_proj,
            target_proj,
            resid_first,
            columns(resid_second),
            columns(edge_to_atom),
        ],
        axis=0,
    )
    large = reorder(gather_chan(large), rank)
    sizes = [
        triplet_bilinear_weight.size // LANES,
        quad_bilinear.size // LANES,
        trip_up.shape[0],
        quad_up.shape[0],
        source_proj.shape[0],
        target_proj.shape[0],
        resid_first.shape[0],
        resid_second.size // LANES,
        edge_to_atom.size // LANES,
    ]
    offsets = [sum(sizes[:i]) for i in range(len(sizes) + 1)]

    def piece(item):
        return [block[offsets[item] : offsets[item + 1]] for block in large]

    trip_bil = jnp.concatenate(
        [
            unfold_lanes(block, triplet_bilinear_weight.shape[2]).reshape(
                triplet_bilinear_weight.shape
            )
            for block in piece(0)
        ],
        axis=1,
    )
    quad_bil = jnp.concatenate(
        [
            unfold_lanes(block, quad_bilinear.shape[2]).reshape(quad_bilinear.shape)
            for block in piece(1)
        ],
        axis=1,
    )
    trip_up_full = jnp.concatenate(piece(2), axis=1)
    quad_up_full = jnp.concatenate(piece(3), axis=1)
    proj_full = jnp.concatenate(
        [jnp.concatenate(piece(4), axis=1), jnp.concatenate(piece(5), axis=1)], axis=0
    )
    first_full = jnp.concatenate(piece(6), axis=1)
    second_full = jnp.concatenate(
        [uncolumns(block, resid_second.shape[1]) for block in piece(7)], axis=0
    )
    to_atom_full = jnp.concatenate(
        [uncolumns(block, edge_to_atom.shape[1]) for block in piece(8)], axis=0
    )

    own_radial = own(radial, 0)
    down_pre = matmul(own_edges, down_full)
    radial_pre = matmul(own_radial, radial_full)
    dense = (jax.nn.silu(down_pre) * radial_pre).astype(BF16)
    trip_piece = fold_lanes(dense[:, :trip_width])
    quad_piece = fold_lanes(dense[:, trip_width:])
    wire = jnp.concatenate([trip_piece, quad_piece], axis=0)
    before = edge_shift(wire, 1)
    after = edge_shift(wire, -1)
    own_pieces = gather_chan(wire)
    side_pieces = gather_chan(jnp.stack([before, after]))
    all_pieces = jnp.stack(
        [side[0] for side in side_pieces] + own_pieces + [side[1] for side in side_pieces]
    )
    trip_rows = trip_piece.shape[0]
    trip_packed = all_pieces[:, :trip_rows]
    quad_packed = all_pieces[:, trip_rows:]

    tag_onehot = (atom_tags[:, None] == jnp.arange(TAGS)[None, :]).astype(F32)
    atom_full = atom_emb.astype(F32) + jnp.dot(
        tag_onehot, tag_table.astype(F32), precision=HIGHEST
    )
    atom_low = atom_full.astype(BF16)
    atom_wide = jnp.concatenate(
        [edge_shift(atom_low, 1), atom_low, edge_shift(atom_low, -1)], axis=0
    )
    atom_total = edge_parts * atoms_here
    source_local = (own(edge_source, 0) - (edge_rank - 1) * atoms_here) % atom_total
    target_local = own(edge_target, 0) - edge_rank * atoms_here
    source_hot = (source_local[:, None] == jnp.arange(3 * atoms_here)[None, :]).astype(BF16)
    target_hot = (target_local[:, None] == jnp.arange(atoms_here)[None, :]).astype(BF16)
    ends = jnp.concatenate(
        [
            matmul(source_hot, atom_wide).astype(BF16),
            matmul(target_hot, atom_low).astype(BF16),
        ],
        axis=1,
    )
    message = matmul(ends, proj_full)

    def places(source):
        local = own(source, 1)
        within = local % edges_here
        owner = (within // edges) ^ rank
        return ((local // edges_here) * edges_here + owner * edges + within % edges).reshape(-1)

    trip_index = places(trip_source)
    quad_index = places(quad_source)
    trip_basis = slot_blocks(own(circular, 2), own(trip_mask, 1))
    quad_basis = slot_blocks(own(spherical, 2), own(quad_mask, 1))
    trip_agg, trip_sum = branch_forward(
        trip_index, trip_packed, trip_basis, trip_bil, edges, "trip_gather"
    )
    quad_agg, quad_sum = branch_forward(
        quad_index, quad_packed, quad_basis, quad_bil, edges, "quad_gather"
    )

    trip_out_pre = matmul(trip_agg, trip_up_full)
    quad_out_pre = matmul(quad_agg, quad_up_full)
    hidden_one = (
        own_edges.astype(F32)
        + jax.nn.silu(trip_out_pre)
        + jax.nn.silu(quad_out_pre)
        + jax.nn.silu(message)
    )
    hidden_low = hidden_one.astype(BF16)
    first_pre = matmul(hidden_low, first_full)
    first_low = jax.nn.silu(first_pre).astype(BF16)
    second_pre = matmul(first_low, second_full)
    edges_low = (hidden_one + jax.nn.silu(second_pre)).astype(BF16)
    edge_sums = inner(target_hot, edges_low)
    sums_high = edge_sums.astype(BF16)
    sums_rest = (edge_sums - sums_high.astype(F32)).astype(BF16)
    atom_sum = matmul(sums_high, to_atom_full) + matmul(sums_rest, to_atom_full)
    atom_sum = atom_sum + chan_swap(atom_sum, 1)
    atom_sum = atom_sum + chan_swap(atom_sum, 2)

    atom_sum_low = atom_sum.astype(BF16)
    update_pre = matmul(atom_sum_low, atom_update)
    atoms_new = atom_full + jax.nn.silu(update_pre)
    atoms_low = atoms_new.astype(BF16)
    output_pre = matmul(atoms_low, output_first)
    output_low = jax.nn.silu(output_pre).astype(BF16)
    energy = matmul(output_low, output_second)
    output_second_grad = jnp.dot(grad_energy, output_low.astype(F32), precision=HIGHEST)
    output_grad = (
        grad_energy[:, None] * output_second.astype(F32)[None, :] * silu_grad(output_pre)
    ).astype(BF16)
    output_first_grad = inner(atoms_low, output_grad)
    atoms_new_grad = grad_atoms.astype(F32) + outer(output_grad, output_first)
    update_grad = (atoms_new_grad * silu_grad(update_pre)).astype(BF16)
    atom_update_grad = inner(atom_sum_low, update_grad)
    atom_sum_grad = outer(update_grad, atom_update).astype(BF16)

    edge_part_grad = matmul(target_hot, atom_sum_grad).astype(BF16)
    edge_to_atom_grad = inner(edges_low, edge_part_grad)
    two_grad = grad_two.astype(F32) + outer(edge_part_grad, to_atom_full)
    second_grad = (two_grad * silu_grad(second_pre)).astype(BF16)
    resid_second_grad = inner(first_low, second_grad)
    first_grad = (outer(second_grad, second_full) * silu_grad(first_pre)).astype(BF16)
    resid_first_grad = inner(hidden_low, first_grad)
    one_grad = two_grad + outer(first_grad, first_full)
    trip_out_grad = (one_grad * silu_grad(trip_out_pre)).astype(BF16)
    quad_out_grad = (one_grad * silu_grad(quad_out_pre)).astype(BF16)
    message_grad = (one_grad * silu_grad(message)).astype(BF16)
    trip_up_grad = inner(trip_agg, trip_out_grad)
    quad_up_grad = inner(quad_agg, quad_out_grad)
    trip_agg_grad = outer(trip_out_grad, trip_up_full).astype(BF16)
    quad_agg_grad = outer(quad_out_grad, quad_up_full).astype(BF16)
    proj_grad = inner(ends, message_grad)
    width = atom_low.shape[1]
    source_sums = inner(source_hot, message_grad).astype(BF16)
    target_sums = inner(target_hot, message_grad).astype(BF16)
    source_back = outer(source_sums, proj_full[:width])
    target_back = outer(target_sums, proj_full[width:])
    wide_atoms = source_back.reshape(3, atoms_here, width)
    wide_atoms = wide_atoms.at[1].add(target_back)

    pieces = 3 * parts
    trip_table = branch_backward(
        trip_index, trip_basis, trip_agg_grad, trip_bil, pieces, "trip_scatter"
    )
    quad_table = branch_backward(
        quad_index, quad_basis, quad_agg_grad, quad_bil, pieces, "quad_scatter"
    )
    table = jnp.concatenate([trip_table, quad_table], axis=1).reshape(3, parts, -1, LANES)
    got = chan_swap(jnp.stack([table[:, 1], table[:, 3]]), 1).astype(F32)
    mine = table[:, 0].astype(F32) + got[0]
    other = (table[:, 2].astype(F32) + got[1]).astype(BF16)
    mine = mine + chan_swap(other, 2).astype(F32)
    to_before = mine[0].astype(BF16)
    to_after = mine[2].astype(BF16)
    branch_grad = (
        mine[1] + edge_shift(to_before, -1).astype(F32) + edge_shift(to_after, 1).astype(F32)
    )
    branch_grad = jnp.concatenate(
        [
            unfold_lanes(branch_grad[:trip_rows], trip_width),
            unfold_lanes(branch_grad[trip_rows:], both.shape[1] - trip_width),
        ],
        axis=1,
    )
    wide_low = wide_atoms.astype(BF16)
    wide_atoms = wide_atoms + chan_swap(wide_low, 1).astype(F32)
    wide_low = wide_atoms.astype(BF16)
    wide_atoms = wide_atoms + chan_swap(wide_low, 2).astype(F32)
    atom_grad = (
        atoms_new_grad
        + wide_atoms[1]
        + edge_shift(wide_atoms[0].astype(BF16), -1).astype(F32)
        + edge_shift(wide_atoms[2].astype(BF16), 1).astype(F32)
    )
    tag_table_grad = jnp.dot(tag_onehot.T, atom_grad, precision=HIGHEST)

    down_grad = (branch_grad * radial_pre * silu_grad(down_pre)).astype(BF16)
    radial_grad = (branch_grad * jax.nn.silu(down_pre)).astype(BF16)
    down_weight_grad = inner(own_edges, down_grad)
    radial_weight_grad = inner(own_radial, radial_grad)
    edge_grad = one_grad + outer(down_grad, down_full)

    def give_back(array):
        blocks = jnp.stack([array[:, i * cols : (i + 1) * cols] for i in range(parts)])
        return jnp.concatenate(exchange(blocks, rank), axis=0)

    edges_out = give_back(edges_low)
    edge_grad = give_back(edge_grad.astype(BF16)).astype(F32)

    def split(array, axis):
        return jnp.split(array, parts, axis=axis)

    trip_bilinear_grad = jnp.einsum(
        "cei,eo->cio", trip_sum, trip_agg_grad, preferred_element_type=F32
    )
    quad_bilinear_grad = jnp.einsum(
        "cei,eo->cio", quad_sum, quad_agg_grad, preferred_element_type=F32
    )
    small_grad = jnp.concatenate([down_weight_grad, radial_weight_grad], axis=0)
    members = [
        [
            fold_lanes(block.reshape(-1, trip_bil.shape[2]))
            for block in split(trip_bilinear_grad, 1)
        ],
        [
            fold_lanes(block.reshape(-1, quad_bil.shape[2]))
            for block in split(quad_bilinear_grad, 1)
        ],
        split(trip_up_grad, 1),
        split(quad_up_grad, 1),
        split(proj_grad[:width], 1),
        split(proj_grad[width:], 1),
        split(resid_first_grad, 1),
        [columns(block) for block in split(resid_second_grad, 0)],
        [columns(block) for block in split(edge_to_atom_grad, 0)],
        [
            columns(jnp.concatenate([trip_block, quad_block], axis=1).T)
            for trip_block, quad_block in zip(
                split(small_grad[:, :trip_width], 1), split(small_grad[:, trip_width:], 1)
            )
        ],
    ]
    packed = [
        jnp.concatenate([member[i] for member in members], axis=0).astype(BF16)
        for i in range(parts)
    ]
    packed = reorder(packed, rank)
    got = chan_swap(jnp.stack([packed[1], packed[3]]), 1).astype(F32)
    mine = packed[0].astype(F32) + got[0]
    other = (packed[2].astype(F32) + got[1]).astype(BF16)
    mine = (mine + chan_swap(other, 2).astype(F32)).astype(BF16)
    atom_rows = jnp.concatenate(
        [columns(atom_update_grad), columns(output_first_grad)], axis=0
    ).astype(BF16)
    early = mine.shape[0]
    summed = edge_reduce(jnp.concatenate([mine, atom_rows], axis=0)).astype(F32)
    tiny = edge_sum(jnp.concatenate([output_second_grad[None], tag_table_grad], axis=0))
    sizes.append(small.shape[1] * small.shape[2] // LANES)
    offsets = [sum(sizes[:i]) for i in range(len(sizes) + 1)]
    parts_out = [summed[offsets[i] : offsets[i + 1]] for i in range(len(sizes))]
    small_out = uncolumns(parts_out[9], small.shape[2]).T
    atom_out = summed[early:]
    half = atom_out.shape[0] // 2
    return (
        edges_out,
        atoms_low,
        energy,
        edge_grad,
        atom_grad,
        small_out[:channels, :trip_cols],
        small_out[channels:, :trip_cols],
        unfold_lanes(parts_out[0], trip_bil.shape[2]).reshape(triplet_bilinear_weight.shape),
        parts_out[2],
        small_out[:channels, trip_cols:],
        small_out[channels:, trip_cols:],
        unfold_lanes(parts_out[1], quad_bil.shape[2]).reshape(quad_bilinear.shape),
        parts_out[3],
        parts_out[4],
        parts_out[5],
        parts_out[6],
        uncolumns(parts_out[7], resid_second.shape[1]),
        uncolumns(parts_out[8], edge_to_atom.shape[1]),
        uncolumns(atom_out[:half], atom_update.shape[1]),
        uncolumns(atom_out[half:], output_first.shape[1]),
        tiny[0],
        tiny[1:],
    )


def solution(mesh):
    return jax.shard_map(
        per_device,
        mesh=mesh,
        in_specs=(
            P("edge", "chan"),
            P("edge", None),
            P("edge", None),
            P(None, None, "edge"),
            P(None, None, "edge"),
            P("edge"),
            P("edge"),
            P("edge"),
            P(None, "edge"),
            P(None, "edge"),
            P(None, "edge"),
            P(None, "edge"),
            P(None, "chan"),
            P(None, "chan"),
            P(None, "chan", None),
            P(None, "chan"),
            P(None, "chan"),
            P(None, "chan"),
            P(None, "chan", None),
            P(None, "chan"),
            P(None, "chan"),
            P(None, "chan"),
            P(None, "chan"),
            P("chan", None),
            P("chan", None),
            P(),
            P(),
            P(),
            P(),
            P("edge", "chan"),
            P("edge", None),
            P("edge"),
        ),
        out_specs=(
            P("edge", "chan"),
            P("edge", None),
            P("edge"),
            P("edge", "chan"),
            P("edge", None),
            P(None, "chan"),
            P(None, "chan"),
            P(None, "chan", None),
            P(None, "chan"),
            P(None, "chan"),
            P(None, "chan"),
            P(None, "chan", None),
            P(None, "chan"),
            P(None, "chan"),
            P(None, "chan"),
            P(None, "chan"),
            P("chan", None),
            P("chan", None),
            P(),
            P(),
            P(),
            P(),
        ),
        check_vma=False,
    )
```

```python
import functools

import jax
import jax.numpy as jnp
from jax import lax
from jax.experimental import pallas as pl
from jax.experimental.pallas import tpu as pltpu
from jax.sharding import PartitionSpec as P

TAGS = 3
LANES = 128
BLOCK = 16
BF16 = jnp.bfloat16
F32 = jnp.float32
HIGHEST = lax.Precision.HIGHEST


def chan_swap(value, mask):
    count = lax.axis_size("chan")
    return lax.ppermute(value, "chan", [(i, i ^ mask) for i in range(count)])


def edge_swap(value, mask):
    count = lax.axis_size("edge")
    return lax.ppermute(value, "edge", [(i, i ^ mask) for i in range(count)])


def edge_shift(value, step):
    count = lax.axis_size("edge")
    return lax.ppermute(value, "edge", [(i, (i + step) % count) for i in range(count)])


def after(value, *others):
    return lax.optimization_barrier((value,) + others)[0]


def gather_direct(value):
    return [value] + [chan_swap(value, step) for step in (1, 2, 3)]


def pick(blocks, place):
    return lax.dynamic_index_in_dim(blocks, place, 0, keepdims=False)


def reorder(blocks, rank):
    low_bit = (rank & 1) == 1
    high_bit = (rank & 2) == 2
    first = [jnp.where(low_bit, blocks[i ^ 1], blocks[i]) for i in range(4)]
    return [jnp.where(high_bit, first[i ^ 2], first[i]) for i in range(4)]


def gather_chan(value):
    across = chan_swap(value, 2)
    beside = chan_swap(jnp.stack([value, across]), 1)
    return [value, beside[0], across, beside[1]]


def exchange(blocks, rank):
    got = [pick(blocks, rank)]
    for step in (1, 2, 3):
        got.append(chan_swap(pick(blocks, rank ^ step), step))
    return reorder(got, rank)


def silu_grad(pre_act):
    sigmoid = jax.nn.sigmoid(pre_act)
    return sigmoid * (1.0 + pre_act * (1.0 - sigmoid))


def matmul(first_op, second_op):
    return jnp.dot(first_op, second_op, preferred_element_type=F32)


def inner(first_op, second_op):
    return lax.dot_general(
        first_op, second_op, (((0,), (0,)), ((), ())), preferred_element_type=F32
    )


def outer(first_op, second_op):
    return lax.dot_general(
        first_op, second_op, (((1,), (1,)), ((), ())), preferred_element_type=F32
    )


def block_weights(basis_ref, block, diagonal):
    basis = basis_ref[block].astype(F32)
    count, width = basis.shape
    spread = jnp.broadcast_to(basis[:, None, :], (count, BLOCK, width))
    spread = spread.reshape(count * BLOCK, width)
    return jnp.where(diagonal, spread, 0.0).astype(BF16)


def diagonal_mask(rows, width):
    row = lax.broadcasted_iota(jnp.int32, (rows, width), 0) % BLOCK
    col = lax.broadcasted_iota(jnp.int32, (rows, width), 1) % BLOCK
    return row == col


def lane_groups(value, width):
    group = lax.broadcasted_iota(jnp.int32, value.shape, 1) // width
    zero = jnp.zeros_like(value)
    masked = [jnp.where(group == fold, value, zero) for fold in range(LANES // width)]
    return jnp.concatenate(masked, axis=0)


def gather_body(
    index_ref, packed_ref, basis_ref, bilinear_ref, agg_ref, sum_ref, table, rows_a, rows_b, *, folds
):
    pieces, piece_rows, _ = packed_ref.shape
    groups, edges, _ = sum_ref.shape
    basis_count = groups * folds
    width = LANES // folds
    slots = basis_ref.shape[2] // BLOCK
    step = min(piece_rows, 128)
    per_piece = piece_rows // step
    lane = lax.broadcasted_iota(jnp.int32, (step, LANES), 1) // width

    def unpack(turn, _):
        piece = turn // per_piece
        start = pl.multiple_of((turn % per_piece) * step, step)
        values = packed_ref[piece, pl.ds(start, step), :].astype(F32)
        turned = [values] + [
            pltpu.roll(values, shift * width, 1) for shift in range(1, folds)
        ]
        for fold in range(folds):
            place = pl.multiple_of((piece * folds + fold) * piece_rows + start, step)
            spread = turned[(0 - fold) % folds]
            for group in range(1, folds):
                spread = jnp.where(lane == group, turned[(group - fold) % folds], spread)
            table[pl.ds(place, step), :] = spread
        return 0

    lax.fori_loop(0, pieces * per_piece, unpack, 0)
    diagonal = diagonal_mask(basis_count * BLOCK, slots * BLOCK)

    def fetch(block, rows):
        base = block * BLOCK
        for slot in range(slots):
            for within in range(BLOCK):
                place = index_ref[slot * edges + base + within]
                at = slot * BLOCK + within
                rows[pl.ds(at, 1), :] = table[pl.ds(place, 1), :]

    def combine(block, rows):
        weights = block_weights(basis_ref, block, diagonal)
        each = groups * BLOCK
        joined = jnp.concatenate(
            [weights[fold * each : (fold + 1) * each] for fold in range(folds)], axis=1
        )
        got = matmul(joined, lane_groups(rows[...].astype(BF16), width)).astype(BF16)
        start = pl.multiple_of(block * BLOCK, BLOCK)
        sum_ref[:, pl.ds(start, BLOCK), :] = got.reshape(groups, BLOCK, LANES)

    blocks = edges // BLOCK
    fetch(0, rows_a)

    def turn(pair, _):
        fetch(2 * pair + 1, rows_b)
        combine(2 * pair, rows_a)
        fetch(jnp.minimum(2 * pair + 2, blocks - 1), rows_a)
        combine(2 * pair + 1, rows_b)
        return 0

    lax.fori_loop(0, blocks // 2, turn, 0)
    total = matmul(sum_ref[0], bilinear_ref[0])
    for group in range(1, groups):
        total = total + matmul(sum_ref[group], bilinear_ref[group])
    agg_ref[...] = total.astype(BF16)


def branch_forward(index, packed, basis, bilinear, name):
    groups, _, out_width = bilinear.shape
    edges = basis.shape[0] * BLOCK
    folds = basis.shape[1] // groups
    vmem = pl.BlockSpec(memory_space=pltpu.VMEM)
    return pl.pallas_call(
        functools.partial(gather_body, folds=folds),
        out_shape=(
            jax.ShapeDtypeStruct((edges, out_width), BF16),
            jax.ShapeDtypeStruct((groups, edges, LANES), BF16),
        ),
        in_specs=[pl.BlockSpec(memory_space=pltpu.SMEM), vmem, vmem, vmem],
        out_specs=(vmem, vmem),
        scratch_shapes=[
            pltpu.VMEM((packed.shape[0] * edges, LANES), F32),
            pltpu.VMEM((basis.shape[2], LANES), F32),
            pltpu.VMEM((basis.shape[2], LANES), F32),
        ],
        compiler_params=pltpu.CompilerParams(vmem_limit_bytes=56 << 20),
        cost_estimate=pl.CostEstimate(flops=20 * 10**9, transcendentals=0, bytes_accessed=10**7),
        name=name,
    )(index, packed, basis, bilinear)


TABLES = 4


def scatter_body(
    index_ref, basis_ref, grad_ref, bilinear_ref, packed_ref, part, rows_a, rows_b, *tables, folds
):
    pieces, piece_rows, _ = packed_ref.shape
    groups, edges, _ = part.shape
    basis_count = groups * folds
    width = LANES // folds
    slots = basis_ref.shape[2] // BLOCK
    chunk = 256
    table_rows = tables[0].shape[0]

    def clear(turn, _):
        start = pl.multiple_of(turn * chunk, chunk)
        for table in tables:
            table[pl.ds(start, chunk), :] = jnp.zeros((chunk, LANES), F32)
        return 0

    lax.fori_loop(0, table_rows // chunk, clear, 0)
    for group in range(groups):
        part[group] = outer(grad_ref[...], bilinear_ref[group]).astype(BF16)
    diagonal = diagonal_mask(basis_count * BLOCK, slots * BLOCK)

    def spread(block, rows):
        weights = block_weights(basis_ref, block, diagonal)
        start = pl.multiple_of(block * BLOCK, BLOCK)
        values = part[:, pl.ds(start, BLOCK), :].reshape(groups * BLOCK, LANES)
        rows[...] = inner(weights, lane_groups(values, width))

    def store(block, rows):
        base = block * BLOCK
        for slot in range(slots):
            for within in range(BLOCK):
                place = index_ref[slot * edges + base + within]
                at = slot * BLOCK + within
                table = tables[at % len(tables)]
                table[pl.ds(place, 1), :] += rows[pl.ds(at, 1), :]

    blocks = edges // BLOCK
    spread(0, rows_a)

    def turn(pair, _):
        spread(2 * pair + 1, rows_b)
        store(2 * pair, rows_a)
        spread(jnp.minimum(2 * pair + 2, blocks - 1), rows_a)
        store(2 * pair + 1, rows_b)
        return 0

    lax.fori_loop(0, blocks // 2, turn, 0)
    step = min(piece_rows, 128)
    per_piece = piece_rows // step
    lane = lax.broadcasted_iota(jnp.int32, (step, LANES), 1) // width

    def pack(turn, _):
        piece = turn // per_piece
        start = pl.multiple_of((turn % per_piece) * step, step)
        joined = jnp.zeros((step, LANES), F32)
        for fold in range(folds):
            place = pl.multiple_of((piece * folds + fold) * piece_rows + start, step)
            total = tables[0][pl.ds(place, step), :]
            for table in tables[1:]:
                total = total + table[pl.ds(place, step), :]
            shift = LANES // 2
            while shift >= width:
                total = total + pltpu.roll(total, shift, 1)
                shift //= 2
            joined = jnp.where(lane == fold, total, joined)
        packed_ref[piece, pl.ds(start, step), :] = joined.astype(BF16)
        return 0

    lax.fori_loop(0, pieces * per_piece, pack, 0)


def branch_backward(index, basis, grad, bilinear, pieces, name):
    edges = grad.shape[0]
    groups = bilinear.shape[0]
    folds = basis.shape[1] // groups
    vmem = pl.BlockSpec(memory_space=pltpu.VMEM)
    return pl.pallas_call(
        functools.partial(scatter_body, folds=folds),
        out_shape=jax.ShapeDtypeStruct((pieces, edges // folds, LANES), BF16),
        in_specs=[pl.BlockSpec(memory_space=pltpu.SMEM), vmem, vmem, vmem],
        out_specs=vmem,
        scratch_shapes=[
            pltpu.VMEM((groups, edges, LANES), BF16),
            pltpu.VMEM((basis.shape[2], LANES), F32),
            pltpu.VMEM((basis.shape[2], LANES), F32),
        ]
        + [pltpu.VMEM((pieces * edges, LANES), F32)] * TABLES,
        compiler_params=pltpu.CompilerParams(vmem_limit_bytes=58 << 20),
        cost_estimate=pl.CostEstimate(flops=20 * 10**9, transcendentals=0, bytes_accessed=10**7),
        name=name,
    )(index, basis, grad, bilinear)


def fold_lanes(rows):
    count, width = rows.shape
    folds = LANES // width
    each = count // folds
    return jnp.concatenate([rows[i * each : (i + 1) * each] for i in range(folds)], axis=1)


def unfold_lanes(packed, width):
    folds = LANES // width
    return jnp.concatenate([packed[:, i * width : (i + 1) * width] for i in range(folds)], axis=0)


def columns(array):
    return jnp.concatenate(
        [array[:, i : i + LANES] for i in range(0, array.shape[1], LANES)], axis=0
    )


def uncolumns(rows, width):
    each = rows.shape[0] * LANES // width
    return jnp.concatenate(
        [rows[i * each : (i + 1) * each] for i in range(width // LANES)], axis=1
    )


def slot_blocks(basis_vals, keep_mask):
    count, slots, edges = basis_vals.shape
    weighted = basis_vals * keep_mask.astype(BF16)[None]
    split = weighted.reshape(count, slots, edges // BLOCK, BLOCK)
    return jnp.transpose(split, (2, 0, 1, 3)).reshape(edges // BLOCK, count, slots * BLOCK)


def edge_reduce(rows):
    count = lax.axis_size("edge")
    rank = lax.axis_index("edge")
    steps = []
    size = 1
    while size < count:
        steps.append(size)
        size *= 2
    total = rows.shape[0]
    padded = -(-total // (16 * count)) * 16 * count
    value = jnp.pad(rows, ((0, padded - total), (0, 0)))
    for mask in steps:
        half = value.shape[0] // 2
        bit = (rank & mask) != 0
        keep = jnp.where(bit, value[half:], value[:half])
        send = jnp.where(bit, value[:half], value[half:])
        got = edge_swap(send, mask)
        value = (keep.astype(F32) + got.astype(F32)).astype(BF16)
    for mask in reversed(steps):
        bit = (rank & mask) != 0
        got = edge_swap(value, mask)
        value = jnp.concatenate(
            [jnp.where(bit, got, value), jnp.where(bit, value, got)], axis=0
        )
    return value[:total]


def edge_sum(value, kind):
    count = lax.axis_size("edge")
    size = 1
    while size < count:
        value = value + edge_swap(value.astype(kind), size).astype(F32)
        size *= 2
    return value


def per_device(
    edge_emb,
    atom_emb,
    radial,
    circular,
    spherical,
    atom_tags,
    edge_source,
    edge_target,
    trip_source,
    trip_mask,
    quad_source,
    quad_mask,
    triplet_down_weight,
    trip_radial,
    triplet_bilinear_weight,
    trip_up,
    quad_down,
    quad_radial,
    quad_bilinear,
    quad_up,
    source_proj,
    target_proj,
    resid_first,
    resid_second,
    edge_to_atom,
    atom_update,
    output_first,
    output_second,
    tag_table,
    grad_edges,
    grad_atoms,
    grad_energy,
):
    edges_here = edge_emb.shape[0]
    atoms_here = atom_emb.shape[0]
    parts = lax.axis_size("chan")
    edge_parts = lax.axis_size("edge")
    rank = lax.axis_index("chan")
    edge_rank = lax.axis_index("edge")
    edges = edges_here // parts
    cols = edge_emb.shape[1]
    start = rank * edges

    def own(array, axis):
        return lax.dynamic_slice_in_dim(array, start, edges, axis)

    own_edges = jnp.concatenate(exchange(edge_emb.reshape(parts, edges, cols), rank), axis=1)

    trip_cols = triplet_down_weight.shape[1]
    quad_cols = quad_down.shape[1]
    trip_out = triplet_bilinear_weight.shape[2]
    quad_out = quad_bilinear.shape[2]
    down_own = jnp.concatenate([triplet_down_weight, quad_down], axis=1)
    small = jnp.concatenate(
        [
            columns(
                jnp.concatenate(
                    [down_own, jnp.concatenate([trip_radial, quad_radial], axis=1)], axis=0
                ).T
            ),
            fold_lanes(triplet_bilinear_weight.reshape(-1, trip_out)),
            fold_lanes(quad_bilinear.reshape(-1, quad_out)),
        ],
        axis=0,
    )
    small = reorder(gather_direct(small), rank)
    channels = parts * cols
    long = channels + radial.shape[1]
    small_rows = (trip_cols + quad_cols) * long // LANES
    trip_bil_rows = triplet_bilinear_weight.size // LANES
    downs = jnp.stack([uncolumns(block[:small_rows], long) for block in small])
    trip_both = downs[:, :trip_cols].reshape(parts * trip_cols, -1).T
    quad_both = downs[:, trip_cols:].reshape(parts * quad_cols, -1).T
    both = jnp.concatenate([trip_both, quad_both], axis=1)
    down_full, radial_full = both[:channels], both[channels:]
    trip_width = trip_both.shape[1]
    quad_width = quad_both.shape[1]
    trip_folds = LANES // trip_width
    quad_folds = LANES // quad_width

    def group_rows(blocks, shape, folds):
        whole = jnp.concatenate(
            [unfold_lanes(block, shape[2]).reshape(shape) for block in blocks], axis=1
        )
        count, width, out = whole.shape
        split = whole.reshape(folds, count // folds, width, out)
        return jnp.transpose(split, (1, 0, 2, 3)).reshape(count // folds, folds * width, out)

    trip_bil = group_rows(
        [block[small_rows : small_rows + trip_bil_rows] for block in small],
        triplet_bilinear_weight.shape,
        trip_folds,
    )
    quad_bil = group_rows(
        [block[small_rows + trip_bil_rows :] for block in small],
        quad_bilinear.shape,
        quad_folds,
    )

    own_radial = own(radial, 0)
    down_pre = matmul(own_edges, down_full)
    radial_pre = matmul(own_radial, radial_full)
    dense = (jax.nn.silu(down_pre) * radial_pre).astype(BF16)
    trip_piece = fold_lanes(dense[:, :trip_width])
    quad_piece = fold_lanes(dense[:, trip_width:])
    trip_rows = trip_piece.shape[0]
    wire = jnp.concatenate([trip_piece, quad_piece], axis=0)
    before = edge_shift(wire, 1)
    after_wire = edge_shift(wire, -1)
    own_pieces = gather_chan(wire)
    sides = jnp.stack([before, after_wire])
    across = chan_swap(sides, 2)
    beside = chan_swap(jnp.stack([sides, across]), 1)
    side_pieces = [sides, beside[0], across, beside[1]]
    all_pieces = jnp.stack(
        [side[0] for side in side_pieces] + own_pieces + [side[1] for side in side_pieces]
    )
    trip_packed = all_pieces[:, :trip_rows]
    quad_packed = all_pieces[:, trip_rows:]

    large = jnp.concatenate(
        [
            trip_up,
            quad_up,
            source_proj,
            target_proj,
            resid_first,
            columns(resid_second),
            columns(edge_to_atom),
        ],
        axis=0,
    )
    large_rel = gather_chan(after(large, across))
    large = reorder(large_rel, rank)
    grad_blocks = after(grad_edges, large_rel[2]).reshape(parts, edges, cols)
    grad_two = jnp.concatenate(exchange(grad_blocks, rank), axis=1)
    sizes = [
        trip_up.shape[0],
        quad_up.shape[0],
        source_proj.shape[0],
        target_proj.shape[0],
        resid_first.shape[0],
        resid_second.size // LANES,
        edge_to_atom.size // LANES,
    ]

    def offsets_of(sizes):
        return [sum(sizes[:i]) for i in range(len(sizes) + 1)]

    offsets = offsets_of(sizes)

    def piece(item):
        return [block[offsets[item] : offsets[item + 1]] for block in large]

    trip_up_full = jnp.concatenate(piece(0), axis=1)
    quad_up_full = jnp.concatenate(piece(1), axis=1)
    proj_full = jnp.concatenate(
        [jnp.concatenate(piece(2), axis=1), jnp.concatenate(piece(3), axis=1)], axis=0
    )
    first_full = jnp.concatenate(piece(4), axis=1)
    second_full = jnp.concatenate(
        [uncolumns(block, resid_second.shape[1]) for block in piece(5)], axis=0
    )
    to_atom_full = jnp.concatenate(
        [uncolumns(block, edge_to_atom.shape[1]) for block in piece(6)], axis=0
    )

    tag_onehot = (atom_tags[:, None] == jnp.arange(TAGS)[None, :]).astype(F32)
    atom_full = atom_emb.astype(F32) + jnp.dot(
        tag_onehot, tag_table.astype(F32), precision=HIGHEST
    )
    atom_low = atom_full.astype(BF16)
    atom_wide = jnp.concatenate(
        [edge_shift(atom_low, 1), atom_low, edge_shift(atom_low, -1)], axis=0
    )
    atom_total = edge_parts * atoms_here
    source_local = (own(edge_source, 0) - (edge_rank - 1) * atoms_here) % atom_total
    target_local = own(edge_target, 0) - edge_rank * atoms_here
    source_hot = (source_local[:, None] == jnp.arange(3 * atoms_here)[None, :]).astype(BF16)
    target_hot = (target_local[:, None] == jnp.arange(atoms_here)[None, :]).astype(BF16)
    ends = jnp.concatenate(
        [
            matmul(source_hot, atom_wide).astype(BF16),
            matmul(target_hot, atom_low).astype(BF16),
        ],
        axis=1,
    )

    def places(source):
        local = own(source, 1)
        within = local % edges_here
        owner = (within // edges) ^ rank
        return ((local // edges_here) * edges_here + owner * edges + within % edges).reshape(-1)

    trip_index = places(trip_source)
    quad_index = places(quad_source)
    circular, spherical = lax.optimization_barrier((circular, spherical, wire))[:2]
    trip_basis = slot_blocks(own(circular, 2), own(trip_mask, 1))
    quad_basis = slot_blocks(own(spherical, 2), own(quad_mask, 1))
    trip_agg, trip_sum = branch_forward(
        trip_index, trip_packed, trip_basis, trip_bil, "trip_gather"
    )
    quad_agg, quad_sum = branch_forward(
        quad_index, quad_packed, quad_basis, quad_bil, "quad_gather"
    )

    message = matmul(ends, proj_full)
    trip_out_pre = matmul(trip_agg, trip_up_full)
    quad_out_pre = matmul(quad_agg, quad_up_full)
    hidden_one = (
        own_edges.astype(F32)
        + jax.nn.silu(trip_out_pre)
        + jax.nn.silu(quad_out_pre)
        + jax.nn.silu(message)
    )
    hidden_low = hidden_one.astype(BF16)
    first_pre = matmul(hidden_low, first_full)
    first_low = jax.nn.silu(first_pre).astype(BF16)
    second_pre = matmul(first_low, second_full)
    edges_low = (hidden_one + jax.nn.silu(second_pre)).astype(BF16)
    edge_sums = inner(target_hot, edges_low)
    sums_high = edge_sums.astype(BF16)
    sums_rest = (edge_sums - sums_high.astype(F32)).astype(BF16)
    atom_sum = matmul(sums_high, to_atom_full) + matmul(sums_rest, to_atom_full)
    atom_sum = atom_sum + chan_swap(atom_sum, 1)
    atom_sum = atom_sum + chan_swap(atom_sum, 2)

    atom_sum_low = atom_sum.astype(BF16)
    update_pre = matmul(atom_sum_low, atom_update)
    atoms_new = atom_full + jax.nn.silu(update_pre)
    atoms_low = atoms_new.astype(BF16)
    output_pre = matmul(atoms_low, output_first)
    output_low = jax.nn.silu(output_pre).astype(BF16)
    energy = matmul(output_low, output_second)
    output_second_grad = jnp.dot(grad_energy, output_low.astype(F32), precision=HIGHEST)
    output_grad = (
        grad_energy[:, None] * output_second.astype(F32)[None, :] * silu_grad(output_pre)
    ).astype(BF16)
    output_first_grad = inner(atoms_low, output_grad)
    atoms_new_grad = grad_atoms.astype(F32) + outer(output_grad, output_first)
    update_grad = (atoms_new_grad * silu_grad(update_pre)).astype(BF16)
    atom_update_grad = inner(atom_sum_low, update_grad)
    atom_sum_grad = outer(update_grad, atom_update).astype(BF16)

    edge_part_grad = matmul(target_hot, atom_sum_grad).astype(BF16)
    edge_to_atom_grad = inner(edges_low, edge_part_grad)
    two_grad = grad_two.astype(F32) + outer(edge_part_grad, to_atom_full)
    second_grad = (two_grad * silu_grad(second_pre)).astype(BF16)
    resid_second_grad = inner(first_low, second_grad)
    first_grad = (outer(second_grad, second_full) * silu_grad(first_pre)).astype(BF16)
    resid_first_grad = inner(hidden_low, first_grad)
    one_grad = two_grad + outer(first_grad, first_full)
    trip_out_grad = (one_grad * silu_grad(trip_out_pre)).astype(BF16)
    quad_out_grad = (one_grad * silu_grad(quad_out_pre)).astype(BF16)
    message_grad = (one_grad * silu_grad(message)).astype(BF16)
    trip_up_grad = inner(trip_agg, trip_out_grad)
    quad_up_grad = inner(quad_agg, quad_out_grad)
    trip_agg_grad = outer(trip_out_grad, trip_up_full).astype(BF16)
    quad_agg_grad = outer(quad_out_grad, quad_up_full).astype(BF16)
    proj_grad = inner(ends, message_grad)
    width = atom_low.shape[1]
    source_sums = inner(source_hot, message_grad).astype(BF16)
    target_sums = inner(target_hot, message_grad).astype(BF16)
    source_back = outer(source_sums, proj_full[:width])
    target_back = outer(target_sums, proj_full[width:])
    wide_atoms = source_back.reshape(3, atoms_here, width)
    wide_atoms = wide_atoms.at[1].add(target_back)

    def split(array, axis):
        return jnp.split(array, parts, axis=axis)

    def share(members):
        packed = [
            jnp.concatenate([member[i] for member in members], axis=0).astype(BF16)
            for i in range(parts)
        ]
        packed = reorder(packed, rank)
        got = chan_swap(jnp.stack([packed[1], packed[3]]), 1).astype(F32)
        mine = packed[0].astype(F32) + got[0]
        return mine, (packed[2].astype(F32) + got[1]).astype(BF16)

    mine, other = share(
        [
            split(trip_up_grad, 1),
            split(quad_up_grad, 1),
            split(proj_grad[:width], 1),
            split(proj_grad[width:], 1),
            split(resid_first_grad, 1),
            [columns(block) for block in split(resid_second_grad, 0)],
            [columns(block) for block in split(edge_to_atom_grad, 0)],
        ]
    )
    other_got = chan_swap(other, 2)
    atom_rows = jnp.concatenate(
        [columns(atom_update_grad), columns(output_first_grad)], axis=0
    ).astype(BF16)

    wide_low = wide_atoms.astype(BF16)
    wide_atoms = wide_atoms + chan_swap(wide_low, 1).astype(F32)
    wide_low = wide_atoms.astype(BF16)
    wide_atoms = wide_atoms + chan_swap(wide_low, 2).astype(F32)
    atom_grad = (
        atoms_new_grad
        + wide_atoms[1]
        + edge_shift(wide_atoms[0].astype(BF16), -1).astype(F32)
        + edge_shift(wide_atoms[2].astype(BF16), 1).astype(F32)
    )
    tag_table_grad = jnp.dot(tag_onehot.T, atom_grad, precision=HIGHEST)

    pieces = 3 * parts

    def fold_table(table):
        table = table.reshape(3, parts, -1, LANES)
        got = chan_swap(jnp.stack([table[:, 1], table[:, 3]]), 1).astype(F32)
        mine = table[:, 0].astype(F32) + got[0]
        return mine, (table[:, 2].astype(F32) + got[1]).astype(BF16)

    def return_table(mine):
        to_before = edge_shift(mine[0].astype(BF16), -1)
        to_after = edge_shift(mine[2].astype(BF16), 1)
        return mine[1] + to_before.astype(F32) + to_after.astype(F32)

    trip_table = branch_backward(
        after(trip_index, other), trip_basis, trip_agg_grad, trip_bil, pieces, "trip_scatter"
    )
    trip_mine, trip_other = fold_table(trip_table)
    trip_got = chan_swap(trip_other, 2)
    quad_table = branch_backward(
        after(quad_index, trip_other), quad_basis, quad_agg_grad, quad_bil, pieces, "quad_scatter"
    )
    trip_grad = return_table(trip_mine + trip_got.astype(F32))
    quad_mine, quad_other = fold_table(quad_table)
    quad_grad = return_table(quad_mine + chan_swap(quad_other, 2).astype(F32))
    branch_grad = jnp.concatenate(
        [unfold_lanes(trip_grad, trip_width), unfold_lanes(quad_grad, quad_width)], axis=1
    )
    down_grad = (branch_grad * radial_pre * silu_grad(down_pre)).astype(BF16)
    radial_grad = (branch_grad * jax.nn.silu(down_pre)).astype(BF16)
    down_weight_grad = inner(own_edges, down_grad)
    radial_weight_grad = inner(own_radial, radial_grad)

    def give_back(array):
        blocks = jnp.stack([array[:, i * cols : (i + 1) * cols] for i in range(parts)])
        return jnp.concatenate(exchange(blocks, rank), axis=0)

    edges_out = give_back(edges_low)
    one_out = give_back(one_grad.astype(BF16)).astype(F32)
    down_wire = jnp.concatenate(
        [fold_lanes(down_grad[:, :trip_width]), fold_lanes(down_grad[:, trip_width:])], axis=0
    )
    down_all = reorder(gather_chan(down_wire), rank)
    down_all = jnp.concatenate(
        [
            jnp.concatenate(
                [
                    unfold_lanes(block[:trip_rows], trip_width),
                    unfold_lanes(block[trip_rows:], quad_width),
                ],
                axis=1,
            )
            for block in down_all
        ],
        axis=0,
    )
    down_rows = lax.dynamic_slice_in_dim(down_full, rank * cols, cols, 0)
    edge_grad = one_out + outer(down_all, down_rows)

    mine = (mine + other_got.astype(F32)).astype(BF16)
    early = mine.shape[0]
    summed = edge_reduce(jnp.concatenate([mine, atom_rows], axis=0)).astype(F32)

    def ungroup(array, folds):
        groups, rows, out = array.shape
        array = array.reshape(groups, folds, rows // folds, out)
        return jnp.transpose(array, (1, 0, 2, 3)).reshape(groups * folds, rows // folds, out)

    trip_bilinear_grad = ungroup(
        jnp.einsum("gej,eo->gjo", trip_sum, trip_agg_grad, preferred_element_type=F32), trip_folds
    )
    quad_bilinear_grad = ungroup(
        jnp.einsum("gej,eo->gjo", quad_sum, quad_agg_grad, preferred_element_type=F32), quad_folds
    )
    small_grad = jnp.concatenate([down_weight_grad, radial_weight_grad], axis=0)
    late_mine, late_other = share(
        [
            [
                columns(jnp.concatenate([trip_block, quad_block], axis=1).T)
                for trip_block, quad_block in zip(
                    split(small_grad[:, :trip_width], 1), split(small_grad[:, trip_width:], 1)
                )
            ],
            [fold_lanes(block.reshape(-1, trip_out)) for block in split(trip_bilinear_grad, 1)],
            [fold_lanes(block.reshape(-1, quad_out)) for block in split(quad_bilinear_grad, 1)],
        ]
    )
    late = late_mine + chan_swap(late_other, 2).astype(F32)
    late = edge_sum(late, BF16)
    tiny = edge_sum(jnp.concatenate([output_second_grad[None], tag_table_grad], axis=0), F32)
    parts_out = [summed[offsets[i] : offsets[i + 1]] for i in range(len(sizes))]
    small_out = uncolumns(late[:small_rows], long).T
    trip_bil_out = late[small_rows : small_rows + trip_bil_rows]
    quad_bil_out = late[small_rows + trip_bil_rows :]
    atom_out = summed[early:]
    half = atom_out.shape[0] // 2
    return (
        edges_out,
        atoms_low,
        energy,
        edge_grad,
        atom_grad,
        small_out[:channels, :trip_cols],
        small_out[channels:, :trip_cols],
        unfold_lanes(trip_bil_out, trip_out).reshape(triplet_bilinear_weight.shape),
        parts_out[0],
        small_out[:channels, trip_cols:],
        small_out[channels:, trip_cols:],
        unfold_lanes(quad_bil_out, quad_out).reshape(quad_bilinear.shape),
        parts_out[1],
        parts_out[2],
        parts_out[3],
        parts_out[4],
        uncolumns(parts_out[5], resid_second.shape[1]),
        uncolumns(parts_out[6], edge_to_atom.shape[1]),
        uncolumns(atom_out[:half], atom_update.shape[1]),
        uncolumns(atom_out[half:], output_first.shape[1]),
        tiny[0],
        tiny[1:],
    )


def solution(mesh):
    return jax.shard_map(
        per_device,
        mesh=mesh,
        in_specs=(
            P("edge", "chan"),
            P("edge", None),
            P("edge", None),
            P(None, None, "edge"),
            P(None, None, "edge"),
            P("edge"),
            P("edge"),
            P("edge"),
            P(None, "edge"),
            P(None, "edge"),
            P(None, "edge"),
            P(None, "edge"),
            P(None, "chan"),
            P(None, "chan"),
            P(None, "chan", None),
            P(None, "chan"),
            P(None, "chan"),
            P(None, "chan"),
            P(None, "chan", None),
            P(None, "chan"),
            P(None, "chan"),
            P(None, "chan"),
            P(None, "chan"),
            P("chan", None),
            P("chan", None),
            P(),
            P(),
            P(),
            P(),
            P("edge", "chan"),
            P("edge", None),
            P("edge"),
        ),
        out_specs=(
            P("edge", "chan"),
            P("edge", None),
            P("edge"),
            P("edge", "chan"),
            P("edge", None),
            P(None, "chan"),
            P(None, "chan"),
            P(None, "chan", None),
            P(None, "chan"),
            P(None, "chan"),
            P(None, "chan"),
            P(None, "chan", None),
            P(None, "chan"),
            P(None, "chan"),
            P(None, "chan"),
            P(None, "chan"),
            P("chan", None),
            P("chan", None),
            P(),
            P(),
            P(),
            P(),
        ),
        check_vma=False,
    )
```

```python
import functools

import jax
import jax.numpy as jnp
from jax import lax
from jax.experimental import pallas as pl
from jax.experimental.pallas import tpu as pltpu
from jax.sharding import PartitionSpec as P

TAGS = 3
LANES = 128
BLOCK = 16
BF16 = jnp.bfloat16
F32 = jnp.float32
HIGHEST = lax.Precision.HIGHEST


def chan_swap(value, mask):
    count = lax.axis_size("chan")
    return lax.ppermute(value, "chan", [(i, i ^ mask) for i in range(count)])


def edge_swap(value, mask):
    count = lax.axis_size("edge")
    return lax.ppermute(value, "edge", [(i, i ^ mask) for i in range(count)])


def edge_shift(value, step):
    count = lax.axis_size("edge")
    return lax.ppermute(value, "edge", [(i, (i + step) % count) for i in range(count)])


def after(value, *others):
    return lax.optimization_barrier((value,) + others)[0]


def gate(values, *others):
    return list(lax.optimization_barrier(tuple(values) + others)[: len(values)])


def gather_direct(value):
    return [value] + [chan_swap(value, step) for step in (1, 2, 3)]


def pick(blocks, place):
    return lax.dynamic_index_in_dim(blocks, place, 0, keepdims=False)


def reorder(blocks, rank):
    low_bit = (rank & 1) == 1
    high_bit = (rank & 2) == 2
    first = [jnp.where(low_bit, blocks[i ^ 1], blocks[i]) for i in range(4)]
    return [jnp.where(high_bit, first[i ^ 2], first[i]) for i in range(4)]


def gather_chan(value):
    across = chan_swap(value, 2)
    beside = chan_swap(jnp.stack([value, across]), 1)
    return [value, beside[0], across, beside[1]]


def exchange(blocks, rank):
    got = [pick(blocks, rank)]
    for step in (1, 2, 3):
        got.append(chan_swap(pick(blocks, rank ^ step), step))
    return reorder(got, rank)


def silu_grad(pre_act):
    sigmoid = jax.nn.sigmoid(pre_act)
    return sigmoid * (1.0 + pre_act * (1.0 - sigmoid))


def matmul(first_op, second_op):
    return jnp.dot(first_op, second_op, preferred_element_type=F32)


def inner(first_op, second_op):
    return lax.dot_general(
        first_op, second_op, (((0,), (0,)), ((), ())), preferred_element_type=F32
    )


def outer(first_op, second_op):
    return lax.dot_general(
        first_op, second_op, (((1,), (1,)), ((), ())), preferred_element_type=F32
    )


def block_weights(basis_ref, block, diagonal):
    basis = basis_ref[block].astype(F32)
    count, width = basis.shape
    spread = jnp.broadcast_to(basis[:, None, :], (count, BLOCK, width))
    spread = spread.reshape(count * BLOCK, width)
    return jnp.where(diagonal, spread, 0.0).astype(BF16)


def diagonal_mask(rows, width):
    row = lax.broadcasted_iota(jnp.int32, (rows, width), 0) % BLOCK
    col = lax.broadcasted_iota(jnp.int32, (rows, width), 1) % BLOCK
    return row == col


def lane_groups(value, width):
    group = lax.broadcasted_iota(jnp.int32, value.shape, 1) // width
    zero = jnp.zeros_like(value)
    masked = [jnp.where(group == fold, value, zero) for fold in range(LANES // width)]
    return jnp.concatenate(masked, axis=0)


def gather_body(index_ref, basis_ref, bilinear_ref, *refs, folds, first_row):
    packed_refs = refs[:-5]
    agg_ref, sum_ref, table, rows_a, rows_b = refs[-5:]
    groups, edges, _ = sum_ref.shape
    basis_count = groups * folds
    width = LANES // folds
    piece_rows = edges // folds
    slots = basis_ref.shape[2] // BLOCK
    step = min(piece_rows, 128)
    lane = lax.broadcasted_iota(jnp.int32, (step, LANES), 1) // width

    for piece, packed_ref in enumerate(packed_refs):

        def unpack(turn, _, piece=piece, packed_ref=packed_ref):
            start = pl.multiple_of(turn * step, step)
            values = packed_ref[pl.ds(first_row + start, step), :].astype(F32)
            turned = [values] + [
                pltpu.roll(values, shift * width, 1) for shift in range(1, folds)
            ]
            for fold in range(folds):
                place = pl.multiple_of((piece * folds + fold) * piece_rows + start, step)
                spread = turned[(0 - fold) % folds]
                for group in range(1, folds):
                    spread = jnp.where(lane == group, turned[(group - fold) % folds], spread)
                table[pl.ds(place, step), :] = spread
            return 0

        lax.fori_loop(0, piece_rows // step, unpack, 0)
    diagonal = diagonal_mask(basis_count * BLOCK, slots * BLOCK)

    def fetch(block, rows):
        base = block * BLOCK
        for slot in range(slots):
            for within in range(BLOCK):
                place = index_ref[slot * edges + base + within]
                at = slot * BLOCK + within
                rows[pl.ds(at, 1), :] = table[pl.ds(place, 1), :]

    def combine(block, rows):
        weights = block_weights(basis_ref, block, diagonal)
        each = groups * BLOCK
        joined = jnp.concatenate(
            [weights[fold * each : (fold + 1) * each] for fold in range(folds)], axis=1
        )
        got = matmul(joined, lane_groups(rows[...].astype(BF16), width)).astype(BF16)
        start = pl.multiple_of(block * BLOCK, BLOCK)
        sum_ref[:, pl.ds(start, BLOCK), :] = got.reshape(groups, BLOCK, LANES)

    blocks = edges // BLOCK
    fetch(0, rows_a)

    def turn(pair, _):
        fetch(2 * pair + 1, rows_b)
        combine(2 * pair, rows_a)
        fetch(jnp.minimum(2 * pair + 2, blocks - 1), rows_a)
        combine(2 * pair + 1, rows_b)
        return 0

    lax.fori_loop(0, blocks // 2, turn, 0)
    total = matmul(sum_ref[0], bilinear_ref[0])
    for group in range(1, groups):
        total = total + matmul(sum_ref[group], bilinear_ref[group])
    agg_ref[...] = total.astype(BF16)


def branch_forward(index, packed, first_row, basis, bilinear, name):
    groups, _, out_width = bilinear.shape
    edges = basis.shape[0] * BLOCK
    folds = basis.shape[1] // groups
    vmem = pl.BlockSpec(memory_space=pltpu.VMEM)
    return pl.pallas_call(
        functools.partial(gather_body, folds=folds, first_row=first_row),
        out_shape=(
            jax.ShapeDtypeStruct((edges, out_width), BF16),
            jax.ShapeDtypeStruct((groups, edges, LANES), BF16),
        ),
        in_specs=[pl.BlockSpec(memory_space=pltpu.SMEM)] + [vmem] * (2 + len(packed)),
        out_specs=(vmem, vmem),
        scratch_shapes=[
            pltpu.VMEM((len(packed) * edges, LANES), F32),
            pltpu.VMEM((basis.shape[2], LANES), F32),
            pltpu.VMEM((basis.shape[2], LANES), F32),
        ],
        compiler_params=pltpu.CompilerParams(vmem_limit_bytes=56 << 20),
        cost_estimate=pl.CostEstimate(flops=20 * 10**9, transcendentals=0, bytes_accessed=10**7),
        name=name,
    )(index, basis, bilinear, *packed)


def basis_body(rank_ref, trip_vals, trip_keep, quad_vals, quad_keep, trip_ref, quad_ref, trip_rows, quad_rows):
    del rank_ref
    tile_slots = LANES // BLOCK

    def build(vals_ref, keep_ref, out_ref, rows):
        count, slots, _ = vals_ref.shape
        vals = vals_ref[...].astype(F32) * keep_ref[...].astype(F32)[None]
        rows[...] = vals.reshape(count * slots, LANES)
        group = lax.broadcasted_iota(jnp.int32, (count, LANES), 1) // BLOCK
        for tile in range(slots // tile_slots):
            by_slot = [
                rows[pl.ds(tile * tile_slots + slot, count, stride=slots), :]
                for slot in range(tile_slots)
            ]
            for block in range(tile_slots):
                joined = None
                for slot, value in enumerate(by_slot):
                    shift = (slot - block) * BLOCK % LANES
                    turned = pltpu.roll(value, shift, 1) if shift else value
                    joined = turned if joined is None else jnp.where(group == slot, turned, joined)
                out_ref[block, :, tile * LANES : (tile + 1) * LANES] = joined.astype(BF16)

    build(trip_vals, trip_keep, trip_ref, trip_rows)
    build(quad_vals, quad_keep, quad_ref, quad_rows)


def slot_basis(rank, circular, trip_mask, spherical, quad_mask, edges):
    steps = edges // LANES
    blocks = LANES // BLOCK

    def source(array):
        shape = array.shape[:-1] + (LANES,)
        lead = (0,) * (len(shape) - 1)
        return pl.BlockSpec(shape, lambda step, rank_ref: lead + (rank_ref[0] * steps + step,))

    def target(count, slots):
        return pl.BlockSpec((blocks, count, slots * BLOCK), lambda step, rank_ref: (step, 0, 0))

    def shape_of(array):
        count, slots, _ = array.shape
        return jax.ShapeDtypeStruct((edges // BLOCK, count, slots * BLOCK), BF16)

    def rows_of(array):
        return pltpu.VMEM((array.shape[0] * array.shape[1], LANES), F32)

    return pl.pallas_call(
        basis_body,
        grid_spec=pltpu.PrefetchScalarGridSpec(
            num_scalar_prefetch=1,
            grid=(steps,),
            in_specs=[source(circular), source(trip_mask), source(spherical), source(quad_mask)],
            out_specs=[target(*circular.shape[:2]), target(*spherical.shape[:2])],
            scratch_shapes=[rows_of(circular), rows_of(spherical)],
        ),
        out_shape=(shape_of(circular), shape_of(spherical)),
        cost_estimate=pl.CostEstimate(flops=10 * 10**9, transcendentals=0, bytes_accessed=10**7),
        name="slot_basis",
    )(rank[None], circular, trip_mask, spherical, quad_mask)


TABLES = 4


def scatter_body(
    index_ref, basis_ref, grad_ref, bilinear_ref, *refs, folds, owners
):
    packed_refs = refs[:owners]
    part, rows_a, rows_b = refs[owners : owners + 3]
    tables = refs[owners + 3 :]
    sides, piece_rows, _ = packed_refs[0].shape
    groups, edges, _ = part.shape
    basis_count = groups * folds
    width = LANES // folds
    slots = basis_ref.shape[2] // BLOCK
    chunk = 256
    table_rows = tables[0].shape[0]

    def clear(turn, _):
        start = pl.multiple_of(turn * chunk, chunk)
        for table in tables:
            table[pl.ds(start, chunk), :] = jnp.zeros((chunk, LANES), F32)
        return 0

    lax.fori_loop(0, table_rows // chunk, clear, 0)
    for group in range(groups):
        part[group] = outer(grad_ref[...], bilinear_ref[group]).astype(BF16)
    diagonal = diagonal_mask(basis_count * BLOCK, slots * BLOCK)

    def spread(block, rows):
        weights = block_weights(basis_ref, block, diagonal)
        start = pl.multiple_of(block * BLOCK, BLOCK)
        values = part[:, pl.ds(start, BLOCK), :].reshape(groups * BLOCK, LANES)
        rows[...] = inner(weights, lane_groups(values, width))

    def store(block, rows):
        base = block * BLOCK
        for slot in range(slots):
            for within in range(BLOCK):
                place = index_ref[slot * edges + base + within]
                at = slot * BLOCK + within
                table = tables[at % len(tables)]
                table[pl.ds(place, 1), :] += rows[pl.ds(at, 1), :]

    blocks = edges // BLOCK
    spread(0, rows_a)

    def turn(pair, _):
        spread(2 * pair + 1, rows_b)
        store(2 * pair, rows_a)
        spread(jnp.minimum(2 * pair + 2, blocks - 1), rows_a)
        store(2 * pair + 1, rows_b)
        return 0

    lax.fori_loop(0, blocks // 2, turn, 0)
    step = min(piece_rows, 128)
    per_piece = piece_rows // step
    lane = lax.broadcasted_iota(jnp.int32, (step, LANES), 1) // width

    for owner, packed_ref in enumerate(packed_refs):

        def pack(turn, _, owner=owner, packed_ref=packed_ref):
            side = turn // per_piece
            piece = side * owners + owner
            start = pl.multiple_of((turn % per_piece) * step, step)
            joined = jnp.zeros((step, LANES), F32)
            for fold in range(folds):
                place = pl.multiple_of((piece * folds + fold) * piece_rows + start, step)
                total = tables[0][pl.ds(place, step), :]
                for table in tables[1:]:
                    total = total + table[pl.ds(place, step), :]
                shift = LANES // 2
                while shift >= width:
                    total = total + pltpu.roll(total, shift, 1)
                    shift //= 2
                joined = jnp.where(lane == fold, total, joined)
            packed_ref[side, pl.ds(start, step), :] = joined.astype(BF16)
            return 0

        lax.fori_loop(0, sides * per_piece, pack, 0)


def branch_backward(index, basis, grad, bilinear, sides, owners, name):
    edges = grad.shape[0]
    groups = bilinear.shape[0]
    folds = basis.shape[1] // groups
    vmem = pl.BlockSpec(memory_space=pltpu.VMEM)
    out = jax.ShapeDtypeStruct((sides, edges // folds, LANES), BF16)
    return pl.pallas_call(
        functools.partial(scatter_body, folds=folds, owners=owners),
        out_shape=(out,) * owners,
        in_specs=[pl.BlockSpec(memory_space=pltpu.SMEM), vmem, vmem, vmem],
        out_specs=(vmem,) * owners,
        scratch_shapes=[
            pltpu.VMEM((groups, edges, LANES), BF16),
            pltpu.VMEM((basis.shape[2], LANES), F32),
            pltpu.VMEM((basis.shape[2], LANES), F32),
        ]
        + [pltpu.VMEM((sides * owners * edges, LANES), F32)] * TABLES,
        compiler_params=pltpu.CompilerParams(vmem_limit_bytes=58 << 20),
        cost_estimate=pl.CostEstimate(flops=20 * 10**9, transcendentals=0, bytes_accessed=10**7),
        name=name,
    )(index, basis, grad, bilinear)


def fold_lanes(rows):
    count, width = rows.shape
    folds = LANES // width
    each = count // folds
    return jnp.concatenate([rows[i * each : (i + 1) * each] for i in range(folds)], axis=1)


def unfold_lanes(packed, width):
    folds = LANES // width
    return jnp.concatenate([packed[:, i * width : (i + 1) * width] for i in range(folds)], axis=0)


def columns(array):
    return jnp.concatenate(
        [array[:, i : i + LANES] for i in range(0, array.shape[1], LANES)], axis=0
    )


def uncolumns(rows, width):
    each = rows.shape[0] * LANES // width
    return jnp.concatenate(
        [rows[i * each : (i + 1) * each] for i in range(width // LANES)], axis=1
    )


def edge_fields():
    count = lax.axis_size("edge")
    fields = []
    size = 1
    while size < count:
        width = min(8, count // size)
        fields.append((size, width))
        size *= width
    return fields


def edge_scatter(value):
    rank = lax.axis_index("edge")
    for size, width in edge_fields():
        place = (rank // size) % width
        chunks = value.reshape(width, -1, value.shape[1])
        total = pick(chunks, place).astype(F32)
        for mask in range(1, width):
            total = total + edge_swap(pick(chunks, place ^ mask), mask * size).astype(F32)
        value = total.astype(BF16)
    return value


def edge_gather(value):
    rank = lax.axis_index("edge")
    for size, width in reversed(edge_fields()):
        mask = 1
        while mask < width:
            bit = (rank & (mask * size)) != 0
            got = edge_swap(value, mask * size)
            value = jnp.concatenate(
                [jnp.where(bit, got, value), jnp.where(bit, value, got)], axis=0
            )
            mask *= 2
    return value


def tree_sum(values):
    values = [value.astype(F32) for value in values]
    while len(values) > 1:
        values = [values[i] + values[i + 1] for i in range(0, len(values), 2)]
    return values[0]


def edge_total(value):
    for size, width in edge_fields():
        got = [value] + [edge_swap(value, mask * size) for mask in range(1, width)]
        value = tree_sum(got).astype(BF16)
    return value


def edge_sum(value):
    count = lax.axis_size("edge")
    size = 1
    while size < count:
        value = value + edge_swap(value, size)
        size *= 2
    return value


def per_device(
    edge_emb,
    atom_emb,
    radial,
    circular,
    spherical,
    atom_tags,
    edge_source,
    edge_target,
    trip_source,
    trip_mask,
    quad_source,
    quad_mask,
    triplet_down_weight,
    trip_radial,
    triplet_bilinear_weight,
    trip_up,
    quad_down,
    quad_radial,
    quad_bilinear,
    quad_up,
    source_proj,
    target_proj,
    resid_first,
    resid_second,
    edge_to_atom,
    atom_update,
    output_first,
    output_second,
    tag_table,
    grad_edges,
    grad_atoms,
    grad_energy,
):
    edges_here = edge_emb.shape[0]
    atoms_here = atom_emb.shape[0]
    parts = lax.axis_size("chan")
    edge_parts = lax.axis_size("edge")
    rank = lax.axis_index("chan")
    edge_rank = lax.axis_index("edge")
    edges = edges_here // parts
    cols = edge_emb.shape[1]
    start = rank * edges

    def own(array, axis):
        return lax.dynamic_slice_in_dim(array, start, edges, axis)

    edge_blocks = edge_emb.reshape(parts, edges, cols)
    own_edges = jnp.concatenate(exchange(edge_blocks, rank), axis=1)

    trip_cols = triplet_down_weight.shape[1]
    quad_cols = quad_down.shape[1]
    trip_out = triplet_bilinear_weight.shape[2]
    quad_out = quad_bilinear.shape[2]
    down_own = jnp.concatenate([triplet_down_weight, quad_down], axis=1)
    small = jnp.concatenate(
        [
            columns(
                jnp.concatenate(
                    [down_own, jnp.concatenate([trip_radial, quad_radial], axis=1)], axis=0
                ).T
            ),
            fold_lanes(triplet_bilinear_weight.reshape(-1, trip_out)),
            fold_lanes(quad_bilinear.reshape(-1, quad_out)),
        ],
        axis=0,
    )
    small = reorder(gather_direct(small), rank)
    channels = parts * cols
    long = channels + radial.shape[1]
    small_rows = (trip_cols + quad_cols) * long // LANES
    trip_bil_rows = triplet_bilinear_weight.size // LANES
    downs = jnp.stack([uncolumns(block[:small_rows], long) for block in small])
    trip_both = downs[:, :trip_cols].reshape(parts * trip_cols, -1).T
    quad_both = downs[:, trip_cols:].reshape(parts * quad_cols, -1).T
    both = jnp.concatenate([trip_both, quad_both], axis=1)
    down_full, radial_full = both[:channels], both[channels:]
    trip_width = trip_both.shape[1]
    quad_width = quad_both.shape[1]
    trip_folds = LANES // trip_width
    quad_folds = LANES // quad_width

    def group_rows(blocks, shape, folds):
        whole = jnp.concatenate(
            [unfold_lanes(block, shape[2]).reshape(shape) for block in blocks], axis=1
        )
        count, width, out = whole.shape
        split = whole.reshape(folds, count // folds, width, out)
        return jnp.transpose(split, (1, 0, 2, 3)).reshape(count // folds, folds * width, out)

    trip_bil = group_rows(
        [block[small_rows : small_rows + trip_bil_rows] for block in small],
        triplet_bilinear_weight.shape,
        trip_folds,
    )
    quad_bil = group_rows(
        [block[small_rows + trip_bil_rows :] for block in small],
        quad_bilinear.shape,
        quad_folds,
    )

    own_radial = own(radial, 0)
    down_pre = matmul(own_edges, down_full)
    radial_pre = matmul(own_radial, radial_full)
    dense = (jax.nn.silu(down_pre) * radial_pre).astype(BF16)
    trip_piece = fold_lanes(dense[:, :trip_width])
    quad_piece = fold_lanes(dense[:, trip_width:])
    trip_rows = trip_piece.shape[0]
    wire = jnp.concatenate([trip_piece, quad_piece], axis=0)
    before = edge_shift(wire, 1)
    later = edge_shift(wire, -1)
    own_across = chan_swap(wire, 2)
    own_beside = chan_swap(wire, 1)

    def spread(first, across):
        return [first, chan_swap(first, 1), across, chan_swap(across, 1)]

    before_across = chan_swap(before, 2)
    later_across = chan_swap(later, 2)
    wire_pieces = (
        spread(before, before_across)
        + [wire, own_beside, own_across, chan_swap(own_across, 1)]
        + spread(later, later_across)
    )

    def places(source):
        local = own(source, 1)
        within = local % edges_here
        owner = (within // edges) ^ rank
        return ((local // edges_here) * edges_here + owner * edges + within % edges).reshape(-1)

    trip_index = places(trip_source)
    quad_index = places(quad_source)
    trip_basis, quad_basis = slot_basis(
        after(rank, wire), circular, trip_mask, spherical, quad_mask, edges
    )

    members = gate(
        [trip_up, quad_up, source_proj, target_proj, resid_first, resid_second, edge_to_atom], wire
    )
    large = jnp.concatenate(members[:5] + [columns(members[5]), columns(members[6])], axis=0)
    tag_onehot = (atom_tags[:, None] == jnp.arange(TAGS)[None, :]).astype(F32)
    atom_full = after(atom_emb, wire).astype(F32) + jnp.dot(
        tag_onehot, tag_table.astype(F32), precision=HIGHEST
    )
    atom_low = atom_full.astype(BF16)
    grad_blocks = after(grad_edges, wire).reshape(parts, edges, cols)
    grad_sent = [pick(grad_blocks, rank ^ step) for step in range(parts)]
    quad_agg, quad_sum = branch_forward(
        after(quad_index, large, atom_low, *grad_sent),
        wire_pieces,
        trip_rows,
        quad_basis,
        quad_bil,
        "quad_gather",
    )
    large_across, large_beside, atom_before, atom_later = gate(
        [chan_swap(large, 2), chan_swap(large, 1), edge_shift(atom_low, 1), edge_shift(atom_low, -1)],
        quad_agg,
    )

    trip_agg, trip_sum = branch_forward(
        after(trip_index, large_across, atom_before, atom_later),
        wire_pieces,
        0,
        trip_basis,
        trip_bil,
        "trip_gather",
    )
    grad_got = [grad_sent[0]] + [chan_swap(grad_sent[step], step) for step in range(1, parts)]
    large_diag, *grad_got = gate([chan_swap(large_across, 1)] + grad_got, trip_agg)
    large = reorder([large, large_beside, large_across, large_diag], rank)
    grad_two = jnp.concatenate(reorder(grad_got, rank), axis=1)
    sizes = [
        trip_up.shape[0],
        quad_up.shape[0],
        source_proj.shape[0],
        target_proj.shape[0],
        resid_first.shape[0],
        resid_second.size // LANES,
        edge_to_atom.size // LANES,
    ]

    def offsets_of(sizes):
        return [sum(sizes[:i]) for i in range(len(sizes) + 1)]

    offsets = offsets_of(sizes)

    def piece(item):
        return [block[offsets[item] : offsets[item + 1]] for block in large]

    trip_up_full = jnp.concatenate(piece(0), axis=1)
    quad_up_full = jnp.concatenate(piece(1), axis=1)
    proj_full = jnp.concatenate(
        [jnp.concatenate(piece(2), axis=1), jnp.concatenate(piece(3), axis=1)], axis=0
    )
    first_full = jnp.concatenate(piece(4), axis=1)
    second_full = jnp.concatenate(
        [uncolumns(block, resid_second.shape[1]) for block in piece(5)], axis=0
    )
    to_atom_full = jnp.concatenate(
        [uncolumns(block, edge_to_atom.shape[1]) for block in piece(6)], axis=0
    )

    atom_wide = jnp.concatenate([atom_before, atom_low, atom_later], axis=0)
    atom_total = edge_parts * atoms_here
    source_local = (own(edge_source, 0) - (edge_rank - 1) * atoms_here) % atom_total
    target_local = own(edge_target, 0) - edge_rank * atoms_here
    source_hot = (source_local[:, None] == jnp.arange(3 * atoms_here)[None, :]).astype(BF16)
    target_hot = (target_local[:, None] == jnp.arange(atoms_here)[None, :]).astype(BF16)
    ends = jnp.concatenate(
        [
            matmul(source_hot, atom_wide).astype(BF16),
            matmul(target_hot, atom_low).astype(BF16),
        ],
        axis=1,
    )

    message = matmul(ends, proj_full)
    trip_out_pre = matmul(trip_agg, trip_up_full)
    quad_out_pre = matmul(quad_agg, quad_up_full)
    hidden_one = (
        own_edges.astype(F32)
        + jax.nn.silu(trip_out_pre)
        + jax.nn.silu(quad_out_pre)
        + jax.nn.silu(message)
    )
    hidden_low = hidden_one.astype(BF16)
    first_pre = matmul(hidden_low, first_full)
    first_low = jax.nn.silu(first_pre).astype(BF16)
    second_pre = matmul(first_low, second_full)
    edges_low = (hidden_one + jax.nn.silu(second_pre)).astype(BF16)
    edge_sums = inner(target_hot, edges_low)
    sums_high = edge_sums.astype(BF16)
    sums_rest = (edge_sums - sums_high.astype(F32)).astype(BF16)
    atom_sum = matmul(sums_high, to_atom_full) + matmul(sums_rest, to_atom_full)
    atom_sum = atom_sum + chan_swap(atom_sum, 1)
    atom_sum = atom_sum + chan_swap(atom_sum, 2)

    atom_sum_low = atom_sum.astype(BF16)
    update_pre = matmul(atom_sum_low, atom_update)
    atoms_new = atom_full + jax.nn.silu(update_pre)
    atoms_low = atoms_new.astype(BF16)
    output_pre = matmul(atoms_low, output_first)
    output_low = jax.nn.silu(output_pre).astype(BF16)
    energy = matmul(output_low, output_second)
    output_second_grad = jnp.dot(grad_energy, output_low.astype(F32), precision=HIGHEST)
    output_grad = (
        grad_energy[:, None] * output_second.astype(F32)[None, :] * silu_grad(output_pre)
    ).astype(BF16)
    output_first_grad = inner(atoms_low, output_grad)
    atoms_new_grad = grad_atoms.astype(F32) + outer(output_grad, output_first)
    update_grad = (atoms_new_grad * silu_grad(update_pre)).astype(BF16)
    atom_update_grad = inner(atom_sum_low, update_grad)
    atom_sum_grad = outer(update_grad, atom_update).astype(BF16)

    edge_part_grad = matmul(target_hot, atom_sum_grad).astype(BF16)
    edge_to_atom_grad = inner(edges_low, edge_part_grad)
    two_grad = grad_two.astype(F32) + outer(edge_part_grad, to_atom_full)
    second_grad = (two_grad * silu_grad(second_pre)).astype(BF16)
    resid_second_grad = inner(first_low, second_grad)
    first_grad = (outer(second_grad, second_full) * silu_grad(first_pre)).astype(BF16)
    resid_first_grad = inner(hidden_low, first_grad)
    one_grad = two_grad + outer(first_grad, first_full)
    trip_out_grad = (one_grad * silu_grad(trip_out_pre)).astype(BF16)
    quad_out_grad = (one_grad * silu_grad(quad_out_pre)).astype(BF16)
    message_grad = (one_grad * silu_grad(message)).astype(BF16)
    trip_up_grad = inner(trip_agg, trip_out_grad)
    quad_up_grad = inner(quad_agg, quad_out_grad)
    trip_agg_grad = outer(trip_out_grad, trip_up_full).astype(BF16)
    quad_agg_grad = outer(quad_out_grad, quad_up_full).astype(BF16)
    proj_grad = inner(ends, message_grad)
    width = atom_low.shape[1]
    source_sums = inner(source_hot, message_grad).astype(BF16)
    target_sums = inner(target_hot, message_grad).astype(BF16)
    source_back = outer(source_sums, proj_full[:width])
    target_back = outer(target_sums, proj_full[width:])
    wide_atoms = source_back.reshape(3, atoms_here, width)
    wide_atoms = wide_atoms.at[1].add(target_back)

    def split(array, axis):
        return jnp.split(array, parts, axis=axis)

    def pack(members):
        packed = [
            jnp.concatenate([member[i] for member in members], axis=0).astype(BF16)
            for i in range(parts)
        ]
        return reorder(packed, rank)

    def ungroup(array, folds):
        groups, rows, out = array.shape
        array = array.reshape(groups, folds, rows // folds, out)
        return jnp.transpose(array, (1, 0, 2, 3)).reshape(groups * folds, rows // folds, out)

    trip_bilinear_grad = ungroup(
        jnp.einsum("gej,eo->gjo", trip_sum, trip_agg_grad, preferred_element_type=F32), trip_folds
    )
    quad_bilinear_grad = ungroup(
        jnp.einsum("gej,eo->gjo", quad_sum, quad_agg_grad, preferred_element_type=F32), quad_folds
    )
    packed = pack(
        [
            split(trip_up_grad, 1),
            split(quad_up_grad, 1),
            split(proj_grad[:width], 1),
            split(proj_grad[width:], 1),
            split(resid_first_grad, 1),
            [columns(block) for block in split(resid_second_grad, 0)],
            [columns(block) for block in split(edge_to_atom_grad, 0)],
            [fold_lanes(block.reshape(-1, trip_out)) for block in split(trip_bilinear_grad, 1)],
            [fold_lanes(block.reshape(-1, quad_out)) for block in split(quad_bilinear_grad, 1)],
        ]
    )
    atom_rows = jnp.concatenate(
        [columns(atom_update_grad), columns(output_first_grad)], axis=0
    ).astype(BF16)
    atom_quarter = pick(atom_rows.reshape(parts, -1, LANES), rank)

    def send_back(array):
        blocks = jnp.stack([array[:, i * cols : (i + 1) * cols] for i in range(parts)])
        return [pick(blocks, rank ^ step) for step in range(parts)]

    def receive(sent):
        return [sent[0]] + [chan_swap(sent[step], step) for step in range(1, parts)]

    out_sent = send_back(edges_low)
    one_sent = send_back(one_grad.astype(BF16))
    wide_low = wide_atoms.astype(BF16)

    trip_tables = branch_backward(
        after(trip_index, wide_low, *packed, *out_sent, *one_sent),
        trip_basis,
        trip_agg_grad,
        trip_bil,
        3,
        parts,
        "trip_scatter",
    )
    arrived = gate(
        [chan_swap(packed[1], 1), chan_swap(packed[3], 1), chan_swap(wide_low, 1)]
        + receive(out_sent)
        + receive(one_sent),
        trip_tables[0],
    )
    mine = packed[0].astype(F32) + arrived[0].astype(F32)
    other = (packed[2].astype(F32) + arrived[1].astype(F32)).astype(BF16)
    wide_low = (wide_low.astype(F32) + arrived[2].astype(F32)).astype(BF16)
    edges_out = jnp.concatenate(reorder(arrived[3 : 3 + parts], rank), axis=0)
    one_out = jnp.concatenate(reorder(arrived[3 + parts :], rank), axis=0)

    quad_tables = branch_backward(
        after(quad_index, wide_low, other, edges_out, one_out, *trip_tables),
        quad_basis,
        quad_agg_grad,
        quad_bil,
        3,
        parts,
        "quad_scatter",
    )
    other_got, wide_got, *trip_got = gate(
        [chan_swap(other, 2), chan_swap(wide_low, 2)] + receive(trip_tables), quad_tables[0]
    )
    quad_got = receive(quad_tables)
    mine = (mine + other_got.astype(F32)).astype(BF16)
    early = mine.shape[0]
    early_rows = jnp.concatenate([mine, atom_quarter], axis=0)
    total_rows = early_rows.shape[0]
    unit = 16 * edge_parts
    early_rows = jnp.pad(early_rows, ((0, -total_rows % unit), (0, 0)))
    early_part = edge_scatter(early_rows)

    table = jnp.concatenate([tree_sum(trip_got), tree_sum(quad_got)], axis=1)
    branch_grad = (
        table[1]
        + edge_shift(table[0].astype(BF16), -1).astype(F32)
        + edge_shift(table[2].astype(BF16), 1).astype(F32)
    )
    branch_grad = jnp.concatenate(
        [
            unfold_lanes(branch_grad[:trip_rows], trip_width),
            unfold_lanes(branch_grad[trip_rows:], quad_width),
        ],
        axis=1,
    )
    down_grad = (branch_grad * radial_pre * silu_grad(down_pre)).astype(BF16)
    radial_grad = (branch_grad * jax.nn.silu(down_pre)).astype(BF16)
    down_weight_grad = inner(own_edges, down_grad)
    radial_weight_grad = inner(own_radial, radial_grad)
    down_wire = jnp.concatenate(
        [fold_lanes(down_grad[:, :trip_width]), fold_lanes(down_grad[:, trip_width:])], axis=0
    )
    down_all = reorder(gather_chan(down_wire), rank)
    down_all = jnp.concatenate(
        [
            jnp.concatenate(
                [
                    unfold_lanes(block[:trip_rows], trip_width),
                    unfold_lanes(block[trip_rows:], quad_width),
                ],
                axis=1,
            )
            for block in down_all
        ],
        axis=0,
    )
    down_rows = lax.dynamic_slice_in_dim(down_full, rank * cols, cols, 0)
    down_all, down_rows = gate([down_all, down_rows])
    edge_grad = one_out.astype(F32) + outer(down_all, down_rows)

    wide_sum = wide_low.astype(F32) + wide_got.astype(F32)
    atom_grad = (
        atoms_new_grad
        + wide_sum[1]
        + edge_shift(wide_sum[0].astype(BF16), -1).astype(F32)
        + edge_shift(wide_sum[2].astype(BF16), 1).astype(F32)
    )
    tag_table_grad = jnp.dot(tag_onehot.T, atom_grad, precision=HIGHEST)
    tiny = edge_sum(jnp.concatenate([output_second_grad[None], tag_table_grad], axis=0))

    small_grad = jnp.concatenate([down_weight_grad, radial_weight_grad], axis=0)
    late_sent = pack(
        [
            [
                columns(jnp.concatenate([trip_block, quad_block], axis=1).T)
                for trip_block, quad_block in zip(
                    split(small_grad[:, :trip_width], 1), split(small_grad[:, trip_width:], 1)
                )
            ]
        ]
    )
    late = edge_total(tree_sum(receive(late_sent)).astype(BF16)).astype(F32)
    summed = edge_gather(early_part)[:total_rows]
    atom_out = jnp.concatenate(reorder(gather_direct(summed[early:]), rank), axis=0).astype(F32)
    summed = summed[:early].astype(F32)
    sizes = sizes + [trip_bil_rows, quad_bilinear.size // LANES]
    offsets = offsets_of(sizes)
    parts_out = [summed[offsets[i] : offsets[i + 1]] for i in range(len(sizes))]
    small_out = uncolumns(late, long).T
    trip_bil_out, quad_bil_out = parts_out[7:]
    half = atom_out.shape[0] // 2
    return (
        edges_out,
        atoms_low,
        energy,
        edge_grad,
        atom_grad,
        small_out[:channels, :trip_cols],
        small_out[channels:, :trip_cols],
        unfold_lanes(trip_bil_out, trip_out).reshape(triplet_bilinear_weight.shape),
        parts_out[0],
        small_out[:channels, trip_cols:],
        small_out[channels:, trip_cols:],
        unfold_lanes(quad_bil_out, quad_out).reshape(quad_bilinear.shape),
        parts_out[1],
        parts_out[2],
        parts_out[3],
        parts_out[4],
        uncolumns(parts_out[5], resid_second.shape[1]),
        uncolumns(parts_out[6], edge_to_atom.shape[1]),
        uncolumns(atom_out[:half], atom_update.shape[1]),
        uncolumns(atom_out[half:], output_first.shape[1]),
        tiny[0],
        tiny[1:],
    )


def solution(mesh):
    return jax.shard_map(
        per_device,
        mesh=mesh,
        in_specs=(
            P("edge", "chan"),
            P("edge", None),
            P("edge", None),
            P(None, None, "edge"),
            P(None, None, "edge"),
            P("edge"),
            P("edge"),
            P("edge"),
            P(None, "edge"),
            P(None, "edge"),
            P(None, "edge"),
            P(None, "edge"),
            P(None, "chan"),
            P(None, "chan"),
            P(None, "chan", None),
            P(None, "chan"),
            P(None, "chan"),
            P(None, "chan"),
            P(None, "chan", None),
            P(None, "chan"),
            P(None, "chan"),
            P(None, "chan"),
            P(None, "chan"),
            P("chan", None),
            P("chan", None),
            P(),
            P(),
            P(),
            P(),
            P("edge", "chan"),
            P("edge", None),
            P("edge"),
        ),
        out_specs=(
            P("edge", "chan"),
            P("edge", None),
            P("edge"),
            P("edge", "chan"),
            P("edge", None),
            P(None, "chan"),
            P(None, "chan"),
            P(None, "chan", None),
            P(None, "chan"),
            P(None, "chan"),
            P(None, "chan"),
            P(None, "chan", None),
            P(None, "chan"),
            P(None, "chan"),
            P(None, "chan"),
            P(None, "chan"),
            P("chan", None),
            P("chan", None),
            P(),
            P(),
            P(),
            P(),
        ),
        check_vma=False,
    )
```

```python
import functools

import jax
import jax.numpy as jnp
from jax import lax
from jax.experimental import pallas as pl
from jax.experimental.pallas import tpu as pltpu
from jax.sharding import PartitionSpec as P

TAGS = 3
LANES = 128
BLOCK = 16
BF16 = jnp.bfloat16
F32 = jnp.float32
HIGHEST = lax.Precision.HIGHEST


def chan_swap(value, mask):
    count = lax.axis_size("chan")
    return lax.ppermute(value, "chan", [(i, i ^ mask) for i in range(count)])


def edge_swap(value, mask):
    count = lax.axis_size("edge")
    return lax.ppermute(value, "edge", [(i, i ^ mask) for i in range(count)])


def edge_shift(value, step):
    count = lax.axis_size("edge")
    return lax.ppermute(value, "edge", [(i, (i + step) % count) for i in range(count)])


def gate(*values):
    return list(lax.optimization_barrier(values))


def gather_direct(value):
    return [value] + [chan_swap(value, step) for step in (1, 2, 3)]


def pick(blocks, place):
    return lax.dynamic_index_in_dim(blocks, place, 0, keepdims=False)


def reorder(blocks, rank):
    low_bit = (rank & 1) == 1
    high_bit = (rank & 2) == 2
    first = [jnp.where(low_bit, blocks[i ^ 1], blocks[i]) for i in range(4)]
    return [jnp.where(high_bit, first[i ^ 2], first[i]) for i in range(4)]


def gather_chan(value):
    across = chan_swap(value, 2)
    beside = chan_swap(jnp.stack([value, across]), 1)
    return [value, beside[0], across, beside[1]]


def exchange(blocks, rank):
    got = [pick(blocks, rank)]
    for step in (1, 2, 3):
        got.append(chan_swap(pick(blocks, rank ^ step), step))
    return reorder(got, rank)


def silu_grad(pre_act):
    sigmoid = jax.nn.sigmoid(pre_act)
    return sigmoid * (1.0 + pre_act * (1.0 - sigmoid))


def matmul(first_op, second_op):
    return jnp.dot(first_op, second_op, preferred_element_type=F32)


def inner(first_op, second_op):
    return lax.dot_general(
        first_op, second_op, (((0,), (0,)), ((), ())), preferred_element_type=F32
    )


def outer(first_op, second_op):
    return lax.dot_general(
        first_op, second_op, (((1,), (1,)), ((), ())), preferred_element_type=F32
    )


def block_weights(basis_ref, block, diagonal):
    basis = basis_ref[block].astype(F32)
    count, width = basis.shape
    spread = jnp.broadcast_to(basis[:, None, :], (count, BLOCK, width))
    spread = spread.reshape(count * BLOCK, width)
    return jnp.where(diagonal, spread, 0.0).astype(BF16)


def diagonal_mask(rows, width):
    row = lax.broadcasted_iota(jnp.int32, (rows, width), 0) % BLOCK
    col = lax.broadcasted_iota(jnp.int32, (rows, width), 1) % BLOCK
    return row == col


def lane_groups(value, width):
    group = lax.broadcasted_iota(jnp.int32, value.shape, 1) // width
    zero = jnp.zeros_like(value)
    masked = [jnp.where(group == fold, value, zero) for fold in range(LANES // width)]
    return jnp.concatenate(masked, axis=0)


def gather_body(index_ref, basis_ref, bilinear_ref, *refs, folds, first_row, count):
    packed_refs = refs[:count]
    agg_ref, sum_ref, table, rows_a, rows_b = refs[-5:]
    groups, edges, _ = sum_ref.shape
    basis_count = groups * folds
    width = LANES // folds
    piece_rows = edges // folds
    slots = basis_ref.shape[2] // BLOCK
    step = min(piece_rows, 128)
    lane = lax.broadcasted_iota(jnp.int32, (step, LANES), 1) // width

    for piece, packed_ref in enumerate(packed_refs):

        def unpack(turn, _, piece=piece, packed_ref=packed_ref):
            start = pl.multiple_of(turn * step, step)
            values = packed_ref[pl.ds(first_row + start, step), :].astype(F32)
            turned = [values] + [
                pltpu.roll(values, shift * width, 1) for shift in range(1, folds)
            ]
            for fold in range(folds):
                place = pl.multiple_of((piece * folds + fold) * piece_rows + start, step)
                spread = turned[(0 - fold) % folds]
                for group in range(1, folds):
                    spread = jnp.where(lane == group, turned[(group - fold) % folds], spread)
                table[pl.ds(place, step), :] = spread
            return 0

        lax.fori_loop(0, piece_rows // step, unpack, 0)
    diagonal = diagonal_mask(basis_count * BLOCK, slots * BLOCK)

    def fetch(block, rows):
        base = block * BLOCK
        for slot in range(slots):
            for within in range(BLOCK):
                place = index_ref[slot * edges + base + within]
                at = slot * BLOCK + within
                rows[pl.ds(at, 1), :] = table[pl.ds(place, 1), :]

    def combine(block, rows):
        weights = block_weights(basis_ref, block, diagonal)
        each = groups * BLOCK
        joined = jnp.concatenate(
            [weights[fold * each : (fold + 1) * each] for fold in range(folds)], axis=1
        )
        got = matmul(joined, lane_groups(rows[...].astype(BF16), width)).astype(BF16)
        start = pl.multiple_of(block * BLOCK, BLOCK)
        sum_ref[:, pl.ds(start, BLOCK), :] = got.reshape(groups, BLOCK, LANES)

    blocks = edges // BLOCK
    fetch(0, rows_a)

    def turn(pair, _):
        fetch(2 * pair + 1, rows_b)
        combine(2 * pair, rows_a)
        fetch(jnp.minimum(2 * pair + 2, blocks - 1), rows_a)
        combine(2 * pair + 1, rows_b)
        return 0

    lax.fori_loop(0, blocks // 2, turn, 0)
    total = matmul(sum_ref[0], bilinear_ref[0])
    for group in range(1, groups):
        total = total + matmul(sum_ref[group], bilinear_ref[group])
    agg_ref[...] = total.astype(BF16)


def branch_forward(index, packed, first_row, basis, bilinear, needed, name):
    groups, _, out_width = bilinear.shape
    edges = basis.shape[0] * BLOCK
    folds = basis.shape[1] // groups
    vmem = pl.BlockSpec(memory_space=pltpu.VMEM)
    return pl.pallas_call(
        functools.partial(
            gather_body, folds=folds, first_row=first_row, count=len(packed)
        ),
        out_shape=(
            jax.ShapeDtypeStruct((edges, out_width), BF16),
            jax.ShapeDtypeStruct((groups, edges, LANES), BF16),
        ),
        in_specs=[pl.BlockSpec(memory_space=pltpu.SMEM)]
        + [vmem] * (2 + len(packed))
        + [pl.BlockSpec(memory_space=pl.ANY)] * len(needed),
        out_specs=(vmem, vmem),
        scratch_shapes=[
            pltpu.VMEM((len(packed) * edges, LANES), F32),
            pltpu.VMEM((basis.shape[2], LANES), F32),
            pltpu.VMEM((basis.shape[2], LANES), F32),
        ],
        compiler_params=pltpu.CompilerParams(vmem_limit_bytes=56 << 20),
        cost_estimate=pl.CostEstimate(flops=20 * 10**9, transcendentals=0, bytes_accessed=10**7),
        name=name,
    )(index, basis, bilinear, *packed, *needed)


def basis_body(rank_ref, trip_vals, trip_keep, quad_vals, quad_keep, trip_ref, quad_ref, trip_rows, quad_rows):
    del rank_ref
    tile_slots = LANES // BLOCK

    def build(vals_ref, keep_ref, out_ref, rows):
        count, slots, _ = vals_ref.shape
        vals = vals_ref[...].astype(F32) * keep_ref[...].astype(F32)[None]
        rows[...] = vals.reshape(count * slots, LANES)
        group = lax.broadcasted_iota(jnp.int32, (count, LANES), 1) // BLOCK
        for tile in range(slots // tile_slots):
            by_slot = [
                rows[pl.ds(tile * tile_slots + slot, count, stride=slots), :]
                for slot in range(tile_slots)
            ]
            for block in range(tile_slots):
                joined = None
                for slot, value in enumerate(by_slot):
                    shift = (slot - block) * BLOCK % LANES
                    turned = pltpu.roll(value, shift, 1) if shift else value
                    joined = turned if joined is None else jnp.where(group == slot, turned, joined)
                out_ref[block, :, tile * LANES : (tile + 1) * LANES] = joined.astype(BF16)

    build(trip_vals, trip_keep, trip_ref, trip_rows)
    build(quad_vals, quad_keep, quad_ref, quad_rows)


def slot_basis(rank, circular, trip_mask, spherical, quad_mask, edges):
    steps = edges // LANES
    blocks = LANES // BLOCK

    def source(array):
        shape = array.shape[:-1] + (LANES,)
        lead = (0,) * (len(shape) - 1)
        return pl.BlockSpec(shape, lambda step, rank_ref: lead + (rank_ref[0] * steps + step,))

    def target(count, slots):
        return pl.BlockSpec((blocks, count, slots * BLOCK), lambda step, rank_ref: (step, 0, 0))

    def shape_of(array):
        count, slots, _ = array.shape
        return jax.ShapeDtypeStruct((edges // BLOCK, count, slots * BLOCK), BF16)

    def rows_of(array):
        return pltpu.VMEM((array.shape[0] * array.shape[1], LANES), F32)

    return pl.pallas_call(
        basis_body,
        grid_spec=pltpu.PrefetchScalarGridSpec(
            num_scalar_prefetch=1,
            grid=(steps,),
            in_specs=[source(circular), source(trip_mask), source(spherical), source(quad_mask)],
            out_specs=[target(*circular.shape[:2]), target(*spherical.shape[:2])],
            scratch_shapes=[rows_of(circular), rows_of(spherical)],
        ),
        out_shape=(shape_of(circular), shape_of(spherical)),
        cost_estimate=pl.CostEstimate(flops=10 * 10**9, transcendentals=0, bytes_accessed=10**7),
        name="slot_basis",
    )(rank[None], circular, trip_mask, spherical, quad_mask)


TABLES = 4


def scatter_body(
    index_ref, basis_ref, grad_ref, bilinear_ref, *refs, folds, owners, needed
):
    refs = refs[needed:]
    packed_refs = refs[:owners]
    part, rows_a, rows_b = refs[owners : owners + 3]
    tables = refs[owners + 3 :]
    sides, piece_rows, _ = packed_refs[0].shape
    groups, edges, _ = part.shape
    basis_count = groups * folds
    width = LANES // folds
    slots = basis_ref.shape[2] // BLOCK
    chunk = 256
    table_rows = tables[0].shape[0]

    def clear(turn, _):
        start = pl.multiple_of(turn * chunk, chunk)
        for table in tables:
            table[pl.ds(start, chunk), :] = jnp.zeros((chunk, LANES), F32)
        return 0

    lax.fori_loop(0, table_rows // chunk, clear, 0)
    for group in range(groups):
        part[group] = outer(grad_ref[...], bilinear_ref[group]).astype(BF16)
    diagonal = diagonal_mask(basis_count * BLOCK, slots * BLOCK)

    def spread(block, rows):
        weights = block_weights(basis_ref, block, diagonal)
        start = pl.multiple_of(block * BLOCK, BLOCK)
        values = part[:, pl.ds(start, BLOCK), :].reshape(groups * BLOCK, LANES)
        rows[...] = inner(weights, lane_groups(values, width))

    def store(block, rows):
        base = block * BLOCK
        for slot in range(slots):
            for within in range(BLOCK):
                place = index_ref[slot * edges + base + within]
                at = slot * BLOCK + within
                table = tables[at % len(tables)]
                table[pl.ds(place, 1), :] += rows[pl.ds(at, 1), :]

    blocks = edges // BLOCK
    spread(0, rows_a)

    def turn(pair, _):
        spread(2 * pair + 1, rows_b)
        store(2 * pair, rows_a)
        spread(jnp.minimum(2 * pair + 2, blocks - 1), rows_a)
        store(2 * pair + 1, rows_b)
        return 0

    lax.fori_loop(0, blocks // 2, turn, 0)
    step = min(piece_rows, 128)
    per_piece = piece_rows // step
    lane = lax.broadcasted_iota(jnp.int32, (step, LANES), 1) // width

    for owner, packed_ref in enumerate(packed_refs):

        def pack(turn, _, owner=owner, packed_ref=packed_ref):
            side = turn // per_piece
            piece = side * owners + owner
            start = pl.multiple_of((turn % per_piece) * step, step)
            joined = jnp.zeros((step, LANES), F32)
            for fold in range(folds):
                place = pl.multiple_of((piece * folds + fold) * piece_rows + start, step)
                total = tables[0][pl.ds(place, step), :]
                for table in tables[1:]:
                    total = total + table[pl.ds(place, step), :]
                shift = LANES // 2
                while shift >= width:
                    total = total + pltpu.roll(total, shift, 1)
                    shift //= 2
                joined = jnp.where(lane == fold, total, joined)
            packed_ref[side, pl.ds(start, step), :] = joined.astype(BF16)
            return 0

        lax.fori_loop(0, sides * per_piece, pack, 0)


def branch_backward(index, basis, grad, bilinear, sides, owners, needed, name):
    edges = grad.shape[0]
    groups = bilinear.shape[0]
    folds = basis.shape[1] // groups
    vmem = pl.BlockSpec(memory_space=pltpu.VMEM)
    out = jax.ShapeDtypeStruct((sides, edges // folds, LANES), BF16)
    return pl.pallas_call(
        functools.partial(scatter_body, folds=folds, owners=owners, needed=len(needed)),
        out_shape=(out,) * owners,
        in_specs=[pl.BlockSpec(memory_space=pltpu.SMEM), vmem, vmem, vmem]
        + [pl.BlockSpec(memory_space=pl.ANY)] * len(needed),
        out_specs=(vmem,) * owners,
        scratch_shapes=[
            pltpu.VMEM((groups, edges, LANES), BF16),
            pltpu.VMEM((basis.shape[2], LANES), F32),
            pltpu.VMEM((basis.shape[2], LANES), F32),
        ]
        + [pltpu.VMEM((sides * owners * edges, LANES), F32)] * TABLES,
        compiler_params=pltpu.CompilerParams(vmem_limit_bytes=58 << 20),
        cost_estimate=pl.CostEstimate(flops=20 * 10**9, transcendentals=0, bytes_accessed=10**7),
        name=name,
    )(index, basis, grad, bilinear, *needed)


def fold_lanes(rows):
    count, width = rows.shape
    folds = LANES // width
    each = count // folds
    return jnp.concatenate([rows[i * each : (i + 1) * each] for i in range(folds)], axis=1)


def unfold_lanes(packed, width):
    folds = LANES // width
    return jnp.concatenate([packed[:, i * width : (i + 1) * width] for i in range(folds)], axis=0)


def columns(array):
    return jnp.concatenate(
        [array[:, i : i + LANES] for i in range(0, array.shape[1], LANES)], axis=0
    )


def uncolumns(rows, width):
    each = rows.shape[0] * LANES // width
    return jnp.concatenate(
        [rows[i * each : (i + 1) * each] for i in range(width // LANES)], axis=1
    )


def edge_steps():
    steps = []
    size = 1
    while size < lax.axis_size("edge"):
        steps.append(size)
        size *= 2
    return steps


def halve(value, mask):
    bit = (lax.axis_index("edge") & mask) != 0
    half = value.shape[0] // 2
    keep = jnp.where(bit, value[half:], value[:half])
    send = jnp.where(bit, value[:half], value[half:])
    return keep, send


def join_halves(value, mask):
    bit = (lax.axis_index("edge") & mask) != 0
    got = edge_swap(value, mask)
    return jnp.concatenate([jnp.where(bit, got, value), jnp.where(bit, value, got)], axis=0)


def tree_sum(values):
    values = [value.astype(F32) for value in values]
    while len(values) > 1:
        values = [values[i] + values[i + 1] for i in range(0, len(values), 2)]
    return values[0]


def edge_total(value):
    for mask in edge_steps():
        value = (value.astype(F32) + edge_swap(value, mask).astype(F32)).astype(BF16)
    return value


def per_device(
    edge_emb,
    atom_emb,
    radial,
    circular,
    spherical,
    atom_tags,
    edge_source,
    edge_target,
    trip_source,
    trip_mask,
    quad_source,
    quad_mask,
    triplet_down_weight,
    trip_radial,
    triplet_bilinear_weight,
    trip_up,
    quad_down,
    quad_radial,
    quad_bilinear,
    quad_up,
    source_proj,
    target_proj,
    resid_first,
    resid_second,
    edge_to_atom,
    atom_update,
    output_first,
    output_second,
    tag_table,
    grad_edges,
    grad_atoms,
    grad_energy,
):
    edges_here = edge_emb.shape[0]
    atoms_here = atom_emb.shape[0]
    parts = lax.axis_size("chan")
    edge_parts = lax.axis_size("edge")
    rank = lax.axis_index("chan")
    edge_rank = lax.axis_index("edge")
    edges = edges_here // parts
    cols = edge_emb.shape[1]
    start = rank * edges

    def own(array, axis):
        return lax.dynamic_slice_in_dim(array, start, edges, axis)

    edge_blocks = edge_emb.reshape(parts, edges, cols)
    own_edges = jnp.concatenate(exchange(edge_blocks, rank), axis=1)

    trip_cols = triplet_down_weight.shape[1]
    quad_cols = quad_down.shape[1]
    trip_out = triplet_bilinear_weight.shape[2]
    quad_out = quad_bilinear.shape[2]
    down_own = jnp.concatenate([triplet_down_weight, quad_down], axis=1)
    small = jnp.concatenate(
        [
            columns(
                jnp.concatenate(
                    [down_own, jnp.concatenate([trip_radial, quad_radial], axis=1)], axis=0
                ).T
            ),
            fold_lanes(triplet_bilinear_weight.reshape(-1, trip_out)),
            fold_lanes(quad_bilinear.reshape(-1, quad_out)),
        ],
        axis=0,
    )
    small = reorder(gather_direct(small), rank)
    channels = parts * cols
    long = channels + radial.shape[1]
    small_rows = (trip_cols + quad_cols) * long // LANES
    trip_bil_rows = triplet_bilinear_weight.size // LANES
    downs = jnp.stack([uncolumns(block[:small_rows], long) for block in small])
    trip_both = downs[:, :trip_cols].reshape(parts * trip_cols, -1).T
    quad_both = downs[:, trip_cols:].reshape(parts * quad_cols, -1).T
    both = jnp.concatenate([trip_both, quad_both], axis=1)
    down_full, radial_full = both[:channels], both[channels:]
    trip_width = trip_both.shape[1]
    quad_width = quad_both.shape[1]
    trip_folds = LANES // trip_width
    quad_folds = LANES // quad_width

    def group_rows(blocks, shape, folds):
        whole = jnp.concatenate(
            [unfold_lanes(block, shape[2]).reshape(shape) for block in blocks], axis=1
        )
        count, width, out = whole.shape
        split = whole.reshape(folds, count // folds, width, out)
        return jnp.transpose(split, (1, 0, 2, 3)).reshape(count // folds, folds * width, out)

    trip_bil = group_rows(
        [block[small_rows : small_rows + trip_bil_rows] for block in small],
        triplet_bilinear_weight.shape,
        trip_folds,
    )
    quad_bil = group_rows(
        [block[small_rows + trip_bil_rows :] for block in small],
        quad_bilinear.shape,
        quad_folds,
    )

    own_radial = own(radial, 0)
    down_pre = matmul(own_edges, down_full)
    radial_pre = matmul(own_radial, radial_full)
    dense = (jax.nn.silu(down_pre) * radial_pre).astype(BF16)
    trip_piece = fold_lanes(dense[:, :trip_width])
    quad_piece = fold_lanes(dense[:, trip_width:])
    trip_rows = trip_piece.shape[0]
    wire = jnp.concatenate([trip_piece, quad_piece], axis=0)
    rank_now, wire, *members, atom_emb, grad_edges = gate(
        rank,
        wire,
        trip_up,
        quad_up,
        source_proj,
        target_proj,
        resid_first,
        resid_second,
        edge_to_atom,
        atom_emb,
        grad_edges,
    )
    before = edge_shift(wire, 1)
    later = edge_shift(wire, -1)
    own_across = chan_swap(wire, 2)
    own_beside = chan_swap(wire, 1)

    def spread(first, across):
        return [first, chan_swap(first, 1), across, chan_swap(across, 1)]

    before_across = chan_swap(before, 2)
    later_across = chan_swap(later, 2)
    wire_pieces = (
        spread(before, before_across)
        + [wire, own_beside, own_across, chan_swap(own_across, 1)]
        + spread(later, later_across)
    )

    def places(source):
        local = own(source, 1)
        within = local % edges_here
        owner = (within // edges) ^ rank
        return ((local // edges_here) * edges_here + owner * edges + within % edges).reshape(-1)

    trip_index = places(trip_source)
    quad_index = places(quad_source)
    trip_basis, quad_basis = slot_basis(
        rank_now, circular, trip_mask, spherical, quad_mask, edges
    )

    large = jnp.concatenate(members[:5] + [columns(members[5]), columns(members[6])], axis=0)
    tag_onehot = (atom_tags[:, None] == jnp.arange(TAGS)[None, :]).astype(F32)
    atom_full = atom_emb.astype(F32) + jnp.dot(
        tag_onehot, tag_table.astype(F32), precision=HIGHEST
    )
    atom_low = atom_full.astype(BF16)
    grad_blocks = grad_edges.reshape(parts, edges, cols)
    grad_sent = [pick(grad_blocks, rank ^ step) for step in range(parts)]
    quad_agg, quad_sum = branch_forward(
        quad_index,
        wire_pieces,
        trip_rows,
        quad_basis,
        quad_bil,
        [large, atom_low] + grad_sent,
        "quad_gather",
    )
    large_across, large_beside, atom_before, atom_later, quad_agg, *grad_sent = gate(
        chan_swap(large, 2),
        chan_swap(large, 1),
        edge_shift(atom_low, 1),
        edge_shift(atom_low, -1),
        quad_agg,
        *grad_sent,
    )

    trip_agg, trip_sum = branch_forward(
        trip_index,
        wire_pieces,
        0,
        trip_basis,
        trip_bil,
        [large_across, atom_before, atom_later] + grad_sent,
        "trip_gather",
    )
    grad_got = [grad_sent[0]] + [chan_swap(grad_sent[step], step) for step in range(1, parts)]
    large_diag, trip_agg, *grad_got = gate(chan_swap(large_across, 1), trip_agg, *grad_got)
    large = reorder([large, large_beside, large_across, large_diag], rank)
    grad_two = jnp.concatenate(reorder(grad_got, rank), axis=1)
    sizes = [
        trip_up.shape[0],
        quad_up.shape[0],
        source_proj.shape[0],
        target_proj.shape[0],
        resid_first.shape[0],
        resid_second.size // LANES,
        edge_to_atom.size // LANES,
    ]

    def offsets_of(sizes):
        return [sum(sizes[:i]) for i in range(len(sizes) + 1)]

    offsets = offsets_of(sizes)

    def piece(item):
        return [block[offsets[item] : offsets[item + 1]] for block in large]

    trip_up_full = jnp.concatenate(piece(0), axis=1)
    quad_up_full = jnp.concatenate(piece(1), axis=1)
    proj_full = jnp.concatenate(
        [jnp.concatenate(piece(2), axis=1), jnp.concatenate(piece(3), axis=1)], axis=0
    )
    first_full = jnp.concatenate(piece(4), axis=1)
    second_full = jnp.concatenate(
        [uncolumns(block, resid_second.shape[1]) for block in piece(5)], axis=0
    )
    to_atom_full = jnp.concatenate(
        [uncolumns(block, edge_to_atom.shape[1]) for block in piece(6)], axis=0
    )

    atom_wide = jnp.concatenate([atom_before, atom_low, atom_later], axis=0)
    atom_total = edge_parts * atoms_here
    source_local = (own(edge_source, 0) - (edge_rank - 1) * atoms_here) % atom_total
    target_local = own(edge_target, 0) - edge_rank * atoms_here
    source_hot = (source_local[:, None] == jnp.arange(3 * atoms_here)[None, :]).astype(BF16)
    target_hot = (target_local[:, None] == jnp.arange(atoms_here)[None, :]).astype(BF16)
    ends = jnp.concatenate(
        [
            matmul(source_hot, atom_wide).astype(BF16),
            matmul(target_hot, atom_low).astype(BF16),
        ],
        axis=1,
    )

    message = matmul(ends, proj_full)
    trip_out_pre = matmul(trip_agg, trip_up_full)
    quad_out_pre = matmul(quad_agg, quad_up_full)
    hidden_one = (
        own_edges.astype(F32)
        + jax.nn.silu(trip_out_pre)
        + jax.nn.silu(quad_out_pre)
        + jax.nn.silu(message)
    )
    hidden_low = hidden_one.astype(BF16)
    first_pre = matmul(hidden_low, first_full)
    first_low = jax.nn.silu(first_pre).astype(BF16)
    second_pre = matmul(first_low, second_full)
    edges_low = (hidden_one + jax.nn.silu(second_pre)).astype(BF16)
    edge_sums = inner(target_hot, edges_low)
    sums_high = edge_sums.astype(BF16)
    sums_rest = (edge_sums - sums_high.astype(F32)).astype(BF16)
    atom_sum = matmul(sums_high, to_atom_full) + matmul(sums_rest, to_atom_full)
    atom_sum = atom_sum + chan_swap(atom_sum, 1)
    atom_sum = atom_sum + chan_swap(atom_sum, 2)
    atom_sum, edges_low = gate(atom_sum, edges_low)

    atom_sum_low = atom_sum.astype(BF16)
    update_pre = matmul(atom_sum_low, atom_update)
    atoms_new = atom_full + jax.nn.silu(update_pre)
    atoms_low = atoms_new.astype(BF16)
    output_pre = matmul(atoms_low, output_first)
    output_low = jax.nn.silu(output_pre).astype(BF16)
    energy = matmul(output_low, output_second)
    output_second_grad = jnp.dot(grad_energy, output_low.astype(F32), precision=HIGHEST)
    output_grad = (
        grad_energy[:, None] * output_second.astype(F32)[None, :] * silu_grad(output_pre)
    ).astype(BF16)
    output_first_grad = inner(atoms_low, output_grad)
    atoms_new_grad = grad_atoms.astype(F32) + outer(output_grad, output_first)
    update_grad = (atoms_new_grad * silu_grad(update_pre)).astype(BF16)
    atom_update_grad = inner(atom_sum_low, update_grad)
    atom_sum_grad = outer(update_grad, atom_update).astype(BF16)

    edge_part_grad = matmul(target_hot, atom_sum_grad).astype(BF16)
    edge_to_atom_grad = inner(edges_low, edge_part_grad)
    two_grad = grad_two.astype(F32) + outer(edge_part_grad, to_atom_full)
    second_grad = (two_grad * silu_grad(second_pre)).astype(BF16)
    resid_second_grad = inner(first_low, second_grad)
    first_grad = (outer(second_grad, second_full) * silu_grad(first_pre)).astype(BF16)
    resid_first_grad = inner(hidden_low, first_grad)
    one_grad = two_grad + outer(first_grad, first_full)
    trip_out_grad = (one_grad * silu_grad(trip_out_pre)).astype(BF16)
    quad_out_grad = (one_grad * silu_grad(quad_out_pre)).astype(BF16)
    message_grad = (one_grad * silu_grad(message)).astype(BF16)
    trip_up_grad = inner(trip_agg, trip_out_grad)
    quad_up_grad = inner(quad_agg, quad_out_grad)
    trip_agg_grad = outer(trip_out_grad, trip_up_full).astype(BF16)
    quad_agg_grad = outer(quad_out_grad, quad_up_full).astype(BF16)
    proj_grad = inner(ends, message_grad)
    width = atom_low.shape[1]
    source_sums = inner(source_hot, message_grad).astype(BF16)
    target_sums = inner(target_hot, message_grad).astype(BF16)
    source_back = outer(source_sums, proj_full[:width])
    target_back = outer(target_sums, proj_full[width:])
    wide_atoms = source_back.reshape(3, atoms_here, width)
    wide_atoms = wide_atoms.at[1].add(target_back)

    def split(array, axis):
        return jnp.split(array, parts, axis=axis)

    def pack(members):
        packed = [
            jnp.concatenate([member[i] for member in members], axis=0).astype(BF16)
            for i in range(parts)
        ]
        return reorder(packed, rank)

    def ungroup(array, folds):
        groups, rows, out = array.shape
        array = array.reshape(groups, folds, rows // folds, out)
        return jnp.transpose(array, (1, 0, 2, 3)).reshape(groups * folds, rows // folds, out)

    trip_bilinear_grad = ungroup(
        jnp.einsum("gej,eo->gjo", trip_sum, trip_agg_grad, preferred_element_type=F32), trip_folds
    )
    quad_bilinear_grad = ungroup(
        jnp.einsum("gej,eo->gjo", quad_sum, quad_agg_grad, preferred_element_type=F32), quad_folds
    )
    packed = pack(
        [
            split(trip_up_grad, 1),
            split(quad_up_grad, 1),
            split(proj_grad[:width], 1),
            split(proj_grad[width:], 1),
            split(resid_first_grad, 1),
            [columns(block) for block in split(resid_second_grad, 0)],
            [columns(block) for block in split(edge_to_atom_grad, 0)],
            [fold_lanes(block.reshape(-1, trip_out)) for block in split(trip_bilinear_grad, 1)],
            [fold_lanes(block.reshape(-1, quad_out)) for block in split(quad_bilinear_grad, 1)],
            [columns(wide_atoms.reshape(3 * atoms_here, width))] * parts,
        ]
    )
    atom_rows = jnp.concatenate(
        [columns(atom_update_grad), columns(output_first_grad)], axis=0
    ).astype(BF16)
    atom_quarter = pick(atom_rows.reshape(parts, -1, LANES), rank)

    def send_back(array):
        blocks = jnp.stack([array[:, i * cols : (i + 1) * cols] for i in range(parts)])
        return [pick(blocks, rank ^ step) for step in range(parts)]

    def receive(sent):
        return [sent[0]] + [chan_swap(sent[step], step) for step in range(1, parts)]

    out_sent = send_back(edges_low)
    edges_out = jnp.concatenate(reorder(receive(out_sent), rank), axis=0)

    trip_tables = branch_backward(
        trip_index,
        trip_basis,
        trip_agg_grad,
        trip_bil,
        3,
        parts,
        [edges_out] + packed,
        "trip_scatter",
    )
    *packed_got, own_table = gate(*receive(packed), trip_tables[0])
    trip_tables = [own_table] + list(trip_tables[1:])
    mine = tree_sum(packed_got)
    early = packed[0].shape[0] - 3 * atoms_here * width // LANES
    wide_sum = uncolumns(mine[early:], width).reshape(3, atoms_here, width)
    early_rows = jnp.concatenate([mine[:early].astype(BF16), atom_quarter], axis=0)
    total_rows = early_rows.shape[0]
    early_rows = jnp.pad(early_rows, ((0, -total_rows % (16 * edge_parts)), (0, 0)))
    steps = edge_steps()
    keep, send = halve(early_rows, steps[0])

    quad_tables = branch_backward(
        quad_index,
        quad_basis,
        quad_agg_grad,
        quad_bil,
        3,
        parts,
        [wide_sum, send] + trip_tables,
        "quad_scatter",
    )
    quad_tables = list(quad_tables)
    early_got, *trip_got = gate(
        edge_swap(send, steps[0]), *receive(trip_tables), *quad_tables
    )
    trip_got, quad_tables = trip_got[:parts], trip_got[parts:]
    quad_got = receive(quad_tables)
    early_part = (keep.astype(F32) + early_got.astype(F32)).astype(BF16)
    for mask in steps[1:]:
        keep, send = halve(early_part, mask)
        early_part = (keep.astype(F32) + edge_swap(send, mask).astype(F32)).astype(BF16)

    table = jnp.concatenate(
        [
            tree_sum(trip_got),
            tree_sum(quad_got),
            jnp.stack([columns(wide_sum[side]) for side in range(3)]),
        ],
        axis=1,
    )
    branch_grad = (
        table[1]
        + edge_shift(table[0].astype(BF16), -1).astype(F32)
        + edge_shift(table[2].astype(BF16), 1).astype(F32)
    )
    wire_rows = wire.shape[0]
    atom_grad = atoms_new_grad + uncolumns(branch_grad[wire_rows:], width)
    branch_grad = branch_grad[:wire_rows]
    branch_grad = jnp.concatenate(
        [
            unfold_lanes(branch_grad[:trip_rows], trip_width),
            unfold_lanes(branch_grad[trip_rows:], quad_width),
        ],
        axis=1,
    )
    down_grad = (branch_grad * radial_pre * silu_grad(down_pre)).astype(BF16)
    radial_grad = (branch_grad * jax.nn.silu(down_pre)).astype(BF16)
    down_weight_grad = inner(own_edges, down_grad)
    radial_weight_grad = inner(own_radial, radial_grad)
    edge_grad = (one_grad + outer(down_grad, down_full)).astype(BF16)
    edge_grad = jnp.concatenate(reorder(receive(send_back(edge_grad)), rank), axis=0).astype(F32)

    tag_table_grad = jnp.dot(tag_onehot.T, atom_grad, precision=HIGHEST)
    tiny = columns(jnp.concatenate([output_second_grad[None], tag_table_grad], axis=0))

    small_grad = jnp.concatenate([down_weight_grad, radial_weight_grad], axis=0)
    late_sent = pack(
        [
            [
                columns(jnp.concatenate([trip_block, quad_block], axis=1).T)
                for trip_block, quad_block in zip(
                    split(small_grad[:, :trip_width], 1), split(small_grad[:, trip_width:], 1)
                )
            ]
        ]
    )
    late = tree_sum(receive(late_sent))
    late_rows = late.shape[0]
    late = edge_total(jnp.concatenate([late, tiny], axis=0).astype(BF16)).astype(F32)
    tiny = uncolumns(late[late_rows:], width)
    late = late[:late_rows]
    summed = early_part
    for mask in reversed(steps):
        summed = join_halves(summed, mask)
    summed = summed[:total_rows]
    atom_out = jnp.concatenate(reorder(gather_direct(summed[early:]), rank), axis=0).astype(F32)
    summed = summed[:early].astype(F32)
    sizes = sizes + [trip_bil_rows, quad_bilinear.size // LANES]
    offsets = offsets_of(sizes)
    parts_out = [summed[offsets[i] : offsets[i + 1]] for i in range(len(sizes))]
    small_out = uncolumns(late, long).T
    trip_bil_out, quad_bil_out = parts_out[7:]
    half = atom_out.shape[0] // 2
    return (
        edges_out,
        atoms_low,
        energy,
        edge_grad,
        atom_grad,
        small_out[:channels, :trip_cols],
        small_out[channels:, :trip_cols],
        unfold_lanes(trip_bil_out, trip_out).reshape(triplet_bilinear_weight.shape),
        parts_out[0],
        small_out[:channels, trip_cols:],
        small_out[channels:, trip_cols:],
        unfold_lanes(quad_bil_out, quad_out).reshape(quad_bilinear.shape),
        parts_out[1],
        parts_out[2],
        parts_out[3],
        parts_out[4],
        uncolumns(parts_out[5], resid_second.shape[1]),
        uncolumns(parts_out[6], edge_to_atom.shape[1]),
        uncolumns(atom_out[:half], atom_update.shape[1]),
        uncolumns(atom_out[half:], output_first.shape[1]),
        tiny[0],
        tiny[1:],
    )


def solution(mesh):
    return jax.shard_map(
        per_device,
        mesh=mesh,
        in_specs=(
            P("edge", "chan"),
            P("edge", None),
            P("edge", None),
            P(None, None, "edge"),
            P(None, None, "edge"),
            P("edge"),
            P("edge"),
            P("edge"),
            P(None, "edge"),
            P(None, "edge"),
            P(None, "edge"),
            P(None, "edge"),
            P(None, "chan"),
            P(None, "chan"),
            P(None, "chan", None),
            P(None, "chan"),
            P(None, "chan"),
            P(None, "chan"),
            P(None, "chan", None),
            P(None, "chan"),
            P(None, "chan"),
            P(None, "chan"),
            P(None, "chan"),
            P("chan", None),
            P("chan", None),
            P(),
            P(),
            P(),
            P(),
            P("edge", "chan"),
            P("edge", None),
            P("edge"),
        ),
        out_specs=(
            P("edge", "chan"),
            P("edge", None),
            P("edge"),
            P("edge", "chan"),
            P("edge", None),
            P(None, "chan"),
            P(None, "chan"),
            P(None, "chan", None),
            P(None, "chan"),
            P(None, "chan"),
            P(None, "chan"),
            P(None, "chan", None),
            P(None, "chan"),
            P(None, "chan"),
            P(None, "chan"),
            P(None, "chan"),
            P("chan", None),
            P("chan", None),
            P(),
            P(),
            P(),
            P(),
        ),
        check_vma=False,
    )
```

```python
import functools

import jax
import jax.numpy as jnp
from jax import lax
from jax.experimental import pallas as pl
from jax.experimental.pallas import tpu as pltpu
from jax.sharding import PartitionSpec as P

TAGS = 3
LANES = 128
BLOCK = 16
BF16 = jnp.bfloat16
F32 = jnp.float32
HIGHEST = lax.Precision.HIGHEST


def chan_swap(value, mask):
    count = lax.axis_size("chan")
    return lax.ppermute(value, "chan", [(i, i ^ mask) for i in range(count)])


def edge_swap(value, mask):
    count = lax.axis_size("edge")
    return lax.ppermute(value, "edge", [(i, i ^ mask) for i in range(count)])


def edge_shift(value, step):
    count = lax.axis_size("edge")
    return lax.ppermute(value, "edge", [(i, (i + step) % count) for i in range(count)])


def gate(*values):
    return list(lax.optimization_barrier(values))


def gather_direct(value):
    return [value] + [chan_swap(value, step) for step in (1, 2, 3)]


def pick(blocks, place):
    return lax.dynamic_index_in_dim(blocks, place, 0, keepdims=False)


def reorder(blocks, rank):
    low_bit = (rank & 1) == 1
    high_bit = (rank & 2) == 2
    first = [jnp.where(low_bit, blocks[i ^ 1], blocks[i]) for i in range(4)]
    return [jnp.where(high_bit, first[i ^ 2], first[i]) for i in range(4)]


def gather_chan(value):
    across = chan_swap(value, 2)
    beside = chan_swap(jnp.stack([value, across]), 1)
    return [value, beside[0], across, beside[1]]


def exchange(blocks, rank):
    got = [pick(blocks, rank)]
    for step in (1, 2, 3):
        got.append(chan_swap(pick(blocks, rank ^ step), step))
    return reorder(got, rank)


def silu_grad(pre_act):
    sigmoid = jax.nn.sigmoid(pre_act)
    return sigmoid * (1.0 + pre_act * (1.0 - sigmoid))


def matmul(first_op, second_op):
    return jnp.dot(first_op, second_op, preferred_element_type=F32)


def inner(first_op, second_op):
    return lax.dot_general(
        first_op, second_op, (((0,), (0,)), ((), ())), preferred_element_type=F32
    )


def outer(first_op, second_op):
    return lax.dot_general(
        first_op, second_op, (((1,), (1,)), ((), ())), preferred_element_type=F32
    )


def block_weights(basis_ref, block, diagonal):
    basis = basis_ref[block].astype(F32)
    count, width = basis.shape
    spread = jnp.broadcast_to(basis[:, None, :], (count, BLOCK, width))
    spread = spread.reshape(count * BLOCK, width)
    return jnp.where(diagonal, spread, 0.0).astype(BF16)


def diagonal_mask(rows, width):
    row = lax.broadcasted_iota(jnp.int32, (rows, width), 0) % BLOCK
    col = lax.broadcasted_iota(jnp.int32, (rows, width), 1) % BLOCK
    return row == col


def lane_groups(value, width):
    group = lax.broadcasted_iota(jnp.int32, value.shape, 1) // width
    zero = jnp.zeros_like(value)
    masked = [jnp.where(group == fold, value, zero) for fold in range(LANES // width)]
    return jnp.concatenate(masked, axis=0)


def slot_copies(whole_ref, slot_refs, sems, first):
    copies = []
    for slot, slot_ref in enumerate(slot_refs):
        size = slot_ref.shape[0]
        copies.append(
            pltpu.make_async_copy(
                whole_ref.at[pl.ds(slot * size, size)], slot_ref, sems.at[first + slot]
            )
        )
    return copies


def gather_body(index_ref, basis_ref, bilinear_ref, *refs, folds, first_row, count):
    packed_refs = refs[:count]
    slots = basis_ref.shape[2] // BLOCK
    agg_ref, sum_ref, table, rows_a, rows_b, sems = refs[-6 - slots : -slots]
    slot_refs = refs[-slots:]
    copies = slot_copies(index_ref, slot_refs, sems, 0)
    for copy in copies:
        copy.start()
    groups, edges, _ = sum_ref.shape
    basis_count = groups * folds
    width = LANES // folds
    piece_rows = edges // folds
    step = min(piece_rows, 256 // folds)
    lane = lax.broadcasted_iota(jnp.int32, (step, LANES), 1) // width

    for piece, packed_ref in enumerate(packed_refs):

        def unpack(turn, _, piece=piece, packed_ref=packed_ref):
            start = pl.multiple_of(turn * step, step)
            values = packed_ref[pl.ds(first_row + start, step), :].astype(F32)
            turned = [values] + [
                pltpu.roll(values, shift * width, 1) for shift in range(1, folds)
            ]
            for fold in range(folds):
                place = pl.multiple_of((piece * folds + fold) * piece_rows + start, step)
                spread = turned[(0 - fold) % folds]
                for group in range(1, folds):
                    spread = jnp.where(lane == group, turned[(group - fold) % folds], spread)
                table[pl.ds(place, step), :] = spread
            return 0

        lax.fori_loop(0, piece_rows // step, unpack, 0)
    for copy in copies:
        copy.wait()
    diagonal = diagonal_mask(basis_count * BLOCK, slots * BLOCK)

    def fetch(block, rows):
        base = block * BLOCK
        for within in range(BLOCK):
            edge = base + within
            for slot in range(slots):
                place = slot_refs[slot][edge]
                at = slot * BLOCK + within
                rows[pl.ds(at, 1), :] = table[pl.ds(place, 1), :]

    def combine(block, values):
        weights = block_weights(basis_ref, block, diagonal)
        each = groups * BLOCK
        joined = jnp.concatenate(
            [weights[fold * each : (fold + 1) * each] for fold in range(folds)], axis=1
        )
        got = matmul(joined, lane_groups(values, width)).astype(BF16)
        start = pl.multiple_of(block * BLOCK, BLOCK)
        sum_ref[:, pl.ds(start, BLOCK), :] = got.reshape(groups, BLOCK, LANES)

    blocks = edges // BLOCK
    fetch(0, rows_a)
    fetch(1, rows_b)

    def turn(pair, _):
        values_a = rows_a[...].astype(BF16)
        values_b = rows_b[...].astype(BF16)
        fetch(jnp.minimum(2 * pair + 2, blocks - 1), rows_a)
        fetch(jnp.minimum(2 * pair + 3, blocks - 1), rows_b)
        combine(2 * pair, values_a)
        combine(2 * pair + 1, values_b)
        return 0

    lax.fori_loop(0, blocks // 2, turn, 0)
    total = matmul(sum_ref[0], bilinear_ref[0])
    for group in range(1, groups):
        total = total + matmul(sum_ref[group], bilinear_ref[group])
    agg_ref[...] = total.astype(BF16)


def branch_forward(index, packed, first_row, basis, bilinear, needed, name):
    groups, _, out_width = bilinear.shape
    edges = basis.shape[0] * BLOCK
    folds = basis.shape[1] // groups
    slots = basis.shape[2] // BLOCK
    vmem = pl.BlockSpec(memory_space=pltpu.VMEM)
    return pl.pallas_call(
        functools.partial(
            gather_body, folds=folds, first_row=first_row, count=len(packed)
        ),
        out_shape=(
            jax.ShapeDtypeStruct((edges, out_width), BF16),
            jax.ShapeDtypeStruct((groups, edges, LANES), BF16),
        ),
        in_specs=[pl.BlockSpec(memory_space=pl.ANY)]
        + [vmem] * (2 + len(packed))
        + [pl.BlockSpec(memory_space=pl.ANY)] * len(needed),
        out_specs=(vmem, vmem),
        scratch_shapes=[
            pltpu.VMEM((len(packed) * edges, LANES), F32),
            pltpu.VMEM((basis.shape[2], LANES), F32),
            pltpu.VMEM((basis.shape[2], LANES), F32),
            pltpu.SemaphoreType.DMA((slots,)),
        ]
        + [pltpu.SMEM((edges,), jnp.int32)] * slots,
        compiler_params=pltpu.CompilerParams(vmem_limit_bytes=56 << 20),
        cost_estimate=pl.CostEstimate(flops=20 * 10**9, transcendentals=0, bytes_accessed=10**7),
        name=name,
    )(index, basis, bilinear, *packed, *needed)


def basis_body(rank_ref, trip_vals, trip_keep, quad_vals, quad_keep, trip_ref, quad_ref, trip_rows, quad_rows):
    del rank_ref
    tile_slots = LANES // BLOCK

    def build(vals_ref, keep_ref, out_ref, rows):
        count, slots, _ = vals_ref.shape
        vals = vals_ref[...].astype(F32) * keep_ref[...].astype(F32)[None]
        rows[...] = vals.reshape(count * slots, LANES)
        group = lax.broadcasted_iota(jnp.int32, (count, LANES), 1) // BLOCK
        for tile in range(slots // tile_slots):
            by_slot = [
                rows[pl.ds(tile * tile_slots + slot, count, stride=slots), :]
                for slot in range(tile_slots)
            ]
            for block in range(tile_slots):
                joined = None
                for slot, value in enumerate(by_slot):
                    shift = (slot - block) * BLOCK % LANES
                    turned = pltpu.roll(value, shift, 1) if shift else value
                    joined = turned if joined is None else jnp.where(group == slot, turned, joined)
                out_ref[block, :, tile * LANES : (tile + 1) * LANES] = joined.astype(BF16)

    build(trip_vals, trip_keep, trip_ref, trip_rows)
    build(quad_vals, quad_keep, quad_ref, quad_rows)


def slot_basis(rank, circular, trip_mask, spherical, quad_mask, edges):
    steps = edges // LANES
    blocks = LANES // BLOCK

    def source(array):
        shape = array.shape[:-1] + (LANES,)
        lead = (0,) * (len(shape) - 1)
        return pl.BlockSpec(shape, lambda step, rank_ref: lead + (rank_ref[0] * steps + step,))

    def target(count, slots):
        return pl.BlockSpec((blocks, count, slots * BLOCK), lambda step, rank_ref: (step, 0, 0))

    def shape_of(array):
        count, slots, _ = array.shape
        return jax.ShapeDtypeStruct((edges // BLOCK, count, slots * BLOCK), BF16)

    def rows_of(array):
        return pltpu.VMEM((array.shape[0] * array.shape[1], LANES), F32)

    return pl.pallas_call(
        basis_body,
        grid_spec=pltpu.PrefetchScalarGridSpec(
            num_scalar_prefetch=1,
            grid=(steps,),
            in_specs=[source(circular), source(trip_mask), source(spherical), source(quad_mask)],
            out_specs=[target(*circular.shape[:2]), target(*spherical.shape[:2])],
            scratch_shapes=[rows_of(circular), rows_of(spherical)],
        ),
        out_shape=(shape_of(circular), shape_of(spherical)),
        cost_estimate=pl.CostEstimate(flops=10 * 10**9, transcendentals=0, bytes_accessed=10**7),
        name="slot_basis",
    )(rank[None], circular, trip_mask, spherical, quad_mask)


TABLES = 4


def scatter_body(
    index_ref, same_ref, basis_ref, grad_ref, bilinear_ref, *refs, folds, owners, needed
):
    refs = refs[needed:]
    packed_refs = refs[:owners]
    slots = basis_ref.shape[2] // BLOCK
    part, rows_a, rows_b = refs[owners : owners + 3]
    tables = refs[owners + 3 : owners + 3 + TABLES]
    sems = refs[owners + 3 + TABLES]
    slot_refs = refs[-2 * slots : -slots]
    same_refs = refs[-slots:]
    copies = slot_copies(index_ref, slot_refs, sems, 0)
    copies += slot_copies(same_ref, same_refs, sems, slots)
    for copy in copies:
        copy.start()
    sides, piece_rows, _ = packed_refs[0].shape
    groups, edges, _ = part.shape
    basis_count = groups * folds
    width = LANES // folds
    chunk = 256
    table_rows = tables[0].shape[0]

    def clear(turn, _):
        start = pl.multiple_of(turn * chunk, chunk)
        for table in tables:
            table[pl.ds(start, chunk), :] = jnp.zeros((chunk, LANES), F32)
        return 0

    lax.fori_loop(0, table_rows // chunk, clear, 0)
    for group in range(groups):
        part[group] = outer(grad_ref[...], bilinear_ref[group]).astype(BF16)
    for copy in copies:
        copy.wait()
    diagonal = diagonal_mask(basis_count * BLOCK, slots * BLOCK)

    def spread(block, rows):
        weights = block_weights(basis_ref, block, diagonal)
        start = pl.multiple_of(block * BLOCK, BLOCK)
        values = part[:, pl.ds(start, BLOCK), :].reshape(groups * BLOCK, LANES)
        rows[...] = inner(weights, lane_groups(values, width))

    def store(block, rows):
        base = block * BLOCK
        for within in range(0, BLOCK, 2):
            edge = base + within
            next_edge = edge + 1
            for slot in range(slots):
                table = tables[slot % TABLES]
                at = slot * BLOCK + within
                place = slot_refs[slot][edge]
                next_place = slot_refs[slot][next_edge]
                same = same_refs[slot][edge]
                value = rows[pl.ds(at, 1), :]
                next_value = rows[pl.ds(at + 1, 1), :] + same * value
                total = table[pl.ds(place, 1), :] + value
                next_total = table[pl.ds(next_place, 1), :] + next_value
                table[pl.ds(place, 1), :] = total
                table[pl.ds(next_place, 1), :] = next_total

    blocks = edges // BLOCK
    spread(0, rows_a)

    def turn(pair, _):
        spread(2 * pair + 1, rows_b)
        store(2 * pair, rows_a)
        spread(jnp.minimum(2 * pair + 2, blocks - 1), rows_a)
        store(2 * pair + 1, rows_b)
        return 0

    lax.fori_loop(0, blocks // 2, turn, 0)
    step = min(piece_rows, 256 // folds)
    per_piece = piece_rows // step
    lane = lax.broadcasted_iota(jnp.int32, (step, LANES), 1) // width
    low = lane < folds // 2
    even = lane % 2 == 0

    def join(first, second):
        return jnp.where(low, first, second) + pltpu.roll(
            jnp.where(low, second, first), LANES // 2, 1
        )

    for owner, packed_ref in enumerate(packed_refs):

        def pack(turn, _, owner=owner, packed_ref=packed_ref):
            side = turn // per_piece
            piece = side * owners + owner
            start = pl.multiple_of((turn % per_piece) * step, step)
            sums = []
            for fold in range(folds):
                place = pl.multiple_of((piece * folds + fold) * piece_rows + start, step)
                total = tables[0][pl.ds(place, step), :]
                for table in tables[1:]:
                    total = total + table[pl.ds(place, step), :]
                sums.append(total)
            if folds == 2:
                joined = join(sums[0], sums[1])
            else:
                first, second = join(sums[0], sums[2]), join(sums[1], sums[3])
                joined = jnp.where(
                    even,
                    first + pltpu.roll(first, LANES - width, 1),
                    second + pltpu.roll(second, width, 1),
                )
            packed_ref[side, pl.ds(start, step), :] = joined.astype(BF16)
            return 0

        lax.fori_loop(0, sides * per_piece, pack, 0)


def branch_backward(index, basis, grad, bilinear, sides, owners, needed, name):
    edges = grad.shape[0]
    groups = bilinear.shape[0]
    folds = basis.shape[1] // groups
    vmem = pl.BlockSpec(memory_space=pltpu.VMEM)
    out = jax.ShapeDtypeStruct((sides, edges // folds, LANES), BF16)
    slots = basis.shape[2] // BLOCK
    same = (index == jnp.roll(index, -1)).astype(F32)
    whole = pl.BlockSpec(memory_space=pl.ANY)
    return pl.pallas_call(
        functools.partial(scatter_body, folds=folds, owners=owners, needed=len(needed)),
        out_shape=(out,) * owners,
        in_specs=[whole, whole, vmem, vmem, vmem]
        + [pl.BlockSpec(memory_space=pl.ANY)] * len(needed),
        out_specs=(vmem,) * owners,
        scratch_shapes=[
            pltpu.VMEM((groups, edges, LANES), BF16),
            pltpu.VMEM((basis.shape[2], LANES), F32),
            pltpu.VMEM((basis.shape[2], LANES), F32),
        ]
        + [pltpu.VMEM((sides * owners * edges, LANES), F32)] * TABLES
        + [pltpu.SemaphoreType.DMA((2 * slots,))]
        + [pltpu.SMEM((edges,), jnp.int32)] * slots
        + [pltpu.SMEM((edges,), F32)] * slots,
        compiler_params=pltpu.CompilerParams(vmem_limit_bytes=58 << 20),
        cost_estimate=pl.CostEstimate(flops=20 * 10**9, transcendentals=0, bytes_accessed=10**7),
        name=name,
    )(index, same, basis, grad, bilinear, *needed)


def large_parts(refs, block_ref, first, place):
    trip_up, quad_up, proj, first_layer, second_layer, to_atom = refs
    lanes = pl.ds(pl.multiple_of(place * LANES, LANES), LANES)
    for whole in (trip_up, quad_up, proj, first_layer):
        count = whole.shape[0]
        yield block_ref.at[pl.ds(first, count)], whole.at[:, lanes]
        first += count
    for whole in (second_layer, to_atom):
        for column in range(0, whole.shape[1], LANES):
            yield block_ref.at[pl.ds(first, LANES)], whole.at[lanes, pl.ds(column, LANES)]
            first += LANES


def unpack_body(rank_ref, *refs, owners):
    for owner in range(owners):
        for block, window in large_parts(refs[owners:], refs[owner], 0, rank_ref[0] ^ owner):
            window[...] = block[...]


def unpack_large(rank, blocks, shapes):
    vmem = pl.BlockSpec(memory_space=pltpu.VMEM)
    return pl.pallas_call(
        functools.partial(unpack_body, owners=len(blocks)),
        out_shape=tuple(jax.ShapeDtypeStruct(shape, BF16) for shape in shapes),
        in_specs=[pl.BlockSpec(memory_space=pltpu.SMEM)] + [vmem] * len(blocks),
        out_specs=(vmem,) * len(shapes),
        compiler_params=pltpu.CompilerParams(vmem_limit_bytes=32 << 20),
        name="unpack_large",
    )(rank[None], *blocks)


def pack_body(rank_ref, *refs, owners, count):
    large, trip_bil, quad_bil, atoms = refs[:6], refs[6], refs[7], refs[8]
    for owner, out_ref in enumerate(refs[count : count + owners]):
        place = rank_ref[0] ^ owner
        row = 0
        for block, window in large_parts(large, out_ref, 0, place):
            block[...] = window[...]
            row += block.shape[0]
        for whole in (trip_bil, quad_bil):
            groups, rows, out = whole.shape
            folds = LANES // out
            each = rows // folds // owners
            together = 16 // each
            for group in range(0, groups, together):
                pieces = [
                    jnp.concatenate(
                        [
                            whole[
                                member,
                                pl.ds(pl.multiple_of(fold * rows // folds + place * each, each), each),
                                :,
                            ]
                            for fold in range(folds)
                        ],
                        axis=1,
                    )
                    for member in range(group, group + together)
                ]
                out_ref[row : row + 16, :] = jnp.concatenate(pieces, axis=0).astype(BF16)
                row += 16
        for column in range(0, atoms.shape[1], LANES):
            out_ref[row : row + atoms.shape[0], :] = atoms[:, column : column + LANES]
            row += atoms.shape[0]


def pack_early(rank, members, owners, needed):
    total = sum(member.size for member in members[:-1]) // owners // LANES
    total += members[-1].size // LANES
    out = jax.ShapeDtypeStruct((total, LANES), BF16)
    vmem = pl.BlockSpec(memory_space=pltpu.VMEM)
    return pl.pallas_call(
        functools.partial(pack_body, owners=owners, count=len(members) + len(needed)),
        out_shape=(out,) * owners,
        in_specs=[pl.BlockSpec(memory_space=pltpu.SMEM)]
        + [vmem] * len(members)
        + [pl.BlockSpec(memory_space=pl.ANY)] * len(needed),
        out_specs=(vmem,) * owners,
        compiler_params=pltpu.CompilerParams(vmem_limit_bytes=32 << 20),
        cost_estimate=pl.CostEstimate(flops=20 * 10**9, transcendentals=0, bytes_accessed=10**7),
        name="pack_early",
    )(rank[None], *members, *needed)


def fold_lanes(rows):
    count, width = rows.shape
    folds = LANES // width
    each = count // folds
    return jnp.concatenate([rows[i * each : (i + 1) * each] for i in range(folds)], axis=1)


def unfold_lanes(packed, width):
    folds = LANES // width
    return jnp.concatenate([packed[:, i * width : (i + 1) * width] for i in range(folds)], axis=0)


def columns(array):
    return jnp.concatenate(
        [array[:, i : i + LANES] for i in range(0, array.shape[1], LANES)], axis=0
    )


def uncolumns(rows, width):
    each = rows.shape[0] * LANES // width
    return jnp.concatenate(
        [rows[i * each : (i + 1) * each] for i in range(width // LANES)], axis=1
    )


def edge_steps():
    steps = []
    size = 1
    while size < lax.axis_size("edge"):
        steps.append(size)
        size *= 2
    return steps


def halve(value, mask):
    bit = (lax.axis_index("edge") & mask) != 0
    half = value.shape[0] // 2
    keep = jnp.where(bit, value[half:], value[:half])
    send = jnp.where(bit, value[:half], value[half:])
    return keep, send


def join_halves(value, mask):
    bit = (lax.axis_index("edge") & mask) != 0
    got = edge_swap(value, mask)
    return jnp.concatenate([jnp.where(bit, got, value), jnp.where(bit, value, got)], axis=0)


def tree_sum(values):
    values = [value.astype(F32) for value in values]
    while len(values) > 1:
        values = [values[i] + values[i + 1] for i in range(0, len(values), 2)]
    return values[0]


def edge_total(value):
    for mask in edge_steps():
        value = (value.astype(F32) + edge_swap(value, mask).astype(F32)).astype(BF16)
    return value


def per_device(
    edge_emb,
    atom_emb,
    radial,
    circular,
    spherical,
    atom_tags,
    edge_source,
    edge_target,
    trip_source,
    trip_mask,
    quad_source,
    quad_mask,
    triplet_down_weight,
    trip_radial,
    triplet_bilinear_weight,
    trip_up,
    quad_down,
    quad_radial,
    quad_bilinear,
    quad_up,
    source_proj,
    target_proj,
    resid_first,
    resid_second,
    edge_to_atom,
    atom_update,
    output_first,
    output_second,
    tag_table,
    grad_edges,
    grad_atoms,
    grad_energy,
):
    edges_here = edge_emb.shape[0]
    atoms_here = atom_emb.shape[0]
    parts = lax.axis_size("chan")
    edge_parts = lax.axis_size("edge")
    rank = lax.axis_index("chan")
    edge_rank = lax.axis_index("edge")
    edges = edges_here // parts
    cols = edge_emb.shape[1]
    start = rank * edges

    def own(array, axis):
        return lax.dynamic_slice_in_dim(array, start, edges, axis)

    edge_blocks = edge_emb.reshape(parts, edges, cols)
    own_edges = jnp.concatenate(exchange(edge_blocks, rank), axis=1)

    trip_cols = triplet_down_weight.shape[1]
    quad_cols = quad_down.shape[1]
    trip_out = triplet_bilinear_weight.shape[2]
    quad_out = quad_bilinear.shape[2]
    down_own = jnp.concatenate([triplet_down_weight, quad_down], axis=1)
    small = jnp.concatenate(
        [
            columns(
                jnp.concatenate(
                    [down_own, jnp.concatenate([trip_radial, quad_radial], axis=1)], axis=0
                ).T
            ),
            fold_lanes(triplet_bilinear_weight.reshape(-1, trip_out)),
            fold_lanes(quad_bilinear.reshape(-1, quad_out)),
        ],
        axis=0,
    )
    small = reorder(gather_direct(small), rank)
    channels = parts * cols
    long = channels + radial.shape[1]
    small_rows = (trip_cols + quad_cols) * long // LANES
    trip_bil_rows = triplet_bilinear_weight.size // LANES
    downs = jnp.stack([uncolumns(block[:small_rows], long) for block in small])
    trip_both = downs[:, :trip_cols].reshape(parts * trip_cols, -1).T
    quad_both = downs[:, trip_cols:].reshape(parts * quad_cols, -1).T
    both = jnp.concatenate([trip_both, quad_both], axis=1)
    down_full, radial_full = both[:channels], both[channels:]
    trip_width = trip_both.shape[1]
    quad_width = quad_both.shape[1]
    trip_folds = LANES // trip_width
    quad_folds = LANES // quad_width

    def group_rows(blocks, shape, folds):
        whole = jnp.concatenate(
            [unfold_lanes(block, shape[2]).reshape(shape) for block in blocks], axis=1
        )
        count, width, out = whole.shape
        split = whole.reshape(folds, count // folds, width, out)
        return jnp.transpose(split, (1, 0, 2, 3)).reshape(count // folds, folds * width, out)

    trip_bil = group_rows(
        [block[small_rows : small_rows + trip_bil_rows] for block in small],
        triplet_bilinear_weight.shape,
        trip_folds,
    )
    quad_bil = group_rows(
        [block[small_rows + trip_bil_rows :] for block in small],
        quad_bilinear.shape,
        quad_folds,
    )

    own_radial = own(radial, 0)
    down_pre = matmul(own_edges, down_full)
    radial_pre = matmul(own_radial, radial_full)
    dense = (jax.nn.silu(down_pre) * radial_pre).astype(BF16)
    trip_piece = fold_lanes(dense[:, :trip_width])
    quad_piece = fold_lanes(dense[:, trip_width:])
    trip_rows = trip_piece.shape[0]
    wire = jnp.concatenate([trip_piece, quad_piece], axis=0)
    rank_now, wire, *members, atom_emb, grad_edges = gate(
        rank,
        wire,
        trip_up,
        quad_up,
        source_proj,
        target_proj,
        resid_first,
        resid_second,
        edge_to_atom,
        atom_emb,
        grad_edges,
    )
    before = edge_shift(wire, 1)
    later = edge_shift(wire, -1)
    own_across = chan_swap(wire, 2)
    own_beside = chan_swap(wire, 1)

    def spread(first, across):
        return [first, chan_swap(first, 1), across, chan_swap(across, 1)]

    before_across = chan_swap(before, 2)
    later_across = chan_swap(later, 2)
    wire_pieces = (
        spread(before, before_across)
        + [wire, own_beside, own_across, chan_swap(own_across, 1)]
        + spread(later, later_across)
    )

    def places(source):
        local = own(source, 1)
        within = local % edges_here
        owner = (within // edges) ^ rank
        return ((local // edges_here) * edges_here + owner * edges + within % edges).reshape(-1)

    trip_index = places(trip_source)
    quad_index = places(quad_source)
    trip_basis, quad_basis = slot_basis(
        rank_now, circular, trip_mask, spherical, quad_mask, edges
    )

    large = jnp.concatenate(members[:5] + [columns(members[5]), columns(members[6])], axis=0)
    tag_onehot = (atom_tags[:, None] == jnp.arange(TAGS)[None, :]).astype(F32)
    atom_full = atom_emb.astype(F32) + jnp.dot(
        tag_onehot, tag_table.astype(F32), precision=HIGHEST
    )
    atom_low = atom_full.astype(BF16)
    grad_blocks = grad_edges.reshape(parts, edges, cols)
    grad_sent = [pick(grad_blocks, rank ^ step) for step in range(parts)]
    quad_agg, quad_sum = branch_forward(
        quad_index,
        wire_pieces,
        trip_rows,
        quad_basis,
        quad_bil,
        [large, atom_low] + grad_sent,
        "quad_gather",
    )
    large_across, large_beside, atom_before, atom_later, quad_agg, *grad_sent = gate(
        chan_swap(large, 2),
        chan_swap(large, 1),
        edge_shift(atom_low, 1),
        edge_shift(atom_low, -1),
        quad_agg,
        *grad_sent,
    )

    trip_agg, trip_sum = branch_forward(
        trip_index,
        wire_pieces,
        0,
        trip_basis,
        trip_bil,
        [large_across, atom_before, atom_later] + grad_sent,
        "trip_gather",
    )
    grad_got = [grad_sent[0]] + [chan_swap(grad_sent[step], step) for step in range(1, parts)]
    large_diag, trip_agg, *grad_got = gate(chan_swap(large_across, 1), trip_agg, *grad_got)
    grad_two = jnp.concatenate(reorder(grad_got, rank), axis=1)
    sizes = [
        trip_up.shape[0],
        quad_up.shape[0],
        source_proj.shape[0],
        target_proj.shape[0],
        resid_first.shape[0],
        resid_second.size // LANES,
        edge_to_atom.size // LANES,
    ]

    def offsets_of(sizes):
        return [sum(sizes[:i]) for i in range(len(sizes) + 1)]

    offsets = offsets_of(sizes)

    trip_up_full, quad_up_full, proj_full, first_full, second_full, to_atom_full = unpack_large(
        rank,
        [large, large_beside, large_across, large_diag],
        [
            (trip_width, channels),
            (quad_width, channels),
            (2 * source_proj.shape[0], channels),
            (channels, channels),
            (channels, channels),
            (channels, edge_to_atom.shape[1]),
        ],
    )

    atom_wide = jnp.concatenate([atom_before, atom_low, atom_later], axis=0)
    atom_total = edge_parts * atoms_here
    source_local = (own(edge_source, 0) - (edge_rank - 1) * atoms_here) % atom_total
    target_local = own(edge_target, 0) - edge_rank * atoms_here
    source_hot = (source_local[:, None] == jnp.arange(3 * atoms_here)[None, :]).astype(BF16)
    target_hot = (target_local[:, None] == jnp.arange(atoms_here)[None, :]).astype(BF16)
    ends = jnp.concatenate(
        [
            matmul(source_hot, atom_wide).astype(BF16),
            matmul(target_hot, atom_low).astype(BF16),
        ],
        axis=1,
    )

    message = matmul(ends, proj_full)
    trip_out_pre = matmul(trip_agg, trip_up_full)
    quad_out_pre = matmul(quad_agg, quad_up_full)
    hidden_one = (
        own_edges.astype(F32)
        + jax.nn.silu(trip_out_pre)
        + jax.nn.silu(quad_out_pre)
        + jax.nn.silu(message)
    )
    hidden_low = hidden_one.astype(BF16)
    first_pre = matmul(hidden_low, first_full)
    first_low = jax.nn.silu(first_pre).astype(BF16)
    second_pre = matmul(first_low, second_full)
    edges_low = (hidden_one + jax.nn.silu(second_pre)).astype(BF16)
    edge_sums = inner(target_hot, edges_low)
    sums_high = edge_sums.astype(BF16)
    sums_rest = (edge_sums - sums_high.astype(F32)).astype(BF16)
    atom_sum = matmul(sums_high, to_atom_full) + matmul(sums_rest, to_atom_full)
    atom_sum = atom_sum + chan_swap(atom_sum, 1)
    atom_sum = atom_sum + chan_swap(atom_sum, 2)
    atom_sum, edges_low = gate(atom_sum, edges_low)

    atom_sum_low = atom_sum.astype(BF16)
    update_pre = matmul(atom_sum_low, atom_update)
    atoms_new = atom_full + jax.nn.silu(update_pre)
    atoms_low = atoms_new.astype(BF16)
    output_pre = matmul(atoms_low, output_first)
    output_low = jax.nn.silu(output_pre).astype(BF16)
    energy = matmul(output_low, output_second)
    output_second_grad = jnp.dot(grad_energy, output_low.astype(F32), precision=HIGHEST)
    output_grad = (
        grad_energy[:, None] * output_second.astype(F32)[None, :] * silu_grad(output_pre)
    ).astype(BF16)
    output_first_grad = inner(atoms_low, output_grad)
    atoms_new_grad = grad_atoms.astype(F32) + outer(output_grad, output_first)
    update_grad = (atoms_new_grad * silu_grad(update_pre)).astype(BF16)
    atom_update_grad = inner(atom_sum_low, update_grad)
    atom_sum_grad = outer(update_grad, atom_update).astype(BF16)

    edge_part_grad = matmul(target_hot, atom_sum_grad).astype(BF16)
    edge_to_atom_grad = inner(edges_low, edge_part_grad)
    two_grad = grad_two.astype(F32) + outer(edge_part_grad, to_atom_full)
    second_grad = (two_grad * silu_grad(second_pre)).astype(BF16)
    resid_second_grad = inner(first_low, second_grad)
    first_grad = (outer(second_grad, second_full) * silu_grad(first_pre)).astype(BF16)
    resid_first_grad = inner(hidden_low, first_grad)
    one_grad = two_grad + outer(first_grad, first_full)
    trip_out_grad = (one_grad * silu_grad(trip_out_pre)).astype(BF16)
    quad_out_grad = (one_grad * silu_grad(quad_out_pre)).astype(BF16)
    message_grad = (one_grad * silu_grad(message)).astype(BF16)
    trip_up_grad = inner(trip_agg, trip_out_grad)
    quad_up_grad = inner(quad_agg, quad_out_grad)
    trip_agg_grad = outer(trip_out_grad, trip_up_full).astype(BF16)
    quad_agg_grad = outer(quad_out_grad, quad_up_full).astype(BF16)
    proj_grad = inner(ends, message_grad)
    width = atom_low.shape[1]
    source_sums = inner(source_hot, message_grad).astype(BF16)
    target_sums = inner(target_hot, message_grad).astype(BF16)
    source_back = outer(source_sums, proj_full[:width])
    target_back = outer(target_sums, proj_full[width:])
    wide_atoms = source_back.reshape(3, atoms_here, width)
    wide_atoms = wide_atoms.at[1].add(target_back)

    def split(array, axis):
        return jnp.split(array, parts, axis=axis)

    def pack(members):
        packed = [
            jnp.concatenate([member[i] for member in members], axis=0).astype(BF16)
            for i in range(parts)
        ]
        return reorder(packed, rank)

    trip_bilinear_grad = jnp.einsum(
        "gej,eo->gjo", trip_sum, trip_agg_grad, preferred_element_type=F32
    )
    quad_bilinear_grad = jnp.einsum(
        "gej,eo->gjo", quad_sum, quad_agg_grad, preferred_element_type=F32
    )
    atom_rows = jnp.concatenate(
        [columns(atom_update_grad), columns(output_first_grad)], axis=0
    ).astype(BF16)
    atom_quarter = pick(atom_rows.reshape(parts, -1, LANES), rank)

    def send_back(array):
        blocks = jnp.stack([array[:, i * cols : (i + 1) * cols] for i in range(parts)])
        return [pick(blocks, rank ^ step) for step in range(parts)]

    def receive(sent):
        return [sent[0]] + [chan_swap(sent[step], step) for step in range(1, parts)]

    out_sent = send_back(edges_low)
    packed = pack_early(
        rank,
        [
            trip_up_grad.astype(BF16),
            quad_up_grad.astype(BF16),
            proj_grad.astype(BF16),
            resid_first_grad.astype(BF16),
            resid_second_grad.astype(BF16),
            edge_to_atom_grad.astype(BF16),
            trip_bilinear_grad,
            quad_bilinear_grad,
            wide_atoms.reshape(3 * atoms_here, width).astype(BF16),
        ],
        parts,
        out_sent,
    )
    *out_got, own_packed = gate(*receive(out_sent), packed[0])
    packed = [own_packed] + list(packed[1:])
    edges_out = jnp.concatenate(reorder(out_got, rank), axis=0)

    trip_tables = branch_backward(
        trip_index,
        trip_basis,
        trip_agg_grad,
        trip_bil,
        3,
        parts,
        [edges_out] + packed,
        "trip_scatter",
    )
    *packed_got, own_table = gate(*receive(packed), trip_tables[0])
    trip_tables = [own_table] + list(trip_tables[1:])
    mine = tree_sum(packed_got)
    early = packed[0].shape[0] - 3 * atoms_here * width // LANES
    wide_sum = uncolumns(mine[early:], width).reshape(3, atoms_here, width)
    early_rows = jnp.concatenate([mine[:early].astype(BF16), atom_quarter], axis=0)
    total_rows = early_rows.shape[0]
    early_rows = jnp.pad(early_rows, ((0, -total_rows % (16 * edge_parts)), (0, 0)))
    steps = edge_steps()
    keep, send = halve(early_rows, steps[0])

    quad_tables = branch_backward(
        quad_index,
        quad_basis,
        quad_agg_grad,
        quad_bil,
        3,
        parts,
        [wide_sum, send] + trip_tables,
        "quad_scatter",
    )
    quad_tables = list(quad_tables)
    early_got, *trip_got = gate(
        edge_swap(send, steps[0]), *receive(trip_tables), *quad_tables
    )
    trip_got, quad_tables = trip_got[:parts], trip_got[parts:]
    quad_got = receive(quad_tables)
    early_part = (keep.astype(F32) + early_got.astype(F32)).astype(BF16)
    for mask in steps[1:]:
        keep, send = halve(early_part, mask)
        early_part = (keep.astype(F32) + edge_swap(send, mask).astype(F32)).astype(BF16)

    table = jnp.concatenate(
        [
            tree_sum(trip_got),
            tree_sum(quad_got),
            jnp.stack([columns(wide_sum[side]) for side in range(3)]),
        ],
        axis=1,
    )
    branch_grad = (
        table[1]
        + edge_shift(table[0].astype(BF16), -1).astype(F32)
        + edge_shift(table[2].astype(BF16), 1).astype(F32)
    )
    wire_rows = wire.shape[0]
    atom_grad = atoms_new_grad + uncolumns(branch_grad[wire_rows:], width)
    branch_grad = branch_grad[:wire_rows]
    branch_grad = jnp.concatenate(
        [
            unfold_lanes(branch_grad[:trip_rows], trip_width),
            unfold_lanes(branch_grad[trip_rows:], quad_width),
        ],
        axis=1,
    )
    down_grad = (branch_grad * radial_pre * silu_grad(down_pre)).astype(BF16)
    radial_grad = (branch_grad * jax.nn.silu(down_pre)).astype(BF16)
    down_weight_grad = inner(own_edges, down_grad)
    radial_weight_grad = inner(own_radial, radial_grad)
    edge_grad = (one_grad + outer(down_grad, down_full)).astype(BF16)
    edge_grad = jnp.concatenate(reorder(receive(send_back(edge_grad)), rank), axis=0).astype(F32)

    tag_table_grad = jnp.dot(tag_onehot.T, atom_grad, precision=HIGHEST)
    tiny = columns(jnp.concatenate([output_second_grad[None], tag_table_grad], axis=0))

    small_grad = jnp.concatenate([down_weight_grad, radial_weight_grad], axis=0)
    late_sent = pack(
        [
            [
                columns(jnp.concatenate([trip_block, quad_block], axis=1).T)
                for trip_block, quad_block in zip(
                    split(small_grad[:, :trip_width], 1), split(small_grad[:, trip_width:], 1)
                )
            ]
        ]
    )
    late = tree_sum(receive(late_sent))
    late_rows = late.shape[0]
    late = edge_total(jnp.concatenate([late, tiny], axis=0).astype(BF16)).astype(F32)
    tiny = uncolumns(late[late_rows:], width)
    late = late[:late_rows]
    summed = early_part
    for mask in reversed(steps):
        summed = join_halves(summed, mask)
    summed = summed[:total_rows]
    atom_out = jnp.concatenate(reorder(gather_direct(summed[early:]), rank), axis=0).astype(F32)
    summed = summed[:early].astype(F32)
    sizes = sizes + [trip_bil_rows, quad_bilinear.size // LANES]
    offsets = offsets_of(sizes)
    parts_out = [summed[offsets[i] : offsets[i + 1]] for i in range(len(sizes))]
    small_out = uncolumns(late, long).T
    trip_bil_out, quad_bil_out = parts_out[7:]
    half = atom_out.shape[0] // 2
    return (
        edges_out,
        atoms_low,
        energy,
        edge_grad,
        atom_grad,
        small_out[:channels, :trip_cols],
        small_out[channels:, :trip_cols],
        unfold_lanes(trip_bil_out, trip_out).reshape(triplet_bilinear_weight.shape),
        parts_out[0],
        small_out[:channels, trip_cols:],
        small_out[channels:, trip_cols:],
        unfold_lanes(quad_bil_out, quad_out).reshape(quad_bilinear.shape),
        parts_out[1],
        parts_out[2],
        parts_out[3],
        parts_out[4],
        uncolumns(parts_out[5], resid_second.shape[1]),
        uncolumns(parts_out[6], edge_to_atom.shape[1]),
        uncolumns(atom_out[:half], atom_update.shape[1]),
        uncolumns(atom_out[half:], output_first.shape[1]),
        tiny[0],
        tiny[1:],
    )


def solution(mesh):
    return jax.shard_map(
        per_device,
        mesh=mesh,
        in_specs=(
            P("edge", "chan"),
            P("edge", None),
            P("edge", None),
            P(None, None, "edge"),
            P(None, None, "edge"),
            P("edge"),
            P("edge"),
            P("edge"),
            P(None, "edge"),
            P(None, "edge"),
            P(None, "edge"),
            P(None, "edge"),
            P(None, "chan"),
            P(None, "chan"),
            P(None, "chan", None),
            P(None, "chan"),
            P(None, "chan"),
            P(None, "chan"),
            P(None, "chan", None),
            P(None, "chan"),
            P(None, "chan"),
            P(None, "chan"),
            P(None, "chan"),
            P("chan", None),
            P("chan", None),
            P(),
            P(),
            P(),
            P(),
            P("edge", "chan"),
            P("edge", None),
            P("edge"),
        ),
        out_specs=(
            P("edge", "chan"),
            P("edge", None),
            P("edge"),
            P("edge", "chan"),
            P("edge", None),
            P(None, "chan"),
            P(None, "chan"),
            P(None, "chan", None),
            P(None, "chan"),
            P(None, "chan"),
            P(None, "chan"),
            P(None, "chan", None),
            P(None, "chan"),
            P(None, "chan"),
            P(None, "chan"),
            P(None, "chan"),
            P("chan", None),
            P("chan", None),
            P(),
            P(),
            P(),
            P(),
        ),
        check_vma=False,
    )
```

```python
import functools

import jax
import jax.numpy as jnp
from jax import lax
from jax.experimental import pallas as pl
from jax.experimental.pallas import tpu as pltpu
from jax.sharding import PartitionSpec as P

TAGS = 3
LANES = 128
BLOCK = 16
BF16 = jnp.bfloat16
F32 = jnp.float32
HIGHEST = lax.Precision.HIGHEST


def chan_swap(value, mask):
    count = lax.axis_size("chan")
    return lax.ppermute(value, "chan", [(i, i ^ mask) for i in range(count)])


def edge_swap(value, mask):
    count = lax.axis_size("edge")
    return lax.ppermute(value, "edge", [(i, i ^ mask) for i in range(count)])


def edge_shift(value, step):
    count = lax.axis_size("edge")
    return lax.ppermute(value, "edge", [(i, (i + step) % count) for i in range(count)])


def gate(*values):
    return list(lax.optimization_barrier(values))


def gather_direct(value):
    return [value] + [chan_swap(value, step) for step in (1, 2, 3)]


def pick(blocks, place):
    return lax.dynamic_index_in_dim(blocks, place, 0, keepdims=False)


def reorder(blocks, rank):
    low_bit = (rank & 1) == 1
    high_bit = (rank & 2) == 2
    first = [jnp.where(low_bit, blocks[i ^ 1], blocks[i]) for i in range(4)]
    return [jnp.where(high_bit, first[i ^ 2], first[i]) for i in range(4)]


def gather_chan(value):
    across = chan_swap(value, 2)
    beside = chan_swap(jnp.stack([value, across]), 1)
    return [value, beside[0], across, beside[1]]


def exchange(blocks, rank):
    got = [pick(blocks, rank)]
    for step in (1, 2, 3):
        got.append(chan_swap(pick(blocks, rank ^ step), step))
    return reorder(got, rank)


def silu_grad(pre_act):
    sigmoid = jax.nn.sigmoid(pre_act)
    return sigmoid * (1.0 + pre_act * (1.0 - sigmoid))


def matmul(first_op, second_op):
    return jnp.dot(first_op, second_op, preferred_element_type=F32)


def inner(first_op, second_op):
    return lax.dot_general(
        first_op, second_op, (((0,), (0,)), ((), ())), preferred_element_type=F32
    )


def outer(first_op, second_op):
    return lax.dot_general(
        first_op, second_op, (((1,), (1,)), ((), ())), preferred_element_type=F32
    )


def block_weights(basis_ref, block, diagonal):
    basis = basis_ref[block].astype(F32)
    count, width = basis.shape
    spread = jnp.broadcast_to(basis[:, None, :], (count, BLOCK, width))
    spread = spread.reshape(count * BLOCK, width)
    return jnp.where(diagonal, spread, 0.0).astype(BF16)


def diagonal_mask(rows, width):
    row = lax.broadcasted_iota(jnp.int32, (rows, width), 0) % BLOCK
    col = lax.broadcasted_iota(jnp.int32, (rows, width), 1) % BLOCK
    return row == col


def lane_groups(value, width):
    group = lax.broadcasted_iota(jnp.int32, value.shape, 1) // width
    zero = jnp.zeros_like(value)
    masked = [jnp.where(group == fold, value, zero) for fold in range(LANES // width)]
    return jnp.concatenate(masked, axis=0)


def slot_copies(whole_ref, slot_refs, sems, first):
    copies = []
    for slot, slot_ref in enumerate(slot_refs):
        size = slot_ref.shape[0]
        copies.append(
            pltpu.make_async_copy(
                whole_ref.at[pl.ds(slot * size, size)], slot_ref, sems.at[first + slot]
            )
        )
    return copies


def gather_body(index_ref, basis_ref, bilinear_ref, *refs, folds, first_row, count):
    packed_refs = refs[:count]
    slots = basis_ref.shape[2] // BLOCK
    agg_ref, sum_ref, table, rows_a, rows_b, sems = refs[-6 - slots : -slots]
    slot_refs = refs[-slots:]
    copies = slot_copies(index_ref, slot_refs, sems, 0)
    for copy in copies:
        copy.start()
    groups, edges, _ = sum_ref.shape
    basis_count = groups * folds
    width = LANES // folds
    piece_rows = edges // folds
    step = min(piece_rows, 64 // folds)
    lane = lax.broadcasted_iota(jnp.int32, (step, LANES), 1) // width

    def unpack(turn, _):
        start = pl.multiple_of(turn * step, step)
        for piece, packed_ref in enumerate(packed_refs):
            values = packed_ref[pl.ds(first_row + start, step), :].astype(F32)
            turned = [values] + [
                pltpu.roll(values, shift * width, 1) for shift in range(1, folds)
            ]
            for fold in range(folds):
                place = pl.multiple_of((piece * folds + fold) * piece_rows + start, step)
                spread = turned[(0 - fold) % folds]
                for group in range(1, folds):
                    spread = jnp.where(lane == group, turned[(group - fold) % folds], spread)
                table[pl.ds(place, step), :] = spread
        return 0

    lax.fori_loop(0, piece_rows // step, unpack, 0)
    for copy in copies:
        copy.wait()
    diagonal = diagonal_mask(basis_count * BLOCK, slots * BLOCK)

    def fetch(block, rows):
        base = block * BLOCK
        for within in range(BLOCK):
            edge = base + within
            for slot in range(slots):
                place = slot_refs[slot][edge]
                at = slot * BLOCK + within
                rows[pl.ds(at, 1), :] = table[pl.ds(place, 1), :]

    def combine(block, values):
        weights = block_weights(basis_ref, block, diagonal)
        each = groups * BLOCK
        joined = jnp.concatenate(
            [weights[fold * each : (fold + 1) * each] for fold in range(folds)], axis=1
        )
        got = matmul(joined, lane_groups(values, width)).astype(BF16)
        start = pl.multiple_of(block * BLOCK, BLOCK)
        sum_ref[:, pl.ds(start, BLOCK), :] = got.reshape(groups, BLOCK, LANES)

    blocks = edges // BLOCK
    fetch(0, rows_a)
    fetch(1, rows_b)

    def turn(pair, _):
        values_a = rows_a[...].astype(BF16)
        values_b = rows_b[...].astype(BF16)
        fetch(jnp.minimum(2 * pair + 2, blocks - 1), rows_a)
        fetch(jnp.minimum(2 * pair + 3, blocks - 1), rows_b)
        combine(2 * pair, values_a)
        combine(2 * pair + 1, values_b)
        return 0

    lax.fori_loop(0, blocks // 2, turn, 0)
    total = matmul(sum_ref[0], bilinear_ref[0])
    for group in range(1, groups):
        total = total + matmul(sum_ref[group], bilinear_ref[group])
    agg_ref[...] = total.astype(BF16)


def branch_forward(index, packed, first_row, basis, bilinear, needed, name):
    groups, _, out_width = bilinear.shape
    edges = basis.shape[0] * BLOCK
    folds = basis.shape[1] // groups
    slots = basis.shape[2] // BLOCK
    vmem = pl.BlockSpec(memory_space=pltpu.VMEM)
    return pl.pallas_call(
        functools.partial(
            gather_body, folds=folds, first_row=first_row, count=len(packed)
        ),
        out_shape=(
            jax.ShapeDtypeStruct((edges, out_width), BF16),
            jax.ShapeDtypeStruct((groups, edges, LANES), BF16),
        ),
        in_specs=[pl.BlockSpec(memory_space=pl.ANY)]
        + [vmem] * (2 + len(packed))
        + [pl.BlockSpec(memory_space=pl.ANY)] * len(needed),
        out_specs=(vmem, vmem),
        scratch_shapes=[
            pltpu.VMEM((len(packed) * edges, LANES), F32),
            pltpu.VMEM((basis.shape[2], LANES), F32),
            pltpu.VMEM((basis.shape[2], LANES), F32),
            pltpu.SemaphoreType.DMA((slots,)),
        ]
        + [pltpu.SMEM((edges,), jnp.int32)] * slots,
        compiler_params=pltpu.CompilerParams(vmem_limit_bytes=56 << 20),
        cost_estimate=pl.CostEstimate(flops=20 * 10**9, transcendentals=0, bytes_accessed=10**7),
        name=name,
    )(index, basis, bilinear, *packed, *needed)


def basis_body(rank_ref, trip_vals, trip_keep, quad_vals, quad_keep, trip_ref, quad_ref, trip_rows, quad_rows):
    del rank_ref
    tile_slots = LANES // BLOCK

    def build(vals_ref, keep_ref, out_ref, rows):
        count, slots, _ = vals_ref.shape
        vals = vals_ref[...].astype(F32) * keep_ref[...].astype(F32)[None]
        rows[...] = vals.reshape(count * slots, LANES)
        group = lax.broadcasted_iota(jnp.int32, (count, LANES), 1) // BLOCK
        for tile in range(slots // tile_slots):
            by_slot = [
                rows[pl.ds(tile * tile_slots + slot, count, stride=slots), :]
                for slot in range(tile_slots)
            ]
            for block in range(tile_slots):
                joined = None
                for slot, value in enumerate(by_slot):
                    shift = (slot - block) * BLOCK % LANES
                    turned = pltpu.roll(value, shift, 1) if shift else value
                    joined = turned if joined is None else jnp.where(group == slot, turned, joined)
                out_ref[block, :, tile * LANES : (tile + 1) * LANES] = joined.astype(BF16)

    build(trip_vals, trip_keep, trip_ref, trip_rows)
    build(quad_vals, quad_keep, quad_ref, quad_rows)


def slot_basis(rank, circular, trip_mask, spherical, quad_mask, edges):
    steps = edges // LANES
    blocks = LANES // BLOCK

    def source(array):
        shape = array.shape[:-1] + (LANES,)
        lead = (0,) * (len(shape) - 1)
        return pl.BlockSpec(shape, lambda step, rank_ref: lead + (rank_ref[0] * steps + step,))

    def target(count, slots):
        return pl.BlockSpec((blocks, count, slots * BLOCK), lambda step, rank_ref: (step, 0, 0))

    def shape_of(array):
        count, slots, _ = array.shape
        return jax.ShapeDtypeStruct((edges // BLOCK, count, slots * BLOCK), BF16)

    def rows_of(array):
        return pltpu.VMEM((array.shape[0] * array.shape[1], LANES), F32)

    return pl.pallas_call(
        basis_body,
        grid_spec=pltpu.PrefetchScalarGridSpec(
            num_scalar_prefetch=1,
            grid=(steps,),
            in_specs=[source(circular), source(trip_mask), source(spherical), source(quad_mask)],
            out_specs=[target(*circular.shape[:2]), target(*spherical.shape[:2])],
            scratch_shapes=[rows_of(circular), rows_of(spherical)],
        ),
        out_shape=(shape_of(circular), shape_of(spherical)),
        cost_estimate=pl.CostEstimate(flops=10 * 10**9, transcendentals=0, bytes_accessed=10**7),
        name="slot_basis",
    )(rank[None], circular, trip_mask, spherical, quad_mask)


TABLES = 4


def scatter_body(
    index_ref, same_ref, basis_ref, grad_ref, bilinear_ref, *refs, folds, owners, needed
):
    refs = refs[needed:]
    packed_refs = refs[:owners]
    slots = basis_ref.shape[2] // BLOCK
    part, rows_a, rows_b = refs[owners : owners + 3]
    tables = refs[owners + 3 : owners + 3 + TABLES]
    sems = refs[owners + 3 + TABLES]
    slot_refs = refs[-2 * slots : -slots]
    same_refs = refs[-slots:]
    copies = slot_copies(index_ref, slot_refs, sems, 0)
    copies += slot_copies(same_ref, same_refs, sems, slots)
    for copy in copies:
        copy.start()
    sides, piece_rows, _ = packed_refs[0].shape
    groups, edges, _ = part.shape
    basis_count = groups * folds
    width = LANES // folds
    chunk = 256
    table_rows = tables[0].shape[0]

    def clear(turn, _):
        start = pl.multiple_of(turn * chunk, chunk)
        for table in tables:
            table[pl.ds(start, chunk), :] = jnp.zeros((chunk, LANES), F32)
        return 0

    lax.fori_loop(0, table_rows // chunk, clear, 0)
    for group in range(groups):
        part[group] = outer(grad_ref[...], bilinear_ref[group]).astype(BF16)
    for copy in copies:
        copy.wait()
    diagonal = diagonal_mask(basis_count * BLOCK, slots * BLOCK)

    def spread(block, rows):
        weights = block_weights(basis_ref, block, diagonal)
        start = pl.multiple_of(block * BLOCK, BLOCK)
        values = part[:, pl.ds(start, BLOCK), :].reshape(groups * BLOCK, LANES)
        rows[...] = inner(weights, lane_groups(values, width))

    def store(block, rows):
        base = block * BLOCK
        for within in range(0, BLOCK, 2):
            edge = base + within
            next_edge = edge + 1
            for slot in range(slots):
                table = tables[slot % TABLES]
                at = slot * BLOCK + within
                place = slot_refs[slot][edge]
                next_place = slot_refs[slot][next_edge]
                same = same_refs[slot][edge]
                value = rows[pl.ds(at, 1), :]
                next_value = rows[pl.ds(at + 1, 1), :] + same * value
                total = table[pl.ds(place, 1), :] + value
                next_total = table[pl.ds(next_place, 1), :] + next_value
                table[pl.ds(place, 1), :] = total
                table[pl.ds(next_place, 1), :] = next_total

    blocks = edges // BLOCK
    spread(0, rows_a)

    def turn(pair, _):
        spread(2 * pair + 1, rows_b)
        store(2 * pair, rows_a)
        spread(jnp.minimum(2 * pair + 2, blocks - 1), rows_a)
        store(2 * pair + 1, rows_b)
        return 0

    lax.fori_loop(0, blocks // 2, turn, 0)
    step = min(piece_rows, 64 // folds)
    per_piece = piece_rows // step
    lane = lax.broadcasted_iota(jnp.int32, (step, LANES), 1) // width
    low = lane < folds // 2
    even = lane % 2 == 0

    def join(first, second):
        return jnp.where(low, first, second) + pltpu.roll(
            jnp.where(low, second, first), LANES // 2, 1
        )

    def pack(turn, _):
        side = turn // per_piece
        start = pl.multiple_of((turn % per_piece) * step, step)
        for owner, packed_ref in enumerate(packed_refs):
            piece = side * owners + owner
            sums = []
            for fold in range(folds):
                place = pl.multiple_of((piece * folds + fold) * piece_rows + start, step)
                total = tables[0][pl.ds(place, step), :]
                for table in tables[1:]:
                    total = total + table[pl.ds(place, step), :]
                sums.append(total)
            if folds == 2:
                joined = join(sums[0], sums[1])
            else:
                first, second = join(sums[0], sums[2]), join(sums[1], sums[3])
                joined = jnp.where(
                    even,
                    first + pltpu.roll(first, LANES - width, 1),
                    second + pltpu.roll(second, width, 1),
                )
            packed_ref[side, pl.ds(start, step), :] = joined.astype(BF16)
        return 0

    lax.fori_loop(0, sides * per_piece, pack, 0)


def branch_backward(index, basis, grad, bilinear, sides, owners, needed, name):
    edges = grad.shape[0]
    groups = bilinear.shape[0]
    folds = basis.shape[1] // groups
    vmem = pl.BlockSpec(memory_space=pltpu.VMEM)
    out = jax.ShapeDtypeStruct((sides, edges // folds, LANES), BF16)
    slots = basis.shape[2] // BLOCK
    same = (index == jnp.roll(index, -1)).astype(F32)
    whole = pl.BlockSpec(memory_space=pl.ANY)
    return pl.pallas_call(
        functools.partial(scatter_body, folds=folds, owners=owners, needed=len(needed)),
        out_shape=(out,) * owners,
        in_specs=[whole, whole, vmem, vmem, vmem]
        + [pl.BlockSpec(memory_space=pl.ANY)] * len(needed),
        out_specs=(vmem,) * owners,
        scratch_shapes=[
            pltpu.VMEM((groups, edges, LANES), BF16),
            pltpu.VMEM((basis.shape[2], LANES), F32),
            pltpu.VMEM((basis.shape[2], LANES), F32),
        ]
        + [pltpu.VMEM((sides * owners * edges, LANES), F32)] * TABLES
        + [pltpu.SemaphoreType.DMA((2 * slots,))]
        + [pltpu.SMEM((edges,), jnp.int32)] * slots
        + [pltpu.SMEM((edges,), F32)] * slots,
        compiler_params=pltpu.CompilerParams(vmem_limit_bytes=58 << 20),
        cost_estimate=pl.CostEstimate(flops=20 * 10**9, transcendentals=0, bytes_accessed=10**7),
        name=name,
    )(index, same, basis, grad, bilinear, *needed)


def large_parts(refs, block_ref, first, place):
    trip_up, quad_up, proj, first_layer, second_layer, to_atom = refs
    lanes = pl.ds(pl.multiple_of(place * LANES, LANES), LANES)
    for whole in (trip_up, quad_up, proj, first_layer):
        count = whole.shape[0]
        yield block_ref.at[pl.ds(first, count)], whole.at[:, lanes]
        first += count
    for whole in (second_layer, to_atom):
        for column in range(0, whole.shape[1], LANES):
            yield block_ref.at[pl.ds(first, LANES)], whole.at[lanes, pl.ds(column, LANES)]
            first += LANES


def unpack_body(rank_ref, *refs, owners):
    for owner in range(owners):
        for block, window in large_parts(refs[owners:], refs[owner], 0, rank_ref[0] ^ owner):
            window[...] = block[...]


def unpack_large(rank, blocks, shapes):
    vmem = pl.BlockSpec(memory_space=pltpu.VMEM)
    return pl.pallas_call(
        functools.partial(unpack_body, owners=len(blocks)),
        out_shape=tuple(jax.ShapeDtypeStruct(shape, BF16) for shape in shapes),
        in_specs=[pl.BlockSpec(memory_space=pltpu.SMEM)] + [vmem] * len(blocks),
        out_specs=(vmem,) * len(shapes),
        compiler_params=pltpu.CompilerParams(vmem_limit_bytes=32 << 20),
        name="unpack_large",
    )(rank[None], *blocks)


def pack_body(rank_ref, *refs, owners, count):
    large, trip_bil, quad_bil, atoms = refs[:6], refs[6], refs[7], refs[8]
    for owner, out_ref in enumerate(refs[count : count + owners]):
        place = rank_ref[0] ^ owner
        row = 0
        for block, window in large_parts(large, out_ref, 0, place):
            block[...] = window[...]
            row += block.shape[0]
        for whole in (trip_bil, quad_bil):
            groups, rows, out = whole.shape
            folds = LANES // out
            each = rows // folds // owners
            together = 16 // each
            for group in range(0, groups, together):
                pieces = [
                    jnp.concatenate(
                        [
                            whole[
                                member,
                                pl.ds(pl.multiple_of(fold * rows // folds + place * each, each), each),
                                :,
                            ]
                            for fold in range(folds)
                        ],
                        axis=1,
                    )
                    for member in range(group, group + together)
                ]
                out_ref[row : row + 16, :] = jnp.concatenate(pieces, axis=0).astype(BF16)
                row += 16
        for column in range(0, atoms.shape[1], LANES):
            out_ref[row : row + atoms.shape[0], :] = atoms[:, column : column + LANES]
            row += atoms.shape[0]


def pack_early(rank, members, owners, needed):
    total = sum(member.size for member in members[:-1]) // owners // LANES
    total += members[-1].size // LANES
    out = jax.ShapeDtypeStruct((total, LANES), BF16)
    vmem = pl.BlockSpec(memory_space=pltpu.VMEM)
    return pl.pallas_call(
        functools.partial(pack_body, owners=owners, count=len(members) + len(needed)),
        out_shape=(out,) * owners,
        in_specs=[pl.BlockSpec(memory_space=pltpu.SMEM)]
        + [vmem] * len(members)
        + [pl.BlockSpec(memory_space=pl.ANY)] * len(needed),
        out_specs=(vmem,) * owners,
        compiler_params=pltpu.CompilerParams(vmem_limit_bytes=32 << 20),
        cost_estimate=pl.CostEstimate(flops=20 * 10**9, transcendentals=0, bytes_accessed=10**7),
        name="pack_early",
    )(rank[None], *members, *needed)


def fold_lanes(rows):
    count, width = rows.shape
    folds = LANES // width
    each = count // folds
    return jnp.concatenate([rows[i * each : (i + 1) * each] for i in range(folds)], axis=1)


def unfold_lanes(packed, width):
    folds = LANES // width
    return jnp.concatenate([packed[:, i * width : (i + 1) * width] for i in range(folds)], axis=0)


def columns(array):
    return jnp.concatenate(
        [array[:, i : i + LANES] for i in range(0, array.shape[1], LANES)], axis=0
    )


def uncolumns(rows, width):
    each = rows.shape[0] * LANES // width
    return jnp.concatenate(
        [rows[i * each : (i + 1) * each] for i in range(width // LANES)], axis=1
    )


def edge_steps():
    steps = []
    size = 1
    while size < lax.axis_size("edge"):
        steps.append(size)
        size *= 2
    return steps


def halve(value, mask):
    bit = (lax.axis_index("edge") & mask) != 0
    half = value.shape[0] // 2
    keep = jnp.where(bit, value[half:], value[:half])
    send = jnp.where(bit, value[:half], value[half:])
    return keep, send


def join_halves(value, mask):
    bit = (lax.axis_index("edge") & mask) != 0
    got = edge_swap(value, mask)
    return jnp.concatenate([jnp.where(bit, got, value), jnp.where(bit, value, got)], axis=0)


def tree_sum(values):
    values = [value.astype(F32) for value in values]
    while len(values) > 1:
        values = [values[i] + values[i + 1] for i in range(0, len(values), 2)]
    return values[0]


def edge_total(value):
    for mask in edge_steps():
        value = (value.astype(F32) + edge_swap(value, mask).astype(F32)).astype(BF16)
    return value


def per_device(
    edge_emb,
    atom_emb,
    radial,
    circular,
    spherical,
    atom_tags,
    edge_source,
    edge_target,
    trip_source,
    trip_mask,
    quad_source,
    quad_mask,
    triplet_down_weight,
    trip_radial,
    triplet_bilinear_weight,
    trip_up,
    quad_down,
    quad_radial,
    quad_bilinear,
    quad_up,
    source_proj,
    target_proj,
    resid_first,
    resid_second,
    edge_to_atom,
    atom_update,
    output_first,
    output_second,
    tag_table,
    grad_edges,
    grad_atoms,
    grad_energy,
):
    edges_here = edge_emb.shape[0]
    atoms_here = atom_emb.shape[0]
    parts = lax.axis_size("chan")
    edge_parts = lax.axis_size("edge")
    rank = lax.axis_index("chan")
    edge_rank = lax.axis_index("edge")
    edges = edges_here // parts
    cols = edge_emb.shape[1]
    start = rank * edges

    def own(array, axis):
        return lax.dynamic_slice_in_dim(array, start, edges, axis)

    edge_blocks = edge_emb.reshape(parts, edges, cols)
    edge_sent = [pick(edge_blocks, rank ^ step) for step in range(parts)]
    *edge_sent, triplet_down_weight, trip_radial, triplet_bilinear_weight, quad_bilinear = gate(
        *edge_sent, triplet_down_weight, trip_radial, triplet_bilinear_weight, quad_bilinear
    )
    edge_got = [edge_sent[0]] + [chan_swap(edge_sent[step], step) for step in range(1, parts)]
    own_edges = jnp.concatenate(reorder(edge_got, rank), axis=1)

    trip_cols = triplet_down_weight.shape[1]
    quad_cols = quad_down.shape[1]
    trip_out = triplet_bilinear_weight.shape[2]
    quad_out = quad_bilinear.shape[2]
    down_own = jnp.concatenate([triplet_down_weight, quad_down], axis=1)
    small = jnp.concatenate(
        [
            columns(
                jnp.concatenate(
                    [down_own, jnp.concatenate([trip_radial, quad_radial], axis=1)], axis=0
                ).T
            ),
            fold_lanes(triplet_bilinear_weight.reshape(-1, trip_out)),
            fold_lanes(quad_bilinear.reshape(-1, quad_out)),
        ],
        axis=0,
    )
    small = reorder(gather_direct(small), rank)
    channels = parts * cols
    long = channels + radial.shape[1]
    small_rows = (trip_cols + quad_cols) * long // LANES
    trip_bil_rows = triplet_bilinear_weight.size // LANES
    downs = jnp.stack([uncolumns(block[:small_rows], long) for block in small])
    trip_both = downs[:, :trip_cols].reshape(parts * trip_cols, -1).T
    quad_both = downs[:, trip_cols:].reshape(parts * quad_cols, -1).T
    both = jnp.concatenate([trip_both, quad_both], axis=1)
    down_full, radial_full = both[:channels], both[channels:]
    trip_width = trip_both.shape[1]
    quad_width = quad_both.shape[1]
    trip_folds = LANES // trip_width
    quad_folds = LANES // quad_width

    def group_rows(blocks, shape, folds):
        whole = jnp.concatenate(
            [unfold_lanes(block, shape[2]).reshape(shape) for block in blocks], axis=1
        )
        count, width, out = whole.shape
        split = whole.reshape(folds, count // folds, width, out)
        return jnp.transpose(split, (1, 0, 2, 3)).reshape(count // folds, folds * width, out)

    trip_bil = group_rows(
        [block[small_rows : small_rows + trip_bil_rows] for block in small],
        triplet_bilinear_weight.shape,
        trip_folds,
    )
    quad_bil = group_rows(
        [block[small_rows + trip_bil_rows :] for block in small],
        quad_bilinear.shape,
        quad_folds,
    )

    own_radial = own(radial, 0)
    down_pre = matmul(own_edges, down_full)
    radial_pre = matmul(own_radial, radial_full)
    dense = (jax.nn.silu(down_pre) * radial_pre).astype(BF16)
    trip_piece = fold_lanes(dense[:, :trip_width])
    quad_piece = fold_lanes(dense[:, trip_width:])
    trip_rows = trip_piece.shape[0]
    wire = jnp.concatenate([trip_piece, quad_piece], axis=0)
    rank_now, wire, *members, atom_emb, grad_edges = gate(
        rank,
        wire,
        trip_up,
        quad_up,
        source_proj,
        target_proj,
        resid_first,
        resid_second,
        edge_to_atom,
        atom_emb,
        grad_edges,
    )
    before = edge_shift(wire, 1)
    later = edge_shift(wire, -1)
    own_across = chan_swap(wire, 2)
    own_beside = chan_swap(wire, 1)

    def spread(first, across):
        return [first, chan_swap(first, 1), across, chan_swap(across, 1)]

    before_across = chan_swap(before, 2)
    later_across = chan_swap(later, 2)
    wire_pieces = (
        spread(before, before_across)
        + [wire, own_beside, own_across, chan_swap(own_across, 1)]
        + spread(later, later_across)
    )

    def places(source):
        local = own(source, 1)
        within = local % edges_here
        owner = (within // edges) ^ rank
        return ((local // edges_here) * edges_here + owner * edges + within % edges).reshape(-1)

    trip_index = places(trip_source)
    quad_index = places(quad_source)
    trip_basis, quad_basis = slot_basis(
        rank_now, circular, trip_mask, spherical, quad_mask, edges
    )

    large = jnp.concatenate(members[:5] + [columns(members[5]), columns(members[6])], axis=0)
    tag_onehot = (atom_tags[:, None] == jnp.arange(TAGS)[None, :]).astype(F32)
    atom_full = atom_emb.astype(F32) + jnp.dot(
        tag_onehot, tag_table.astype(F32), precision=HIGHEST
    )
    atom_low = atom_full.astype(BF16)
    grad_blocks = grad_edges.reshape(parts, edges, cols)
    grad_sent = [pick(grad_blocks, rank ^ step) for step in range(parts)]
    quad_agg, quad_sum = branch_forward(
        quad_index,
        wire_pieces,
        trip_rows,
        quad_basis,
        quad_bil,
        [large, atom_low] + grad_sent,
        "quad_gather",
    )
    large_across, large_beside, atom_before, atom_later, quad_agg, *grad_sent = gate(
        chan_swap(large, 2),
        chan_swap(large, 1),
        edge_shift(atom_low, 1),
        edge_shift(atom_low, -1),
        quad_agg,
        *grad_sent,
    )

    trip_agg, trip_sum = branch_forward(
        trip_index,
        wire_pieces,
        0,
        trip_basis,
        trip_bil,
        [large_across, atom_before, atom_later] + grad_sent,
        "trip_gather",
    )
    grad_got = [grad_sent[0]] + [chan_swap(grad_sent[step], step) for step in range(1, parts)]
    large_diag, trip_agg, *grad_got = gate(chan_swap(large_across, 1), trip_agg, *grad_got)
    grad_two = jnp.concatenate(reorder(grad_got, rank), axis=1)
    sizes = [
        trip_up.shape[0],
        quad_up.shape[0],
        source_proj.shape[0],
        target_proj.shape[0],
        resid_first.shape[0],
        resid_second.size // LANES,
        edge_to_atom.size // LANES,
    ]

    def offsets_of(sizes):
        return [sum(sizes[:i]) for i in range(len(sizes) + 1)]

    offsets = offsets_of(sizes)

    trip_up_full, quad_up_full, proj_full, first_full, second_full, to_atom_full = unpack_large(
        rank,
        [large, large_beside, large_across, large_diag],
        [
            (trip_width, channels),
            (quad_width, channels),
            (2 * source_proj.shape[0], channels),
            (channels, channels),
            (channels, channels),
            (channels, edge_to_atom.shape[1]),
        ],
    )

    atom_wide = jnp.concatenate([atom_before, atom_low, atom_later], axis=0)
    atom_total = edge_parts * atoms_here
    source_local = (own(edge_source, 0) - (edge_rank - 1) * atoms_here) % atom_total
    target_local = own(edge_target, 0) - edge_rank * atoms_here
    source_hot = (source_local[:, None] == jnp.arange(3 * atoms_here)[None, :]).astype(BF16)
    target_hot = (target_local[:, None] == jnp.arange(atoms_here)[None, :]).astype(BF16)
    ends = jnp.concatenate(
        [
            matmul(source_hot, atom_wide).astype(BF16),
            matmul(target_hot, atom_low).astype(BF16),
        ],
        axis=1,
    )

    message = matmul(ends, proj_full)
    trip_out_pre = matmul(trip_agg, trip_up_full)
    quad_out_pre = matmul(quad_agg, quad_up_full)
    hidden_one = (
        own_edges.astype(F32)
        + jax.nn.silu(trip_out_pre)
        + jax.nn.silu(quad_out_pre)
        + jax.nn.silu(message)
    )
    hidden_low = hidden_one.astype(BF16)
    first_pre = matmul(hidden_low, first_full)
    first_low = jax.nn.silu(first_pre).astype(BF16)
    second_pre = matmul(first_low, second_full)
    edges_low = (hidden_one + jax.nn.silu(second_pre)).astype(BF16)
    edge_sums = inner(target_hot, edges_low)
    sums_high = edge_sums.astype(BF16)
    sums_rest = (edge_sums - sums_high.astype(F32)).astype(BF16)
    atom_sum = matmul(sums_high, to_atom_full) + matmul(sums_rest, to_atom_full)
    atom_sum = atom_sum + chan_swap(atom_sum, 1)
    atom_sum = atom_sum + chan_swap(atom_sum, 2)
    atom_sum, edges_low = gate(atom_sum, edges_low)

    atom_sum_low = atom_sum.astype(BF16)
    update_pre = matmul(atom_sum_low, atom_update)
    atoms_new = atom_full + jax.nn.silu(update_pre)
    atoms_low = atoms_new.astype(BF16)
    output_pre = matmul(atoms_low, output_first)
    output_low = jax.nn.silu(output_pre).astype(BF16)
    energy = matmul(output_low, output_second)
    output_second_grad = jnp.dot(grad_energy, output_low.astype(F32), precision=HIGHEST)
    output_grad = (
        grad_energy[:, None] * output_second.astype(F32)[None, :] * silu_grad(output_pre)
    ).astype(BF16)
    output_first_grad = inner(atoms_low, output_grad)
    atoms_new_grad = grad_atoms.astype(F32) + outer(output_grad, output_first)
    update_grad = (atoms_new_grad * silu_grad(update_pre)).astype(BF16)
    atom_update_grad = inner(atom_sum_low, update_grad)
    atom_sum_grad = outer(update_grad, atom_update).astype(BF16)

    edge_part_grad = matmul(target_hot, atom_sum_grad).astype(BF16)
    edge_to_atom_grad = inner(edges_low, edge_part_grad)
    two_grad = grad_two.astype(F32) + outer(edge_part_grad, to_atom_full)
    second_grad = (two_grad * silu_grad(second_pre)).astype(BF16)
    resid_second_grad = inner(first_low, second_grad)
    first_grad = (outer(second_grad, second_full) * silu_grad(first_pre)).astype(BF16)
    resid_first_grad = inner(hidden_low, first_grad)
    one_grad = two_grad + outer(first_grad, first_full)
    trip_out_grad = (one_grad * silu_grad(trip_out_pre)).astype(BF16)
    quad_out_grad = (one_grad * silu_grad(quad_out_pre)).astype(BF16)
    message_grad = (one_grad * silu_grad(message)).astype(BF16)
    trip_up_grad = inner(trip_agg, trip_out_grad)
    quad_up_grad = inner(quad_agg, quad_out_grad)
    trip_agg_grad = outer(trip_out_grad, trip_up_full).astype(BF16)
    quad_agg_grad = outer(quad_out_grad, quad_up_full).astype(BF16)
    proj_grad = inner(ends, message_grad)
    width = atom_low.shape[1]
    source_sums = inner(source_hot, message_grad).astype(BF16)
    target_sums = inner(target_hot, message_grad).astype(BF16)
    source_back = outer(source_sums, proj_full[:width])
    target_back = outer(target_sums, proj_full[width:])
    wide_atoms = source_back.reshape(3, atoms_here, width)
    wide_atoms = wide_atoms.at[1].add(target_back)

    def split(array, axis):
        return jnp.split(array, parts, axis=axis)

    def pack(members):
        packed = [
            jnp.concatenate([member[i] for member in members], axis=0).astype(BF16)
            for i in range(parts)
        ]
        return reorder(packed, rank)

    trip_bilinear_grad = jnp.einsum(
        "gej,eo->gjo", trip_sum, trip_agg_grad, preferred_element_type=F32
    )
    quad_bilinear_grad = jnp.einsum(
        "gej,eo->gjo", quad_sum, quad_agg_grad, preferred_element_type=F32
    )
    atom_rows = jnp.concatenate(
        [columns(atom_update_grad), columns(output_first_grad)], axis=0
    ).astype(BF16)
    atom_quarter = pick(atom_rows.reshape(parts, -1, LANES), rank)

    def send_back(array):
        blocks = jnp.stack([array[:, i * cols : (i + 1) * cols] for i in range(parts)])
        return [pick(blocks, rank ^ step) for step in range(parts)]

    def receive(sent):
        return [sent[0]] + [chan_swap(sent[step], step) for step in range(1, parts)]

    out_sent = send_back(edges_low)
    packed = pack_early(
        rank,
        [
            trip_up_grad.astype(BF16),
            quad_up_grad.astype(BF16),
            proj_grad.astype(BF16),
            resid_first_grad.astype(BF16),
            resid_second_grad.astype(BF16),
            edge_to_atom_grad.astype(BF16),
            trip_bilinear_grad,
            quad_bilinear_grad,
            wide_atoms.reshape(3 * atoms_here, width).astype(BF16),
        ],
        parts,
        out_sent,
    )
    *out_got, own_packed = gate(*receive(out_sent), packed[0])
    packed = [own_packed] + list(packed[1:])
    edges_out = jnp.concatenate(reorder(out_got, rank), axis=0)

    trip_tables = branch_backward(
        trip_index,
        trip_basis,
        trip_agg_grad,
        trip_bil,
        3,
        parts,
        [edges_out] + packed,
        "trip_scatter",
    )
    *packed_got, own_table = gate(*receive(packed), trip_tables[0])
    trip_tables = [own_table] + list(trip_tables[1:])
    mine = tree_sum(packed_got)
    early = packed[0].shape[0] - 3 * atoms_here * width // LANES
    wide_sum = uncolumns(mine[early:], width).reshape(3, atoms_here, width)
    early_rows = jnp.concatenate([mine[:early].astype(BF16), atom_quarter], axis=0)
    total_rows = early_rows.shape[0]
    early_rows = jnp.pad(early_rows, ((0, -total_rows % (16 * edge_parts)), (0, 0)))
    steps = edge_steps()
    keep, send = halve(early_rows, steps[0])

    quad_tables = branch_backward(
        quad_index,
        quad_basis,
        quad_agg_grad,
        quad_bil,
        3,
        parts,
        [wide_sum, send] + trip_tables,
        "quad_scatter",
    )
    quad_tables = list(quad_tables)
    early_got, *trip_got = gate(
        edge_swap(send, steps[0]), *receive(trip_tables), *quad_tables
    )
    trip_got, quad_tables = trip_got[:parts], trip_got[parts:]
    quad_got = receive(quad_tables)
    early_part = (keep.astype(F32) + early_got.astype(F32)).astype(BF16)
    for mask in steps[1:]:
        keep, send = halve(early_part, mask)
        early_part = (keep.astype(F32) + edge_swap(send, mask).astype(F32)).astype(BF16)

    table = jnp.concatenate(
        [
            tree_sum(trip_got),
            tree_sum(quad_got),
            jnp.stack([columns(wide_sum[side]) for side in range(3)]),
        ],
        axis=1,
    )
    branch_grad = (
        table[1]
        + edge_shift(table[0].astype(BF16), -1).astype(F32)
        + edge_shift(table[2].astype(BF16), 1).astype(F32)
    )
    wire_rows = wire.shape[0]
    atom_grad = atoms_new_grad + uncolumns(branch_grad[wire_rows:], width)
    branch_grad = branch_grad[:wire_rows]
    branch_grad = jnp.concatenate(
        [
            unfold_lanes(branch_grad[:trip_rows], trip_width),
            unfold_lanes(branch_grad[trip_rows:], quad_width),
        ],
        axis=1,
    )
    down_grad = (branch_grad * radial_pre * silu_grad(down_pre)).astype(BF16)
    radial_grad = (branch_grad * jax.nn.silu(down_pre)).astype(BF16)
    down_weight_grad = inner(own_edges, down_grad)
    radial_weight_grad = inner(own_radial, radial_grad)
    edge_grad = (one_grad + outer(down_grad, down_full)).astype(BF16)
    edge_grad = jnp.concatenate(reorder(receive(send_back(edge_grad)), rank), axis=0).astype(F32)

    tag_table_grad = jnp.dot(tag_onehot.T, atom_grad, precision=HIGHEST)
    tiny = columns(jnp.concatenate([output_second_grad[None], tag_table_grad], axis=0))

    small_grad = jnp.concatenate([down_weight_grad, radial_weight_grad], axis=0)
    late_sent = pack(
        [
            [
                columns(jnp.concatenate([trip_block, quad_block], axis=1).T)
                for trip_block, quad_block in zip(
                    split(small_grad[:, :trip_width], 1), split(small_grad[:, trip_width:], 1)
                )
            ]
        ]
    )
    late = tree_sum(receive(late_sent))
    late_rows = late.shape[0]
    late = edge_total(jnp.concatenate([late, tiny], axis=0).astype(BF16)).astype(F32)
    tiny = uncolumns(late[late_rows:], width)
    late = late[:late_rows]
    summed = early_part
    for mask in reversed(steps):
        summed = join_halves(summed, mask)
    summed = summed[:total_rows]
    atom_out = jnp.concatenate(reorder(gather_direct(summed[early:]), rank), axis=0).astype(F32)
    summed = summed[:early].astype(F32)
    sizes = sizes + [trip_bil_rows, quad_bilinear.size // LANES]
    offsets = offsets_of(sizes)
    parts_out = [summed[offsets[i] : offsets[i + 1]] for i in range(len(sizes))]
    small_out = uncolumns(late, long).T
    trip_bil_out, quad_bil_out = parts_out[7:]
    half = atom_out.shape[0] // 2
    return (
        edges_out,
        atoms_low,
        energy,
        edge_grad,
        atom_grad,
        small_out[:channels, :trip_cols],
        small_out[channels:, :trip_cols],
        unfold_lanes(trip_bil_out, trip_out).reshape(triplet_bilinear_weight.shape),
        parts_out[0],
        small_out[:channels, trip_cols:],
        small_out[channels:, trip_cols:],
        unfold_lanes(quad_bil_out, quad_out).reshape(quad_bilinear.shape),
        parts_out[1],
        parts_out[2],
        parts_out[3],
        parts_out[4],
        uncolumns(parts_out[5], resid_second.shape[1]),
        uncolumns(parts_out[6], edge_to_atom.shape[1]),
        uncolumns(atom_out[:half], atom_update.shape[1]),
        uncolumns(atom_out[half:], output_first.shape[1]),
        tiny[0],
        tiny[1:],
    )


def solution(mesh):
    return jax.shard_map(
        per_device,
        mesh=mesh,
        in_specs=(
            P("edge", "chan"),
            P("edge", None),
            P("edge", None),
            P(None, None, "edge"),
            P(None, None, "edge"),
            P("edge"),
            P("edge"),
            P("edge"),
            P(None, "edge"),
            P(None, "edge"),
            P(None, "edge"),
            P(None, "edge"),
            P(None, "chan"),
            P(None, "chan"),
            P(None, "chan", None),
            P(None, "chan"),
            P(None, "chan"),
            P(None, "chan"),
            P(None, "chan", None),
            P(None, "chan"),
            P(None, "chan"),
            P(None, "chan"),
            P(None, "chan"),
            P("chan", None),
            P("chan", None),
            P(),
            P(),
            P(),
            P(),
            P("edge", "chan"),
            P("edge", None),
            P("edge"),
        ),
        out_specs=(
            P("edge", "chan"),
            P("edge", None),
            P("edge"),
            P("edge", "chan"),
            P("edge", None),
            P(None, "chan"),
            P(None, "chan"),
            P(None, "chan", None),
            P(None, "chan"),
            P(None, "chan"),
            P(None, "chan"),
            P(None, "chan", None),
            P(None, "chan"),
            P(None, "chan"),
            P(None, "chan"),
            P(None, "chan"),
            P("chan", None),
            P("chan", None),
            P(),
            P(),
            P(),
            P(),
        ),
        check_vma=False,
    )
```

```python
import functools

import jax
import jax.numpy as jnp
from jax import lax
from jax.experimental import pallas as pl
from jax.experimental.pallas import tpu as pltpu
from jax.sharding import PartitionSpec as P

TAGS = 3
LANES = 128
BLOCK = 16
BF16 = jnp.bfloat16
F32 = jnp.float32
HIGHEST = lax.Precision.HIGHEST


def chan_swap(value, mask):
    count = lax.axis_size("chan")
    return lax.ppermute(value, "chan", [(i, i ^ mask) for i in range(count)])


def edge_swap(value, mask):
    count = lax.axis_size("edge")
    return lax.ppermute(value, "edge", [(i, i ^ mask) for i in range(count)])


def edge_shift(value, step):
    count = lax.axis_size("edge")
    return lax.ppermute(value, "edge", [(i, (i + step) % count) for i in range(count)])


def gate(*values):
    return list(lax.optimization_barrier(values))


def gather_direct(value):
    return [value] + [chan_swap(value, step) for step in (1, 2, 3)]


def pick(blocks, place):
    return lax.dynamic_index_in_dim(blocks, place, 0, keepdims=False)


def reorder(blocks, rank):
    low_bit = (rank & 1) == 1
    high_bit = (rank & 2) == 2
    first = [jnp.where(low_bit, blocks[i ^ 1], blocks[i]) for i in range(4)]
    return [jnp.where(high_bit, first[i ^ 2], first[i]) for i in range(4)]


def gather_chan(value):
    across = chan_swap(value, 2)
    beside = chan_swap(jnp.stack([value, across]), 1)
    return [value, beside[0], across, beside[1]]


def exchange(blocks, rank):
    got = [pick(blocks, rank)]
    for step in (1, 2, 3):
        got.append(chan_swap(pick(blocks, rank ^ step), step))
    return reorder(got, rank)


def silu_grad(pre_act):
    sigmoid = jax.nn.sigmoid(pre_act)
    return sigmoid * (1.0 + pre_act * (1.0 - sigmoid))


def matmul(first_op, second_op):
    return jnp.dot(first_op, second_op, preferred_element_type=F32)


def inner(first_op, second_op):
    return lax.dot_general(
        first_op, second_op, (((0,), (0,)), ((), ())), preferred_element_type=F32
    )


def outer(first_op, second_op):
    return lax.dot_general(
        first_op, second_op, (((1,), (1,)), ((), ())), preferred_element_type=F32
    )


def block_weights(basis_ref, block, diagonal):
    basis = basis_ref[block].astype(F32)
    count, width = basis.shape
    spread = jnp.broadcast_to(basis[:, None, :], (count, BLOCK, width))
    spread = spread.reshape(count * BLOCK, width)
    return jnp.where(diagonal, spread, 0.0).astype(BF16)


def diagonal_mask(rows, width):
    row = lax.broadcasted_iota(jnp.int32, (rows, width), 0) % BLOCK
    col = lax.broadcasted_iota(jnp.int32, (rows, width), 1) % BLOCK
    return row == col


def lane_groups(value, width):
    group = lax.broadcasted_iota(jnp.int32, value.shape, 1) // width
    zero = jnp.zeros_like(value)
    masked = [jnp.where(group == fold, value, zero) for fold in range(LANES // width)]
    return jnp.concatenate(masked, axis=0)


def slot_copies(whole_ref, slot_refs, sems, first):
    copies = []
    for slot, slot_ref in enumerate(slot_refs):
        size = slot_ref.shape[0]
        copies.append(
            pltpu.make_async_copy(
                whole_ref.at[pl.ds(slot * size, size)], slot_ref, sems.at[first + slot]
            )
        )
    return copies


def gather_body(index_ref, basis_ref, bilinear_ref, *refs, folds, first_row, count):
    packed_refs = refs[:count]
    slots = basis_ref.shape[2] // BLOCK
    agg_ref, sum_ref, table, rows_a, rows_b, sems = refs[-6 - slots : -slots]
    slot_refs = refs[-slots:]
    copies = slot_copies(index_ref, slot_refs, sems, 0)
    for copy in copies:
        copy.start()
    groups, edges, _ = sum_ref.shape
    basis_count = groups * folds
    width = LANES // folds
    piece_rows = edges // folds
    step = min(piece_rows, 64 // folds)
    lane = lax.broadcasted_iota(jnp.int32, (step, LANES), 1) // width

    def unpack(turn, _):
        start = pl.multiple_of(turn * step, step)
        for piece, packed_ref in enumerate(packed_refs):
            values = packed_ref[pl.ds(first_row + start, step), :].astype(F32)
            turned = [values] + [
                pltpu.roll(values, shift * width, 1) for shift in range(1, folds)
            ]
            for fold in range(folds):
                place = pl.multiple_of((piece * folds + fold) * piece_rows + start, step)
                spread = turned[(0 - fold) % folds]
                for group in range(1, folds):
                    spread = jnp.where(lane == group, turned[(group - fold) % folds], spread)
                table[pl.ds(place, step), :] = spread
        return 0

    lax.fori_loop(0, piece_rows // step, unpack, 0)
    for copy in copies:
        copy.wait()
    diagonal = diagonal_mask(basis_count * BLOCK, slots * BLOCK)

    def fetch(block, rows):
        base = block * BLOCK
        for within in range(BLOCK):
            edge = base + within
            for slot in range(slots):
                place = slot_refs[slot][edge]
                at = slot * BLOCK + within
                rows[pl.ds(at, 1), :] = table[pl.ds(place, 1), :]

    def combine(block, values):
        weights = block_weights(basis_ref, block, diagonal)
        each = groups * BLOCK
        joined = jnp.concatenate(
            [weights[fold * each : (fold + 1) * each] for fold in range(folds)], axis=1
        )
        got = matmul(joined, lane_groups(values, width)).astype(BF16)
        start = pl.multiple_of(block * BLOCK, BLOCK)
        sum_ref[:, pl.ds(start, BLOCK), :] = got.reshape(groups, BLOCK, LANES)

    blocks = edges // BLOCK
    fetch(0, rows_a)
    fetch(1, rows_b)

    def turn(pair, _):
        values_a = rows_a[...].astype(BF16)
        values_b = rows_b[...].astype(BF16)
        fetch(jnp.minimum(2 * pair + 2, blocks - 1), rows_a)
        fetch(jnp.minimum(2 * pair + 3, blocks - 1), rows_b)
        combine(2 * pair, values_a)
        combine(2 * pair + 1, values_b)
        return 0

    lax.fori_loop(0, blocks // 2, turn, 0)
    total = matmul(sum_ref[0], bilinear_ref[0])
    for group in range(1, groups):
        total = total + matmul(sum_ref[group], bilinear_ref[group])
    agg_ref[...] = total.astype(BF16)


def branch_forward(index, packed, first_row, basis, bilinear, needed, name):
    groups, _, out_width = bilinear.shape
    edges = basis.shape[0] * BLOCK
    folds = basis.shape[1] // groups
    slots = basis.shape[2] // BLOCK
    vmem = pl.BlockSpec(memory_space=pltpu.VMEM)
    return pl.pallas_call(
        functools.partial(
            gather_body, folds=folds, first_row=first_row, count=len(packed)
        ),
        out_shape=(
            jax.ShapeDtypeStruct((edges, out_width), BF16),
            jax.ShapeDtypeStruct((groups, edges, LANES), BF16),
        ),
        in_specs=[pl.BlockSpec(memory_space=pl.ANY)]
        + [vmem] * (2 + len(packed))
        + [pl.BlockSpec(memory_space=pl.ANY)] * len(needed),
        out_specs=(vmem, vmem),
        scratch_shapes=[
            pltpu.VMEM((len(packed) * edges, LANES), F32),
            pltpu.VMEM((basis.shape[2], LANES), F32),
            pltpu.VMEM((basis.shape[2], LANES), F32),
            pltpu.SemaphoreType.DMA((slots,)),
        ]
        + [pltpu.SMEM((edges,), jnp.int32)] * slots,
        compiler_params=pltpu.CompilerParams(vmem_limit_bytes=56 << 20),
        cost_estimate=pl.CostEstimate(flops=20 * 10**9, transcendentals=0, bytes_accessed=10**7),
        name=name,
    )(index, basis, bilinear, *packed, *needed)


def basis_body(rank_ref, trip_vals, trip_keep, quad_vals, quad_keep, trip_ref, quad_ref, trip_rows, quad_rows):
    del rank_ref
    tile_slots = LANES // BLOCK

    def build(vals_ref, keep_ref, out_ref, rows):
        count, slots, _ = vals_ref.shape
        vals = vals_ref[...].astype(F32) * keep_ref[...].astype(F32)[None]
        rows[...] = vals.reshape(count * slots, LANES)
        group = lax.broadcasted_iota(jnp.int32, (count, LANES), 1) // BLOCK
        for tile in range(slots // tile_slots):
            by_slot = [
                rows[pl.ds(tile * tile_slots + slot, count, stride=slots), :]
                for slot in range(tile_slots)
            ]
            for block in range(tile_slots):
                joined = None
                for slot, value in enumerate(by_slot):
                    shift = (slot - block) * BLOCK % LANES
                    turned = pltpu.roll(value, shift, 1) if shift else value
                    joined = turned if joined is None else jnp.where(group == slot, turned, joined)
                out_ref[block, :, tile * LANES : (tile + 1) * LANES] = joined.astype(BF16)

    build(trip_vals, trip_keep, trip_ref, trip_rows)
    build(quad_vals, quad_keep, quad_ref, quad_rows)


def slot_basis(rank, circular, trip_mask, spherical, quad_mask, edges):
    steps = edges // LANES
    blocks = LANES // BLOCK

    def source(array):
        shape = array.shape[:-1] + (LANES,)
        lead = (0,) * (len(shape) - 1)
        return pl.BlockSpec(shape, lambda step, rank_ref: lead + (rank_ref[0] * steps + step,))

    def target(count, slots):
        return pl.BlockSpec((blocks, count, slots * BLOCK), lambda step, rank_ref: (step, 0, 0))

    def shape_of(array):
        count, slots, _ = array.shape
        return jax.ShapeDtypeStruct((edges // BLOCK, count, slots * BLOCK), BF16)

    def rows_of(array):
        return pltpu.VMEM((array.shape[0] * array.shape[1], LANES), F32)

    return pl.pallas_call(
        basis_body,
        grid_spec=pltpu.PrefetchScalarGridSpec(
            num_scalar_prefetch=1,
            grid=(steps,),
            in_specs=[source(circular), source(trip_mask), source(spherical), source(quad_mask)],
            out_specs=[target(*circular.shape[:2]), target(*spherical.shape[:2])],
            scratch_shapes=[rows_of(circular), rows_of(spherical)],
        ),
        out_shape=(shape_of(circular), shape_of(spherical)),
        cost_estimate=pl.CostEstimate(flops=10 * 10**9, transcendentals=0, bytes_accessed=10**7),
        name="slot_basis",
    )(rank[None], circular, trip_mask, spherical, quad_mask)


TABLES = 4


def scatter_body(
    index_ref, same_ref, basis_ref, grad_ref, bilinear_ref, *refs, folds, owners, needed
):
    refs = refs[needed:]
    packed_refs = refs[:owners]
    slots = basis_ref.shape[2] // BLOCK
    part, rows_a, rows_b = refs[owners : owners + 3]
    tables = refs[owners + 3 : owners + 3 + TABLES]
    sems = refs[owners + 3 + TABLES]
    slot_refs = refs[-2 * slots : -slots]
    same_refs = refs[-slots:]
    copies = slot_copies(index_ref, slot_refs, sems, 0)
    copies += slot_copies(same_ref, same_refs, sems, slots)
    for copy in copies:
        copy.start()
    sides, piece_rows, _ = packed_refs[0].shape
    groups, edges, _ = part.shape
    basis_count = groups * folds
    width = LANES // folds
    chunk = 256
    table_rows = tables[0].shape[0]

    def clear(turn, _):
        start = pl.multiple_of(turn * chunk, chunk)
        for table in tables:
            table[pl.ds(start, chunk), :] = jnp.zeros((chunk, LANES), F32)
        return 0

    lax.fori_loop(0, table_rows // chunk, clear, 0)
    for group in range(groups):
        part[group] = outer(grad_ref[...], bilinear_ref[group]).astype(BF16)
    for copy in copies:
        copy.wait()
    diagonal = diagonal_mask(basis_count * BLOCK, slots * BLOCK)

    def spread(block, rows):
        weights = block_weights(basis_ref, block, diagonal)
        start = pl.multiple_of(block * BLOCK, BLOCK)
        values = part[:, pl.ds(start, BLOCK), :].reshape(groups * BLOCK, LANES)
        rows[...] = inner(weights, lane_groups(values, width))

    def store(block, rows):
        base = block * BLOCK
        for within in range(0, BLOCK, 2):
            edge = base + within
            next_edge = edge + 1
            for slot in range(slots):
                table = tables[slot % TABLES]
                at = slot * BLOCK + within
                place = slot_refs[slot][edge]
                next_place = slot_refs[slot][next_edge]
                same = same_refs[slot][edge]
                value = rows[pl.ds(at, 1), :]
                next_value = rows[pl.ds(at + 1, 1), :] + same * value
                total = table[pl.ds(place, 1), :] + value
                next_total = table[pl.ds(next_place, 1), :] + next_value
                table[pl.ds(place, 1), :] = total
                table[pl.ds(next_place, 1), :] = next_total

    blocks = edges // BLOCK
    spread(0, rows_a)

    def turn(pair, _):
        spread(2 * pair + 1, rows_b)
        store(2 * pair, rows_a)
        spread(jnp.minimum(2 * pair + 2, blocks - 1), rows_a)
        store(2 * pair + 1, rows_b)
        return 0

    lax.fori_loop(0, blocks // 2, turn, 0)
    step = min(piece_rows, 64 // folds)
    per_piece = piece_rows // step
    lane = lax.broadcasted_iota(jnp.int32, (step, LANES), 1) // width
    low = lane < folds // 2
    even = lane % 2 == 0

    def join(first, second):
        return jnp.where(low, first, second) + pltpu.roll(
            jnp.where(low, second, first), LANES // 2, 1
        )

    def pack(turn, _):
        side = turn // per_piece
        start = pl.multiple_of((turn % per_piece) * step, step)
        for owner, packed_ref in enumerate(packed_refs):
            piece = side * owners + owner
            sums = []
            for fold in range(folds):
                place = pl.multiple_of((piece * folds + fold) * piece_rows + start, step)
                total = tables[0][pl.ds(place, step), :]
                for table in tables[1:]:
                    total = total + table[pl.ds(place, step), :]
                sums.append(total)
            if folds == 2:
                joined = join(sums[0], sums[1])
            else:
                first, second = join(sums[0], sums[2]), join(sums[1], sums[3])
                joined = jnp.where(
                    even,
                    first + pltpu.roll(first, LANES - width, 1),
                    second + pltpu.roll(second, width, 1),
                )
            packed_ref[side, pl.ds(start, step), :] = joined.astype(BF16)
        return 0

    lax.fori_loop(0, sides * per_piece, pack, 0)


def branch_backward(index, basis, grad, bilinear, sides, owners, needed, name):
    edges = grad.shape[0]
    groups = bilinear.shape[0]
    folds = basis.shape[1] // groups
    vmem = pl.BlockSpec(memory_space=pltpu.VMEM)
    out = jax.ShapeDtypeStruct((sides, edges // folds, LANES), BF16)
    slots = basis.shape[2] // BLOCK
    same = (index == jnp.roll(index, -1)).astype(F32)
    whole = pl.BlockSpec(memory_space=pl.ANY)
    return pl.pallas_call(
        functools.partial(scatter_body, folds=folds, owners=owners, needed=len(needed)),
        out_shape=(out,) * owners,
        in_specs=[whole, whole, vmem, vmem, vmem]
        + [pl.BlockSpec(memory_space=pl.ANY)] * len(needed),
        out_specs=(vmem,) * owners,
        scratch_shapes=[
            pltpu.VMEM((groups, edges, LANES), BF16),
            pltpu.VMEM((basis.shape[2], LANES), F32),
            pltpu.VMEM((basis.shape[2], LANES), F32),
        ]
        + [pltpu.VMEM((sides * owners * edges, LANES), F32)] * TABLES
        + [pltpu.SemaphoreType.DMA((2 * slots,))]
        + [pltpu.SMEM((edges,), jnp.int32)] * slots
        + [pltpu.SMEM((edges,), F32)] * slots,
        compiler_params=pltpu.CompilerParams(vmem_limit_bytes=58 << 20),
        cost_estimate=pl.CostEstimate(flops=20 * 10**9, transcendentals=0, bytes_accessed=10**7),
        name=name,
    )(index, same, basis, grad, bilinear, *needed)


def large_parts(refs, block_ref, first, place):
    trip_up, quad_up, proj, first_layer, second_layer, to_atom = refs
    lanes = pl.ds(pl.multiple_of(place * LANES, LANES), LANES)
    for whole in (trip_up, quad_up, proj, first_layer):
        count = whole.shape[0]
        yield block_ref.at[pl.ds(first, count)], whole.at[:, lanes]
        first += count
    for whole in (second_layer, to_atom):
        for column in range(0, whole.shape[1], LANES):
            yield block_ref.at[pl.ds(first, LANES)], whole.at[lanes, pl.ds(column, LANES)]
            first += LANES


def unpack_body(rank_ref, *refs, owners):
    for owner in range(owners):
        for block, window in large_parts(refs[owners:], refs[owner], 0, rank_ref[0] ^ owner):
            window[...] = block[...]


def unpack_large(rank, blocks, shapes):
    vmem = pl.BlockSpec(memory_space=pltpu.VMEM)
    return pl.pallas_call(
        functools.partial(unpack_body, owners=len(blocks)),
        out_shape=tuple(jax.ShapeDtypeStruct(shape, BF16) for shape in shapes),
        in_specs=[pl.BlockSpec(memory_space=pltpu.SMEM)] + [vmem] * len(blocks),
        out_specs=(vmem,) * len(shapes),
        compiler_params=pltpu.CompilerParams(vmem_limit_bytes=32 << 20),
        name="unpack_large",
    )(rank[None], *blocks)


def pack_body(rank_ref, *refs, owners, count):
    large, trip_bil, quad_bil, atoms = refs[:6], refs[6], refs[7], refs[8]
    for owner, out_ref in enumerate(refs[count : count + owners]):
        place = rank_ref[0] ^ owner
        row = 0
        for block, window in large_parts(large, out_ref, 0, place):
            block[...] = window[...]
            row += block.shape[0]
        for whole in (trip_bil, quad_bil):
            groups, rows, out = whole.shape
            folds = LANES // out
            each = rows // folds // owners
            together = 16 // each
            for group in range(0, groups, together):
                pieces = [
                    jnp.concatenate(
                        [
                            whole[
                                member,
                                pl.ds(pl.multiple_of(fold * rows // folds + place * each, each), each),
                                :,
                            ]
                            for fold in range(folds)
                        ],
                        axis=1,
                    )
                    for member in range(group, group + together)
                ]
                out_ref[row : row + 16, :] = jnp.concatenate(pieces, axis=0).astype(BF16)
                row += 16
        for column in range(0, atoms.shape[1], LANES):
            out_ref[row : row + atoms.shape[0], :] = atoms[:, column : column + LANES]
            row += atoms.shape[0]


def pack_early(rank, members, owners, needed):
    total = sum(member.size for member in members[:-1]) // owners // LANES
    total += members[-1].size // LANES
    out = jax.ShapeDtypeStruct((total, LANES), BF16)
    vmem = pl.BlockSpec(memory_space=pltpu.VMEM)
    return pl.pallas_call(
        functools.partial(pack_body, owners=owners, count=len(members) + len(needed)),
        out_shape=(out,) * owners,
        in_specs=[pl.BlockSpec(memory_space=pltpu.SMEM)]
        + [vmem] * len(members)
        + [pl.BlockSpec(memory_space=pl.ANY)] * len(needed),
        out_specs=(vmem,) * owners,
        compiler_params=pltpu.CompilerParams(vmem_limit_bytes=32 << 20),
        cost_estimate=pl.CostEstimate(flops=20 * 10**9, transcendentals=0, bytes_accessed=10**7),
        name="pack_early",
    )(rank[None], *members, *needed)


def fold_lanes(rows):
    count, width = rows.shape
    folds = LANES // width
    each = count // folds
    return jnp.concatenate([rows[i * each : (i + 1) * each] for i in range(folds)], axis=1)


def unfold_lanes(packed, width):
    folds = LANES // width
    return jnp.concatenate([packed[:, i * width : (i + 1) * width] for i in range(folds)], axis=0)


def columns(array):
    return jnp.concatenate(
        [array[:, i : i + LANES] for i in range(0, array.shape[1], LANES)], axis=0
    )


def uncolumns(rows, width):
    each = rows.shape[0] * LANES // width
    return jnp.concatenate(
        [rows[i * each : (i + 1) * each] for i in range(width // LANES)], axis=1
    )


def edge_steps():
    steps = []
    size = 1
    while size < lax.axis_size("edge"):
        steps.append(size)
        size *= 2
    return steps


def halve(value, mask):
    bit = (lax.axis_index("edge") & mask) != 0
    half = value.shape[0] // 2
    keep = jnp.where(bit, value[half:], value[:half])
    send = jnp.where(bit, value[:half], value[half:])
    return keep, send


def join_halves(value, mask):
    bit = (lax.axis_index("edge") & mask) != 0
    got = edge_swap(value, mask)
    return jnp.concatenate([jnp.where(bit, got, value), jnp.where(bit, value, got)], axis=0)


def tree_sum(values):
    values = [value.astype(F32) for value in values]
    while len(values) > 1:
        values = [values[i] + values[i + 1] for i in range(0, len(values), 2)]
    return values[0]


def edge_total(value):
    for mask in edge_steps():
        value = (value.astype(F32) + edge_swap(value, mask).astype(F32)).astype(BF16)
    return value


def per_device(
    edge_emb,
    atom_emb,
    radial,
    circular,
    spherical,
    atom_tags,
    edge_source,
    edge_target,
    trip_source,
    trip_mask,
    quad_source,
    quad_mask,
    triplet_down_weight,
    trip_radial,
    triplet_bilinear_weight,
    trip_up,
    quad_down,
    quad_radial,
    quad_bilinear,
    quad_up,
    source_proj,
    target_proj,
    resid_first,
    resid_second,
    edge_to_atom,
    atom_update,
    output_first,
    output_second,
    tag_table,
    grad_edges,
    grad_atoms,
    grad_energy,
):
    edges_here = edge_emb.shape[0]
    atoms_here = atom_emb.shape[0]
    parts = lax.axis_size("chan")
    edge_parts = lax.axis_size("edge")
    rank = lax.axis_index("chan")
    edge_rank = lax.axis_index("edge")
    edges = edges_here // parts
    cols = edge_emb.shape[1]
    start = rank * edges

    def own(array, axis):
        return lax.dynamic_slice_in_dim(array, start, edges, axis)

    edge_blocks = edge_emb.reshape(parts, edges, cols)
    edge_sent = [pick(edge_blocks, rank ^ step) for step in range(parts)]
    *edge_sent, triplet_down_weight, trip_radial, triplet_bilinear_weight, quad_bilinear = gate(
        *edge_sent, triplet_down_weight, trip_radial, triplet_bilinear_weight, quad_bilinear
    )
    edge_got = [edge_sent[0]] + [chan_swap(edge_sent[step], step) for step in range(1, parts)]
    own_edges = jnp.concatenate(reorder(edge_got, rank), axis=1)

    trip_cols = triplet_down_weight.shape[1]
    quad_cols = quad_down.shape[1]
    trip_out = triplet_bilinear_weight.shape[2]
    quad_out = quad_bilinear.shape[2]
    down_own = jnp.concatenate([triplet_down_weight, quad_down], axis=1)
    small = jnp.concatenate(
        [
            columns(
                jnp.concatenate(
                    [down_own, jnp.concatenate([trip_radial, quad_radial], axis=1)], axis=0
                ).T
            ),
            fold_lanes(triplet_bilinear_weight.reshape(-1, trip_out)),
            fold_lanes(quad_bilinear.reshape(-1, quad_out)),
        ],
        axis=0,
    )
    small = reorder(gather_direct(small), rank)
    channels = parts * cols
    long = channels + radial.shape[1]
    small_rows = (trip_cols + quad_cols) * long // LANES
    trip_bil_rows = triplet_bilinear_weight.size // LANES
    downs = jnp.stack([uncolumns(block[:small_rows], long) for block in small])
    trip_both = downs[:, :trip_cols].reshape(parts * trip_cols, -1).T
    quad_both = downs[:, trip_cols:].reshape(parts * quad_cols, -1).T
    both = jnp.concatenate([trip_both, quad_both], axis=1)
    down_full, radial_full = both[:channels], both[channels:]
    trip_width = trip_both.shape[1]
    quad_width = quad_both.shape[1]
    trip_folds = LANES // trip_width
    quad_folds = LANES // quad_width

    def group_rows(blocks, shape, folds):
        whole = jnp.concatenate(
            [unfold_lanes(block, shape[2]).reshape(shape) for block in blocks], axis=1
        )
        count, width, out = whole.shape
        split = whole.reshape(folds, count // folds, width, out)
        return jnp.transpose(split, (1, 0, 2, 3)).reshape(count // folds, folds * width, out)

    trip_bil = group_rows(
        [block[small_rows : small_rows + trip_bil_rows] for block in small],
        triplet_bilinear_weight.shape,
        trip_folds,
    )
    quad_bil = group_rows(
        [block[small_rows + trip_bil_rows :] for block in small],
        quad_bilinear.shape,
        quad_folds,
    )

    own_radial = own(radial, 0)
    down_pre = matmul(own_edges, down_full)
    radial_pre = matmul(own_radial, radial_full)
    dense = (jax.nn.silu(down_pre) * radial_pre).astype(BF16)
    trip_piece = fold_lanes(dense[:, :trip_width])
    quad_piece = fold_lanes(dense[:, trip_width:])
    trip_rows = trip_piece.shape[0]
    wire = jnp.concatenate([trip_piece, quad_piece], axis=0)
    rank_now, wire, *members, atom_emb, grad_edges = gate(
        rank,
        wire,
        trip_up,
        quad_up,
        source_proj,
        target_proj,
        resid_first,
        resid_second,
        edge_to_atom,
        atom_emb,
        grad_edges,
    )
    tag_onehot = (atom_tags[:, None] == jnp.arange(TAGS)[None, :]).astype(F32)
    atom_full = atom_emb.astype(F32) + jnp.dot(
        tag_onehot, tag_table.astype(F32), precision=HIGHEST
    )
    atom_low = atom_full.astype(BF16)
    before = edge_shift(wire, 1)
    later = edge_shift(wire, -1)
    own_across = chan_swap(wire, 2)
    own_beside = chan_swap(wire, 1)

    def spread(first, across):
        return [first, chan_swap(first, 1), across, chan_swap(across, 1)]

    before_across = chan_swap(before, 2)
    later_across = chan_swap(later, 2)
    before_across, later_across, atom_before, atom_later = gate(
        before_across, later_across, edge_shift(atom_low, 1), edge_shift(atom_low, -1)
    )
    wire_pieces = (
        spread(before, before_across)
        + [wire, own_beside, own_across, chan_swap(own_across, 1)]
        + spread(later, later_across)
    )

    def places(source):
        local = own(source, 1)
        within = local % edges_here
        owner = (within // edges) ^ rank
        return ((local // edges_here) * edges_here + owner * edges + within % edges).reshape(-1)

    trip_index = places(trip_source)
    quad_index = places(quad_source)
    trip_basis, quad_basis = slot_basis(
        rank_now, circular, trip_mask, spherical, quad_mask, edges
    )

    large = jnp.concatenate(members[:5] + [columns(members[5]), columns(members[6])], axis=0)
    grad_blocks = grad_edges.reshape(parts, edges, cols)
    grad_sent = [pick(grad_blocks, rank ^ step) for step in range(parts)]
    quad_agg, quad_sum = branch_forward(
        quad_index,
        wire_pieces,
        trip_rows,
        quad_basis,
        quad_bil,
        [large] + grad_sent,
        "quad_gather",
    )
    large_across, large_beside, quad_agg, *grad_sent = gate(
        chan_swap(large, 2),
        chan_swap(large, 1),
        quad_agg,
        *grad_sent,
    )

    trip_agg, trip_sum = branch_forward(
        trip_index,
        wire_pieces,
        0,
        trip_basis,
        trip_bil,
        [large_across] + grad_sent,
        "trip_gather",
    )
    grad_got = [grad_sent[0]] + [chan_swap(grad_sent[step], step) for step in range(1, parts)]
    large_diag, trip_agg, *grad_got = gate(chan_swap(large_across, 1), trip_agg, *grad_got)
    grad_two = jnp.concatenate(reorder(grad_got, rank), axis=1)
    sizes = [
        trip_up.shape[0],
        quad_up.shape[0],
        source_proj.shape[0],
        target_proj.shape[0],
        resid_first.shape[0],
        resid_second.size // LANES,
        edge_to_atom.size // LANES,
    ]

    def offsets_of(sizes):
        return [sum(sizes[:i]) for i in range(len(sizes) + 1)]

    offsets = offsets_of(sizes)

    trip_up_full, quad_up_full, proj_full, first_full, second_full, to_atom_full = unpack_large(
        rank,
        [large, large_beside, large_across, large_diag],
        [
            (trip_width, channels),
            (quad_width, channels),
            (2 * source_proj.shape[0], channels),
            (channels, channels),
            (channels, channels),
            (channels, edge_to_atom.shape[1]),
        ],
    )

    atom_wide = jnp.concatenate([atom_before, atom_low, atom_later], axis=0)
    atom_total = edge_parts * atoms_here
    source_local = (own(edge_source, 0) - (edge_rank - 1) * atoms_here) % atom_total
    target_local = own(edge_target, 0) - edge_rank * atoms_here
    source_hot = (source_local[:, None] == jnp.arange(3 * atoms_here)[None, :]).astype(BF16)
    target_hot = (target_local[:, None] == jnp.arange(atoms_here)[None, :]).astype(BF16)
    ends = jnp.concatenate(
        [
            matmul(source_hot, atom_wide).astype(BF16),
            matmul(target_hot, atom_low).astype(BF16),
        ],
        axis=1,
    )

    message = matmul(ends, proj_full)
    trip_out_pre = matmul(trip_agg, trip_up_full)
    quad_out_pre = matmul(quad_agg, quad_up_full)
    hidden_one = (
        own_edges.astype(F32)
        + jax.nn.silu(trip_out_pre)
        + jax.nn.silu(quad_out_pre)
        + jax.nn.silu(message)
    )
    hidden_low = hidden_one.astype(BF16)
    first_pre = matmul(hidden_low, first_full)
    first_low = jax.nn.silu(first_pre).astype(BF16)
    second_pre = matmul(first_low, second_full)
    edges_low = (hidden_one + jax.nn.silu(second_pre)).astype(BF16)
    edge_sums = inner(target_hot, edges_low)
    sums_high = edge_sums.astype(BF16)
    sums_rest = (edge_sums - sums_high.astype(F32)).astype(BF16)
    atom_sum = matmul(sums_high, to_atom_full) + matmul(sums_rest, to_atom_full)
    atom_sum = atom_sum + chan_swap(atom_sum, 1)
    atom_sum = atom_sum + chan_swap(atom_sum, 2)
    atom_sum, edges_low = gate(atom_sum, edges_low)

    atom_sum_low = atom_sum.astype(BF16)
    update_pre = matmul(atom_sum_low, atom_update)
    atoms_new = atom_full + jax.nn.silu(update_pre)
    atoms_low = atoms_new.astype(BF16)
    output_pre = matmul(atoms_low, output_first)
    output_low = jax.nn.silu(output_pre).astype(BF16)
    energy = matmul(output_low, output_second)
    output_second_grad = jnp.dot(grad_energy, output_low.astype(F32), precision=HIGHEST)
    output_grad = (
        grad_energy[:, None] * output_second.astype(F32)[None, :] * silu_grad(output_pre)
    ).astype(BF16)
    output_first_grad = inner(atoms_low, output_grad)
    atoms_new_grad = grad_atoms.astype(F32) + outer(output_grad, output_first)
    update_grad = (atoms_new_grad * silu_grad(update_pre)).astype(BF16)
    atom_update_grad = inner(atom_sum_low, update_grad)
    atom_sum_grad = outer(update_grad, atom_update).astype(BF16)

    edge_part_grad = matmul(target_hot, atom_sum_grad).astype(BF16)
    edge_to_atom_grad = inner(edges_low, edge_part_grad)
    two_grad = grad_two.astype(F32) + outer(edge_part_grad, to_atom_full)
    second_grad = (two_grad * silu_grad(second_pre)).astype(BF16)
    resid_second_grad = inner(first_low, second_grad)
    first_grad = (outer(second_grad, second_full) * silu_grad(first_pre)).astype(BF16)
    resid_first_grad = inner(hidden_low, first_grad)
    one_grad = two_grad + outer(first_grad, first_full)
    trip_out_grad = (one_grad * silu_grad(trip_out_pre)).astype(BF16)
    quad_out_grad = (one_grad * silu_grad(quad_out_pre)).astype(BF16)
    message_grad = (one_grad * silu_grad(message)).astype(BF16)
    trip_up_grad = inner(trip_agg, trip_out_grad)
    quad_up_grad = inner(quad_agg, quad_out_grad)
    trip_agg_grad = outer(trip_out_grad, trip_up_full).astype(BF16)
    quad_agg_grad = outer(quad_out_grad, quad_up_full).astype(BF16)
    proj_grad = inner(ends, message_grad)
    width = atom_low.shape[1]
    source_sums = inner(source_hot, message_grad).astype(BF16)
    target_sums = inner(target_hot, message_grad).astype(BF16)
    source_back = outer(source_sums, proj_full[:width])
    target_back = outer(target_sums, proj_full[width:])
    wide_atoms = source_back.reshape(3, atoms_here, width)
    wide_atoms = wide_atoms.at[1].add(target_back)

    def split(array, axis):
        return jnp.split(array, parts, axis=axis)

    def pack(members):
        packed = [
            jnp.concatenate([member[i] for member in members], axis=0).astype(BF16)
            for i in range(parts)
        ]
        return reorder(packed, rank)

    trip_bilinear_grad = jnp.einsum(
        "gej,eo->gjo", trip_sum, trip_agg_grad, preferred_element_type=F32
    )
    quad_bilinear_grad = jnp.einsum(
        "gej,eo->gjo", quad_sum, quad_agg_grad, preferred_element_type=F32
    )
    atom_rows = jnp.concatenate(
        [columns(atom_update_grad), columns(output_first_grad)], axis=0
    ).astype(BF16)
    atom_quarter = pick(atom_rows.reshape(parts, -1, LANES), rank)

    def send_back(array):
        blocks = jnp.stack([array[:, i * cols : (i + 1) * cols] for i in range(parts)])
        return [pick(blocks, rank ^ step) for step in range(parts)]

    def receive(sent):
        return [sent[0]] + [chan_swap(sent[step], step) for step in range(1, parts)]

    out_sent = send_back(edges_low)
    packed = pack_early(
        rank,
        [
            trip_up_grad.astype(BF16),
            quad_up_grad.astype(BF16),
            proj_grad.astype(BF16),
            resid_first_grad.astype(BF16),
            resid_second_grad.astype(BF16),
            edge_to_atom_grad.astype(BF16),
            trip_bilinear_grad,
            quad_bilinear_grad,
            wide_atoms.reshape(3 * atoms_here, width).astype(BF16),
        ],
        parts,
        out_sent,
    )
    *out_got, own_packed = gate(*receive(out_sent), packed[0])
    packed = [own_packed] + list(packed[1:])
    edges_out = jnp.concatenate(reorder(out_got, rank), axis=0)

    trip_tables = branch_backward(
        trip_index,
        trip_basis,
        trip_agg_grad,
        trip_bil,
        3,
        parts,
        [edges_out] + packed,
        "trip_scatter",
    )
    *packed_got, own_table = gate(*receive(packed), trip_tables[0])
    trip_tables = [own_table] + list(trip_tables[1:])
    mine = tree_sum(packed_got)
    early = packed[0].shape[0] - 3 * atoms_here * width // LANES
    wide_sum = uncolumns(mine[early:], width).reshape(3, atoms_here, width)
    early_rows = jnp.concatenate([mine[:early].astype(BF16), atom_quarter], axis=0)
    total_rows = early_rows.shape[0]
    early_rows = jnp.pad(early_rows, ((0, -total_rows % (16 * edge_parts)), (0, 0)))
    steps = edge_steps()
    keep, send = halve(early_rows, steps[0])

    quad_tables = branch_backward(
        quad_index,
        quad_basis,
        quad_agg_grad,
        quad_bil,
        3,
        parts,
        [wide_sum, send] + trip_tables,
        "quad_scatter",
    )
    quad_tables = list(quad_tables)
    early_got, *trip_got = gate(
        edge_swap(send, steps[0]), *receive(trip_tables), *quad_tables
    )
    trip_got, quad_tables = trip_got[:parts], trip_got[parts:]
    quad_got = receive(quad_tables)
    early_part = (keep.astype(F32) + early_got.astype(F32)).astype(BF16)
    for mask in steps[1:]:
        keep, send = halve(early_part, mask)
        early_part = (keep.astype(F32) + edge_swap(send, mask).astype(F32)).astype(BF16)

    table = jnp.concatenate(
        [
            tree_sum(trip_got),
            tree_sum(quad_got),
            jnp.stack([columns(wide_sum[side]) for side in range(3)]),
        ],
        axis=1,
    )
    branch_grad = (
        table[1]
        + edge_shift(table[0].astype(BF16), -1).astype(F32)
        + edge_shift(table[2].astype(BF16), 1).astype(F32)
    )
    wire_rows = wire.shape[0]
    atom_grad = atoms_new_grad + uncolumns(branch_grad[wire_rows:], width)
    branch_grad = branch_grad[:wire_rows]
    branch_grad = jnp.concatenate(
        [
            unfold_lanes(branch_grad[:trip_rows], trip_width),
            unfold_lanes(branch_grad[trip_rows:], quad_width),
        ],
        axis=1,
    )
    down_grad = (branch_grad * radial_pre * silu_grad(down_pre)).astype(BF16)
    radial_grad = (branch_grad * jax.nn.silu(down_pre)).astype(BF16)
    down_weight_grad = inner(own_edges, down_grad)
    radial_weight_grad = inner(own_radial, radial_grad)
    edge_grad = (one_grad + outer(down_grad, down_full)).astype(BF16)
    edge_grad = jnp.concatenate(reorder(receive(send_back(edge_grad)), rank), axis=0).astype(F32)

    tag_table_grad = jnp.dot(tag_onehot.T, atom_grad, precision=HIGHEST)
    tiny = columns(jnp.concatenate([output_second_grad[None], tag_table_grad], axis=0))

    small_grad = jnp.concatenate([down_weight_grad, radial_weight_grad], axis=0)
    late_sent = pack(
        [
            [
                columns(jnp.concatenate([trip_block, quad_block], axis=1).T)
                for trip_block, quad_block in zip(
                    split(small_grad[:, :trip_width], 1), split(small_grad[:, trip_width:], 1)
                )
            ]
        ]
    )
    late = tree_sum(receive(late_sent))
    late_rows = late.shape[0]
    late = edge_total(jnp.concatenate([late, tiny], axis=0).astype(BF16)).astype(F32)
    tiny = uncolumns(late[late_rows:], width)
    late = late[:late_rows]
    summed = early_part
    for mask in reversed(steps):
        summed = join_halves(summed, mask)
    summed = summed[:total_rows]
    atom_out = jnp.concatenate(reorder(gather_direct(summed[early:]), rank), axis=0).astype(F32)
    summed = summed[:early].astype(F32)
    sizes = sizes + [trip_bil_rows, quad_bilinear.size // LANES]
    offsets = offsets_of(sizes)
    parts_out = [summed[offsets[i] : offsets[i + 1]] for i in range(len(sizes))]
    small_out = uncolumns(late, long).T
    trip_bil_out, quad_bil_out = parts_out[7:]
    half = atom_out.shape[0] // 2
    return (
        edges_out,
        atoms_low,
        energy,
        edge_grad,
        atom_grad,
        small_out[:channels, :trip_cols],
        small_out[channels:, :trip_cols],
        unfold_lanes(trip_bil_out, trip_out).reshape(triplet_bilinear_weight.shape),
        parts_out[0],
        small_out[:channels, trip_cols:],
        small_out[channels:, trip_cols:],
        unfold_lanes(quad_bil_out, quad_out).reshape(quad_bilinear.shape),
        parts_out[1],
        parts_out[2],
        parts_out[3],
        parts_out[4],
        uncolumns(parts_out[5], resid_second.shape[1]),
        uncolumns(parts_out[6], edge_to_atom.shape[1]),
        uncolumns(atom_out[:half], atom_update.shape[1]),
        uncolumns(atom_out[half:], output_first.shape[1]),
        tiny[0],
        tiny[1:],
    )


def solution(mesh):
    return jax.shard_map(
        per_device,
        mesh=mesh,
        in_specs=(
            P("edge", "chan"),
            P("edge", None),
            P("edge", None),
            P(None, None, "edge"),
            P(None, None, "edge"),
            P("edge"),
            P("edge"),
            P("edge"),
            P(None, "edge"),
            P(None, "edge"),
            P(None, "edge"),
            P(None, "edge"),
            P(None, "chan"),
            P(None, "chan"),
            P(None, "chan", None),
            P(None, "chan"),
            P(None, "chan"),
            P(None, "chan"),
            P(None, "chan", None),
            P(None, "chan"),
            P(None, "chan"),
            P(None, "chan"),
            P(None, "chan"),
            P("chan", None),
            P("chan", None),
            P(),
            P(),
            P(),
            P(),
            P("edge", "chan"),
            P("edge", None),
            P("edge"),
        ),
        out_specs=(
            P("edge", "chan"),
            P("edge", None),
            P("edge"),
            P("edge", "chan"),
            P("edge", None),
            P(None, "chan"),
            P(None, "chan"),
            P(None, "chan", None),
            P(None, "chan"),
            P(None, "chan"),
            P(None, "chan"),
            P(None, "chan", None),
            P(None, "chan"),
            P(None, "chan"),
            P(None, "chan"),
            P(None, "chan"),
            P("chan", None),
            P("chan", None),
            P(),
            P(),
            P(),
            P(),
        ),
        check_vma=False,
    )
```
